128 devices in a mesh: tp: 4 (over y_lo, core), dp: 32 (over x, z, y_hi).
Axes of the slice: x: 4, y: 4 (y_hi: 2, y_lo: 2; y = y_hi * 2 + y_lo), z: 4, core: 2. Of those that a mesh axis runs over, the one named last changes fastest.
Arguments:
- teacher_query: bfloat16 [8192, 8192], P('dp', 'tp'), may hold values from -8 to 8
- student_hidden: bfloat16 [8192, 4096], P('dp', 'tp'), may hold values from -16 to 16
- query_weight: bfloat16 [4096, 4096], P('dp', 'tp'), may hold values from -0.039794922 to 0.039794922
Outputs:
- kl_rows: float32 [128, 2048], P(('tp', 'dp'))
- weight_grad: float32 [4096, 4096], P('dp', 'tp')
The draws below stay inside these ranges and needn't reach their ends.
All inputs are finite; a program needn't handle non-finite values.
Results may differ from the reference program's by a relative error of at most 0.0029.
Values may be sent and summed in bfloat16 or wider, within the bound.
No kernel may reach another device: no remote copies, remote signals or barrier semaphores. Data moves between devices by JAX's collectives and lax.ppermute only.
A program may use at most 64 MiB of HBM per device.

```python
import jax
import jax.numpy as jnp
from jax import lax

DT = 8192
DS = 4096
RHEADS = 32
NSEQ = 2
SEQ = 4096
QBLOCKS = 4
QROWS = 1024


def draw_teacher_query(key, part):
    values = 0.5 * jnp.clip(jax.random.normal(jax.random.fold_in(key, 1), (NSEQ * SEQ, DT), jnp.float32), -4.0, 4.0)
    return values.astype(jnp.bfloat16)


def draw_student_hidden(key, part):
    values = jnp.clip(jax.random.normal(jax.random.fold_in(key, 2), (NSEQ * SEQ, DS), jnp.float32), -4.0, 4.0)
    return values.astype(jnp.bfloat16)


def steps_of(rng, dims, cuts, smallest, largest):
    def one(position, parts):
        heights = jax.random.uniform(jax.random.fold_in(jax.random.fold_in(rng, 6), position), (parts,), jnp.float32, smallest / len(cuts), largest / len(cuts))
        return jnp.repeat(jnp.exp(heights), dims[position] // parts).reshape((-1,) + (1,) * (len(dims) - position - 1))

    factor_of = one(*cuts[0])
    for cut in cuts[1:]:
        factor_of = factor_of * one(*cut)
    return factor_of


def noise(stream_key, shape, scale, bound, shards=(), held_as=jnp.bfloat16):
    drawn = jax.random.normal(stream_key, shape, jnp.float32) * scale
    if len(shards) > 0:
        drawn = steps_of(stream_key, shape, shards, -0.22, 0.18) * drawn
    return jnp.clip(drawn, min=-bound, max=bound).astype(held_as)


def setup_inputs(seed: int = 0) -> dict:
    arg_keys = jax.random.split(jax.random.key(seed), 4)
    return {
        "teacher_query": draw_teacher_query(jax.random.fold_in(arg_keys[3], 71), 0),
        "student_hidden": draw_student_hidden(jax.random.fold_in(arg_keys[3], 71), 0),
        "query_weight": noise(arg_keys[2], (DS, DS), 0.0078125, 0.039794922, ((0, 32), (1, 4))),
    }


def head_terms(pair):
    teacher_head, student_head = pair
    teacher_scale = teacher_head.shape[1] ** -0.5
    student_scale = student_head.shape[1] ** -0.5
    teacher_scores = lax.dot_general(teacher_head, teacher_head, (((1,), (1,)), ((), ())), preferred_element_type=jnp.float32) * teacher_scale
    student_scores = lax.dot_general(student_head, student_head, (((1,), (1,)), ((), ())), preferred_element_type=jnp.float32) * student_scale
    teacher_log = jax.nn.log_softmax(teacher_scores, axis=-1)
    student_log = jax.nn.log_softmax(student_scores, axis=-1)
    teacher_prob = jnp.exp(teacher_log)
    divergence = jnp.sum(teacher_prob * (teacher_log - student_log), axis=-1)
    score_grad = (jnp.exp(student_log) - teacher_prob).astype(jnp.bfloat16)
    row_part = jnp.dot(score_grad, student_head, preferred_element_type=jnp.float32)
    key_part = lax.dot_general(score_grad, student_head, (((0,), (0,)), ((), ())), preferred_element_type=jnp.float32)
    return divergence, (row_part + key_part) * student_scale


def reference(teacher_query, student_hidden, query_weight):
    student_query = jnp.dot(student_hidden, query_weight, preferred_element_type=jnp.float32).astype(jnp.bfloat16)
    teacher_width = DT // RHEADS
    student_width = DS // RHEADS
    teacher_heads = teacher_query.reshape(NSEQ, SEQ, RHEADS, teacher_width).transpose(2, 0, 1, 3).reshape(RHEADS * NSEQ, SEQ, teacher_width)
    student_heads = student_query.reshape(NSEQ, SEQ, RHEADS, student_width).transpose(2, 0, 1, 3).reshape(RHEADS * NSEQ, SEQ, student_width)
    divergence, head_grads = lax.map(head_terms, (teacher_heads, student_heads))
    query_grad = head_grads.reshape(RHEADS, NSEQ, SEQ, student_width).transpose(1, 2, 0, 3).reshape(NSEQ * SEQ, DS).astype(jnp.bfloat16)
    weight_grad = lax.dot_general(student_hidden, query_grad, (((0,), (0,)), ((), ())), preferred_element_type=jnp.float32)
    kl_rows = divergence.reshape(RHEADS, NSEQ, QBLOCKS, QROWS).transpose(0, 2, 1, 3).reshape(RHEADS * QBLOCKS, NSEQ * QROWS)
    return kl_rows, weight_grad
```

```python
import functools

import jax
import jax.numpy as jnp
from jax import lax
from jax.experimental import pallas as pl
from jax.experimental.pallas import tpu as pltpu
from jax.sharding import Mesh, PartitionSpec as P

RHEADS = 32
NSEQ = 2
SEQ = 4096
LOG2E = 1.4426950408889634
LN2 = 0.6931471805599453
LANES = 128

TP = ("yl", "core")
DP = ("xh", "xl", "zh", "zl", "yh")
BLOCK = ("xl", "zh")
COLUMN = ("zl", "yh")

CONTRACT_LAST = (((1,), (1,)), ((), ()))
CONTRACT_FIRST = (((0,), (0,)), ((), ()))


def lane_fold(x, op):
    acc = x[:, :LANES]
    for j in range(1, x.shape[1] // LANES):
        acc = op(acc, x[:, j * LANES : (j + 1) * LANES])
    return acc


def relation_kernel(block, chunk, sub, t_rows, s_rows, t_all, s_all, kl_ref, grad_ref, u_scr, v_scr, g_scr):
    step = pl.program_id(0)
    seq = t_all.shape[0]
    student_scale = s_all.shape[1] ** -0.5
    t_mul = LOG2E * t_all.shape[1] ** -0.5
    s_mul = LOG2E * student_scale

    @pl.when(step == 0)
    def _():
        grad_ref[...] = jnp.zeros_like(grad_ref)

    tr = t_rows[...]
    sr = s_rows[...]
    mt = ms = None
    for c in range(0, seq, chunk):
        u = t_mul * lax.dot_general(tr, t_all[c : c + chunk, :], CONTRACT_LAST, preferred_element_type=jnp.float32)
        u_scr[:, c : c + chunk] = u
        fold = lane_fold(u, jnp.maximum)
        mt = fold if mt is None else jnp.maximum(mt, fold)
        v = s_mul * lax.dot_general(sr, s_all[c : c + chunk, :], CONTRACT_LAST, preferred_element_type=jnp.float32)
        v_scr[:, c : c + chunk] = v
        fold = lane_fold(v, jnp.maximum)
        ms = fold if ms is None else jnp.maximum(ms, fold)
    mt = jnp.max(mt, axis=1, keepdims=True)
    ms = jnp.max(ms, axis=1, keepdims=True)
    for r in range(0, block, sub):
        rows = slice(r, r + sub)
        m_t = jnp.broadcast_to(mt[rows], (sub, LANES))
        m_s = jnp.broadcast_to(ms[rows], (sub, LANES))
        zero = jnp.zeros((sub, LANES), jnp.float32)
        lt, ls, a = zero, zero, zero
        for c in range(0, seq, LANES):
            x = u_scr[rows, c : c + LANES] - m_t
            y = v_scr[rows, c : c + LANES] - m_s
            et = jnp.exp2(x)
            lt = lt + et
            ls = ls + jnp.exp2(y)
            a = a + et * (x - y)
        lt = jnp.sum(lt, axis=1, keepdims=True)
        ls = jnp.sum(ls, axis=1, keepdims=True)
        a = jnp.sum(a, axis=1, keepdims=True)
        log_t = jnp.log2(lt)
        log_s = jnp.log2(ls)
        kl = (a / lt - log_t + log_s) * LN2
        kl_ref[rows, :] = jnp.broadcast_to(kl, (sub, LANES))
        z_t = jnp.broadcast_to(mt[rows] + log_t, (sub, LANES))
        z_s = jnp.broadcast_to(ms[rows] + log_s, (sub, LANES))
        for c in range(0, seq, LANES):
            g = jnp.exp2(v_scr[rows, c : c + LANES] - z_s) - jnp.exp2(u_scr[rows, c : c + LANES] - z_t)
            g_scr[rows, c : c + LANES] = g.astype(jnp.bfloat16)
    acc = jnp.zeros((block, s_all.shape[1]), jnp.float32)
    for c in range(0, seq, chunk):
        g = g_scr[:, c : c + chunk]
        acc = acc + jnp.dot(g, s_all[c : c + chunk, :], preferred_element_type=jnp.float32)
        grad_ref[c : c + chunk, :] += lax.dot_general(g, sr, CONTRACT_FIRST, preferred_element_type=jnp.float32)
    start = pl.multiple_of(lax.axis_index("zh") * (seq // 2) + step * block, block)
    grad_ref[pl.ds(start, block), :] += acc

    @pl.when(step == pl.num_programs(0) - 1)
    def _():
        grad_ref[...] = grad_ref[...] * student_scale


def relation(t_all, s_all, block=256, chunk=512, sub=32):
    seq, t_width = t_all.shape
    s_width = s_all.shape[1]
    rows = seq // 2
    steps = rows // block

    def row_map(i):
        return (lax.axis_index("zh") * steps + i, 0)

    def whole(i):
        return (0, 0)

    return pl.pallas_call(
        functools.partial(relation_kernel, block, chunk, sub),
        grid=(steps,),
        in_specs=[
            pl.BlockSpec((block, t_width), row_map),
            pl.BlockSpec((block, s_width), row_map),
            pl.BlockSpec((seq, t_width), whole),
            pl.BlockSpec((seq, s_width), whole),
        ],
        out_specs=[
            pl.BlockSpec((block, LANES), lambda i: (i, 0)),
            pl.BlockSpec((seq, s_width), whole),
        ],
        out_shape=[
            jax.ShapeDtypeStruct((rows, LANES), jnp.float32),
            jax.ShapeDtypeStruct((seq, s_width), jnp.float32),
        ],
        scratch_shapes=[
            pltpu.VMEM((block, seq), jnp.float32),
            pltpu.VMEM((block, seq), jnp.float32),
            pltpu.VMEM((block, seq), jnp.bfloat16),
        ],
        compiler_params=pltpu.CompilerParams(vmem_limit_bytes=56 << 20),
    )(t_all, s_all, t_all, s_all)


def exchange(chunks, axes):
    return lax.all_to_all(chunks, axes, split_axis=0, concat_axis=0, tiled=True)


def local(teacher_query, student_hidden, query_weight):
    rows = teacher_query.shape[0]
    depth, columns = query_weight.shape
    t_width = teacher_query.shape[1] // 8
    s_width = columns // 8
    width = columns // 4
    hidden = lax.all_gather(student_hidden, TP + COLUMN, axis=0, tiled=True)
    hidden = hidden.reshape(4, 4 * rows, columns)
    parts = jnp.moveaxis(query_weight.reshape(depth, 4, width), 1, 0)
    weight = exchange(jnp.broadcast_to(parts, (8, 4, depth, width)).reshape(32, depth, width), DP)
    weight = weight.reshape(4, 8 * depth, width)
    heads = jnp.moveaxis(teacher_query.reshape(rows, 4, 2, t_width), 0, 2)
    heads = jnp.moveaxis(heads, 1, 0)[:, None]
    heads = jnp.broadcast_to(heads, (2, 2, 4, rows, t_width)).reshape(16, rows, t_width)
    teacher = exchange(heads, BLOCK + COLUMN).reshape(SEQ, t_width)
    student = lax.dot_general(
        hidden, weight, (((0, 2), (0, 1)), ((), ())), preferred_element_type=jnp.float32
    ).astype(jnp.bfloat16)
    pair = jnp.moveaxis(student.reshape(4 * rows, 2, s_width), 1, 0)[:, None]
    pair = jnp.broadcast_to(pair, (2, 2, 4 * rows, s_width)).reshape(4, 4 * rows, s_width)
    student_all = exchange(pair, BLOCK).reshape(SEQ, s_width)
    kl, grad = relation(teacher, student_all)
    terms = exchange(grad.reshape(4, 4 * rows, s_width), BLOCK)
    terms = terms.reshape(2, 2, 4 * rows, s_width)
    summed = (terms[:, 0] + terms[:, 1]).astype(jnp.bfloat16)
    query_grad = jnp.moveaxis(summed, 0, 1).reshape(4 * rows, width)
    partial = lax.dot_general(
        hidden, query_grad, (((1,), (0,)), ((), ())), preferred_element_type=jnp.float32
    )
    sent = exchange(partial.astype(jnp.bfloat16).reshape(32, depth, width), DP)
    weight_grad = jnp.sum(sent.reshape(8, 4, depth, width).astype(jnp.float32), axis=0)
    weight_grad = jnp.moveaxis(weight_grad, 0, 1).reshape(depth, columns)
    all_kl = lax.all_gather(kl[:, 0], DP, axis=0).reshape(2, 2, 2, 4, 2, SEQ // 4)
    dp = lax.axis_index(DP)
    head, quarter = dp // 4, dp % 4
    row = lax.dynamic_slice(
        all_kl, (0, head % 2, quarter // 2, head // 2, quarter % 2, 0), (2, 1, 1, 1, 1, SEQ // 4)
    )
    return row.reshape(1, NSEQ * (SEQ // 4)), weight_grad


def solution(mesh):
    bits = Mesh(mesh.devices.reshape((2,) * 7), TP + DP)
    return jax.shard_map(
        local,
        mesh=bits,
        in_specs=(P(DP, TP), P(DP, TP), P(DP, TP)),
        out_specs=(P(TP + DP, None), P(DP, TP)),
        check_vma=False,
    )
```

```python
import functools

import jax
import jax.numpy as jnp
from jax import lax
from jax.experimental import pallas as pl
from jax.experimental.pallas import tpu as pltpu
from jax.sharding import Mesh, PartitionSpec as P

RHEADS = 32
NSEQ = 2
SEQ = 4096
LOG2E = 1.4426950408889634
LN2 = 0.6931471805599453
LANES = 128

TP = ("yl", "core")
DP = ("xh", "xl", "zh", "zl", "yh")
BLOCK = ("xl", "zh")
COLUMN = ("zl", "yh")

CONTRACT_LAST = (((1,), (1,)), ((), ()))
CONTRACT_FIRST = (((0,), (0,)), ((), ()))


def lane_fold(x, op):
    acc = x[:, :LANES]
    for j in range(1, x.shape[1] // LANES):
        acc = op(acc, x[:, j * LANES : (j + 1) * LANES])
    return acc


def relation_kernel(block, chunk, sub, t_rows, s_rows, t_all, s_all, kl_ref, grad_ref, u_scr, v_scr, g_scr, kl_scr):
    step = pl.program_id(0)
    seq = t_all.shape[0]
    student_scale = s_all.shape[1] ** -0.5
    t_mul = LOG2E * t_all.shape[1] ** -0.5
    s_mul = LOG2E * student_scale

    @pl.when(step == 0)
    def _():
        grad_ref[...] = jnp.zeros_like(grad_ref)

    tr = t_rows[...]
    sr = s_rows[...]
    mt = ms = None
    for c in range(0, seq, chunk):
        u = t_mul * lax.dot_general(tr, t_all[c : c + chunk, :], CONTRACT_LAST, preferred_element_type=jnp.float32)
        u_scr[:, c : c + chunk] = u
        fold = lane_fold(u, jnp.maximum)
        mt = fold if mt is None else jnp.maximum(mt, fold)
        v = s_mul * lax.dot_general(sr, s_all[c : c + chunk, :], CONTRACT_LAST, preferred_element_type=jnp.float32)
        v_scr[:, c : c + chunk] = v
        fold = lane_fold(v, jnp.maximum)
        ms = fold if ms is None else jnp.maximum(ms, fold)
    mt = jnp.max(mt, axis=1, keepdims=True)
    ms = jnp.max(ms, axis=1, keepdims=True)
    for r in range(0, block, sub):
        rows = slice(r, r + sub)
        m_t = jnp.broadcast_to(mt[rows], (sub, LANES))
        m_s = jnp.broadcast_to(ms[rows], (sub, LANES))
        zero = jnp.zeros((sub, LANES), jnp.float32)
        lt, ls, a = zero, zero, zero
        for c in range(0, seq, LANES):
            x = u_scr[rows, c : c + LANES] - m_t
            y = v_scr[rows, c : c + LANES] - m_s
            et = jnp.exp2(x)
            lt = lt + et
            ls = ls + jnp.exp2(y)
            a = a + et * (x - y)
        lt = jnp.sum(lt, axis=1, keepdims=True)
        ls = jnp.sum(ls, axis=1, keepdims=True)
        a = jnp.sum(a, axis=1, keepdims=True)
        log_t = jnp.log2(lt)
        log_s = jnp.log2(ls)
        kl = (a / lt - log_t + log_s) * LN2
        kl_scr[rows, :] = jnp.broadcast_to(kl, (sub, LANES))
        z_t = jnp.broadcast_to(mt[rows] + log_t, (sub, LANES))
        z_s = jnp.broadcast_to(ms[rows] + log_s, (sub, LANES))
        for c in range(0, seq, LANES):
            g = jnp.exp2(v_scr[rows, c : c + LANES] - z_s) - jnp.exp2(u_scr[rows, c : c + LANES] - z_t)
            g_scr[rows, c : c + LANES] = g.astype(jnp.bfloat16)
    kl_ref[pl.ds(step, 1), :] = jnp.transpose(kl_scr[...])[:1]
    acc = jnp.zeros((block, s_all.shape[1]), jnp.float32)
    for c in range(0, seq, chunk):
        g = g_scr[:, c : c + chunk]
        acc = acc + jnp.dot(g, s_all[c : c + chunk, :], preferred_element_type=jnp.float32)
        grad_ref[c : c + chunk, :] += lax.dot_general(g, sr, CONTRACT_FIRST, preferred_element_type=jnp.float32)
    start = pl.multiple_of(lax.axis_index("zh") * (seq // 2) + step * block, block)
    grad_ref[pl.ds(start, block), :] += acc

    @pl.when(step == pl.num_programs(0) - 1)
    def _():
        grad_ref[...] = grad_ref[...] * student_scale


def relation(t_all, s_all, block=256, chunk=512, sub=32):
    seq, t_width = t_all.shape
    s_width = s_all.shape[1]
    rows = seq // 2
    steps = rows // block

    def row_map(i):
        return (lax.axis_index("zh") * steps + i, 0)

    def whole(i):
        return (0, 0)

    return pl.pallas_call(
        functools.partial(relation_kernel, block, chunk, sub),
        grid=(steps,),
        in_specs=[
            pl.BlockSpec((block, t_width), row_map),
            pl.BlockSpec((block, s_width), row_map),
            pl.BlockSpec((seq, t_width), whole),
            pl.BlockSpec((seq, s_width), whole),
        ],
        out_specs=[
            pl.BlockSpec((steps, block), whole),
            pl.BlockSpec((seq, s_width), whole),
        ],
        out_shape=[
            jax.ShapeDtypeStruct((steps, block), jnp.float32),
            jax.ShapeDtypeStruct((seq, s_width), jnp.float32),
        ],
        scratch_shapes=[
            pltpu.VMEM((block, seq), jnp.float32),
            pltpu.VMEM((block, seq), jnp.float32),
            pltpu.VMEM((block, seq), jnp.bfloat16),
            pltpu.VMEM((block, LANES), jnp.float32),
        ],
        compiler_params=pltpu.CompilerParams(vmem_limit_bytes=56 << 20),
    )(t_all, s_all, t_all, s_all)


def exchange(chunks, axes):
    return lax.all_to_all(chunks, axes, split_axis=0, concat_axis=0, tiled=True)


def owned_rows(kl):
    mine = lax.axis_index("xh")

    def moved(flip):
        pairs = []
        for source in range(32):
            xh, xl, zh, zl, yh = ((source >> k) & 1 for k in (4, 3, 2, 1, 0))
            pairs.append((source, zl * 16 + yh * 8 + xl * 4 + zh * 2 + (xh ^ flip)))
        return lax.ppermute(jnp.where(mine == flip, kl[0], kl[1])[None], DP, pairs)

    same, other = moved(0), moved(1)
    first = lax.axis_index("yh") == 0
    return jnp.concatenate([jnp.where(first, same, other), jnp.where(first, other, same)], axis=1)


def local(teacher_query, student_hidden, query_weight):
    rows = teacher_query.shape[0]
    depth, columns = query_weight.shape
    t_width = teacher_query.shape[1] // 8
    s_width = columns // 8
    width = columns // 4
    hidden = lax.all_gather(student_hidden, TP + COLUMN, axis=0, tiled=True)
    hidden = hidden.reshape(4, 4 * rows, columns)
    parts = jnp.moveaxis(query_weight.reshape(depth, 4, width), 1, 0)
    weight = exchange(jnp.broadcast_to(parts, (8, 4, depth, width)).reshape(32, depth, width), DP)
    weight = weight.reshape(4, 8 * depth, width)
    heads = jnp.moveaxis(teacher_query.reshape(rows, 4, 2, t_width), 0, 2)
    heads = jnp.moveaxis(heads, 1, 0)[:, None]
    heads = jnp.broadcast_to(heads, (2, 2, 4, rows, t_width)).reshape(16, rows, t_width)
    teacher = exchange(heads, BLOCK + COLUMN).reshape(SEQ, t_width)
    student = lax.dot_general(
        hidden, weight, (((0, 2), (0, 1)), ((), ())), preferred_element_type=jnp.float32
    ).astype(jnp.bfloat16)
    pair = jnp.moveaxis(student.reshape(4 * rows, 2, s_width), 1, 0)[:, None]
    pair = jnp.broadcast_to(pair, (2, 2, 4 * rows, s_width)).reshape(4, 4 * rows, s_width)
    student_all = exchange(pair, BLOCK).reshape(SEQ, s_width)
    kl, grad = relation(teacher, student_all)
    terms = exchange(grad.reshape(4, 4 * rows, s_width), BLOCK)
    terms = terms.reshape(2, 2, 4 * rows, s_width)
    summed = (terms[:, 0] + terms[:, 1]).astype(jnp.bfloat16)
    query_grad = jnp.moveaxis(summed, 0, 1).reshape(4 * rows, width)
    partial = lax.dot_general(
        hidden, query_grad, (((1,), (0,)), ((), ())), preferred_element_type=jnp.float32
    )
    sent = exchange(partial.astype(jnp.bfloat16).reshape(32, depth, width), DP)
    sent = sent.reshape(8, 4, depth, width)
    total = sent[0].astype(jnp.float32)
    for i in range(1, 8):
        total = total + sent[i].astype(jnp.float32)
    weight_grad = jnp.moveaxis(total, 0, 1).reshape(depth, columns)
    return owned_rows(kl.reshape(2, SEQ // 4)), weight_grad


def solution(mesh):
    bits = Mesh(mesh.devices.reshape((2,) * 7), TP + DP)
    return jax.shard_map(
        local,
        mesh=bits,
        in_specs=(P(DP, TP), P(DP, TP), P(DP, TP)),
        out_specs=(P(TP + DP, None), P(DP, TP)),
        check_vma=False,
    )
```

```python
import functools

import jax
import jax.numpy as jnp
from jax import lax
from jax.experimental import pallas as pl
from jax.experimental.pallas import tpu as pltpu
from jax.sharding import Mesh, PartitionSpec as P

LOG2E = 1.4426950408889634
LN2 = 0.6931471805599453
LANES = 128

TP = ("yl", "core")
DP = ("xh", "xl", "zh", "zl", "yh")
BLOCK = ("zh", "yh")
SPREAD = ("zh", "yh", "xl", "zl")
SWAP = [(0, 1), (1, 0)]

CONTRACT_LAST = (((1,), (1,)), ((), ()))
CONTRACT_FIRST = (((0,), (0,)), ((), ()))
WHOLE = pl.BlockSpec(memory_space=pltpu.VMEM)


def swap(value, axis):
    return lax.ppermute(value, axis, SWAP)


def exchange(chunks, axes):
    return lax.all_to_all(chunks, axes, split_axis=0, concat_axis=0, tiled=True)


RUNS = ((0, 96, (0, 1, 2)), (96, 176, (1, 2, 0)), (176, 256, (2, 0, 1)))
CUBE = ("xl", "yl", "zl")


def gather_cube(share):
    held = [share[None, first:last] for first, last, _ in RUNS]
    far = held
    for stage in range(3):
        far = [swap(piece, CUBE[order[stage]]) for piece, (_, _, order) in zip(held, RUNS)]
        if stage < 2:
            held = [jnp.concatenate(both) for both in zip(held, far)]
    return [piece for both in zip(held, far) for piece in both]


def run_piece(refs, run, hops, first, last):
    order = RUNS[run][2]
    place = sum(hops[order[k]] << k for k in range(3))
    return refs[2 * run + place // 4][place % 4, first:last, :]


def hidden_tile(refs, dy, rel):
    rows = []
    for dx in range(2):
        for dz in range(2):
            hops = (dx, dy, dz)
            if rel == 0:
                rows += [run_piece(refs, 0, hops, 0, 96), run_piece(refs, 1, hops, 0, 32)]
            else:
                rows += [run_piece(refs, 1, hops, 32, 80), run_piece(refs, 2, hops, 0, 80)]
    return jnp.concatenate(rows, axis=0)


def token_place(dx, dz):
    return (lax.axis_index("xl") ^ dx) * 2 + (lax.axis_index("zl") ^ dz)


def project_kernel(*refs):
    hidden, (w_own, w_other, out) = refs[:6], refs[6:]
    core = lax.axis_index("core")
    features = w_own.shape[0] // 4
    parts = [None, None]
    for dy in range(2):
        for rel in range(2):
            tile = hidden_tile(hidden, dy, rel)
            block = (lax.axis_index("yl") ^ dy) * 2 + (core ^ rel)
            depth = pl.ds(pl.multiple_of(block * features, features), features)
            for i, weight in enumerate((w_own, w_other)):
                term = jnp.dot(tile, weight[depth, :], preferred_element_type=jnp.float32)
                parts[i] = term if parts[i] is None else parts[i] + term
    for i in range(2):
        value = parts[i].astype(jnp.bfloat16)
        for j in range(2):
            for dx in range(2):
                for dz in range(2):
                    at = (dx * 2 + dz) * 128
                    rows = pl.ds(pl.multiple_of(token_place(dx, dz) * 128, 128), 128)
                    out[(core ^ i) * 2 + j, rows, :] = value[at : at + 128, j * 128 : (j + 1) * 128]


def project(hidden, w_own, w_other):
    return pl.pallas_call(
        project_kernel,
        in_specs=[WHOLE] * 8,
        out_specs=WHOLE,
        out_shape=jax.ShapeDtypeStruct((4, 512, 128), jnp.bfloat16),
        compiler_params=pltpu.CompilerParams(vmem_limit_bytes=48 << 20),
    )(*hidden, w_own, w_other)


def weight_grad_kernel(*refs):
    own, other, (q_own, q_other, out) = refs[:6], refs[6:12], refs[12:]
    core = lax.axis_index("core")

    def in_place(ref):
        rows = []
        for dx in range(2):
            for dz in range(2):
                at = pl.ds(pl.multiple_of(token_place(dx, dz) * 128, 128), 128)
                rows.append(jnp.concatenate([ref[0, at, :], ref[1, at, :]], axis=1))
        return rows

    grad = jnp.concatenate(in_place(q_own) + in_place(q_other), axis=0)
    for dy in range(2):
        for rel in range(2):
            tile = jnp.concatenate([hidden_tile(own, dy, rel), hidden_tile(other, dy, 1 - rel)], axis=0)
            block = (lax.axis_index("yl") ^ dy) * 2 + (core ^ rel)
            value = lax.dot_general(tile, grad, CONTRACT_FIRST, preferred_element_type=jnp.float32)
            count = value.shape[0] // 128
            out[pl.ds(block * count, count)] = value.astype(jnp.bfloat16).reshape(count, 128, value.shape[1])


def weight_grad_part(own, other, q_own, q_other):
    return pl.pallas_call(
        weight_grad_kernel,
        in_specs=[WHOLE] * 14,
        out_specs=WHOLE,
        out_shape=jax.ShapeDtypeStruct((32, 128, 256), jnp.bfloat16),
        compiler_params=pltpu.CompilerParams(vmem_limit_bytes=48 << 20),
    )(*own, *other, q_own, q_other)


def lane_fold(x, op):
    acc = x[:, :LANES]
    for j in range(1, x.shape[1] // LANES):
        acc = op(acc, x[:, j * LANES : (j + 1) * LANES])
    return acc


def relation_kernel(
    block, chunk, sub, t_own, s_own, t_other, s_other, kl_ref, own_ref, other_ref, u_scr, v_scr, g_scr, kl_scr
):
    step = pl.program_id(0)
    half = t_own.shape[0]
    width = s_own.shape[1]
    student_scale = width**-0.5
    t_mul = LOG2E * t_own.shape[1] ** -0.5
    s_mul = LOG2E * student_scale

    @pl.when(step == 0)
    def _():
        own_ref[...] = jnp.zeros_like(own_ref)
        other_ref[...] = jnp.zeros_like(other_ref)

    mine = pl.ds(pl.multiple_of(step * block, block), block)
    tr = t_own[mine, :]
    sr = s_own[mine, :]
    keys = [(t, s, g, c) for t, s, g in ((t_own, s_own, own_ref), (t_other, s_other, other_ref)) for c in range(0, half, chunk)]
    mt = ms = None
    for i, (t_keys, s_keys, _, c) in enumerate(keys):
        at = slice(i * chunk, (i + 1) * chunk)
        u = t_mul * lax.dot_general(tr, t_keys[c : c + chunk, :], CONTRACT_LAST, preferred_element_type=jnp.float32)
        u_scr[:, at] = u
        fold = lane_fold(u, jnp.maximum)
        mt = fold if mt is None else jnp.maximum(mt, fold)
        v = s_mul * lax.dot_general(sr, s_keys[c : c + chunk, :], CONTRACT_LAST, preferred_element_type=jnp.float32)
        v_scr[:, at] = v
        fold = lane_fold(v, jnp.maximum)
        ms = fold if ms is None else jnp.maximum(ms, fold)
    mt = jnp.max(mt, axis=1, keepdims=True)
    ms = jnp.max(ms, axis=1, keepdims=True)
    for r in range(0, block, sub):
        rows = slice(r, r + sub)
        m_t = jnp.broadcast_to(mt[rows], (sub, LANES))
        m_s = jnp.broadcast_to(ms[rows], (sub, LANES))
        zero = jnp.zeros((sub, LANES), jnp.float32)
        lt, ls, a = zero, zero, zero
        for c in range(0, 2 * half, LANES):
            x = u_scr[rows, c : c + LANES] - m_t
            y = v_scr[rows, c : c + LANES] - m_s
            et = jnp.exp2(x)
            lt = lt + et
            ls = ls + jnp.exp2(y)
            a = a + et * (x - y)
        lt = jnp.sum(lt, axis=1, keepdims=True)
        ls = jnp.sum(ls, axis=1, keepdims=True)
        a = jnp.sum(a, axis=1, keepdims=True)
        log_t = jnp.log2(lt)
        log_s = jnp.log2(ls)
        kl = (a / lt - log_t + log_s) * LN2
        kl_scr[rows, :] = jnp.broadcast_to(kl, (sub, LANES))
        z_t = jnp.broadcast_to(mt[rows] + log_t, (sub, LANES))
        z_s = jnp.broadcast_to(ms[rows] + log_s, (sub, LANES))
        for c in range(0, 2 * half, LANES):
            g = jnp.exp2(v_scr[rows, c : c + LANES] - z_s) - jnp.exp2(u_scr[rows, c : c + LANES] - z_t)
            g_scr[rows, c : c + LANES] = g.astype(jnp.bfloat16)
    kl_ref[pl.ds(step, 1), :] = jnp.transpose(kl_scr[...])[:1]
    acc = jnp.zeros((block, width), jnp.float32)
    for i, (_, s_keys, g_ref, c) in enumerate(keys):
        g = g_scr[:, i * chunk : (i + 1) * chunk]
        acc = acc + jnp.dot(g, s_keys[c : c + chunk, :], preferred_element_type=jnp.float32)
        g_ref[c : c + chunk, :] += lax.dot_general(g, sr, CONTRACT_FIRST, preferred_element_type=jnp.float32)
    own_ref[mine, :] += acc

    @pl.when(step == pl.num_programs(0) - 1)
    def _():
        own_ref[...] = own_ref[...] * student_scale
        other_ref[...] = other_ref[...] * student_scale


def relation(t_own, s_own, t_other, s_other, block=256, chunk=512, sub=32):
    half, t_width = t_own.shape
    s_width = s_own.shape[1]
    steps = half // block

    def whole(*shape):
        return pl.BlockSpec(shape, lambda i: (0, 0))

    return pl.pallas_call(
        functools.partial(relation_kernel, block, chunk, sub),
        grid=(steps,),
        in_specs=[whole(half, t_width), whole(half, s_width)] * 2,
        out_specs=[whole(steps, block), whole(half, s_width), whole(half, s_width)],
        out_shape=[
            jax.ShapeDtypeStruct((steps, block), jnp.float32),
            jax.ShapeDtypeStruct((half, s_width), jnp.float32),
            jax.ShapeDtypeStruct((half, s_width), jnp.float32),
        ],
        scratch_shapes=[
            pltpu.VMEM((block, 2 * half), jnp.float32),
            pltpu.VMEM((block, 2 * half), jnp.float32),
            pltpu.VMEM((block, 2 * half), jnp.bfloat16),
            pltpu.VMEM((block, LANES), jnp.float32),
        ],
        compiler_params=pltpu.CompilerParams(vmem_limit_bytes=50 << 20),
    )(t_own, s_own, t_other, s_other)


def owned_rows(kl):
    kl = kl.reshape(2, 2, 2, 2, LANES).transpose(2, 0, 3, 1, 4).reshape(4, 4, LANES)
    source = lax.axis_index("xh") * 2 + lax.axis_index("core")
    got = []
    for turn in range(4):
        pairs = []
        for c in range(2):
            for dp in range(32):
                xh, xl, zh, zl, yh = ((dp >> k) & 1 for k in (4, 3, 2, 1, 0))
                quarter = turn ^ (xh * 2 + c)
                pairs.append((c * 32 + dp, zh * 32 + xl * 16 + zl * 8 + yh * 4 + quarter))
        sent = lax.dynamic_index_in_dim(kl, turn ^ source, 0, keepdims=False)
        got.append(lax.ppermute(sent, ("core",) + DP, pairs))
    got = jnp.stack(got)
    quarter = lax.axis_index(DP) % 4
    rows = [lax.dynamic_index_in_dim(got, f ^ quarter, 0, keepdims=False) for f in range(4)]
    rows = jnp.stack(rows).reshape(2, 2, 4, LANES)
    return rows.transpose(0, 2, 1, 3).reshape(1, 2 * 4 * 2 * LANES)


def local(teacher_query, student_hidden, query_weight):
    rows = teacher_query.shape[0]
    depth, columns = query_weight.shape
    t_width = teacher_query.shape[1] // 8
    width = columns // 4
    core = lax.axis_index("core")
    low = core == 0

    def token_halves(value):
        first, second = value[: rows // 2], value[rows // 2 :]
        return jnp.where(low, first, second), swap(jnp.where(low, second, first), "core")

    hidden = gather_cube(jnp.concatenate(token_halves(student_hidden)))
    parts = jnp.moveaxis(query_weight.reshape(depth, 2, 1, 2, 1, width), 0, 4)
    w_own = exchange(jnp.broadcast_to(parts, (2, 2, 2, 2, 2, depth, width)).reshape(32, depth, width), DP)
    w_own = w_own.reshape(32 * depth, width)
    w_other = swap(w_own, "core")
    student = exchange(project(hidden, w_own, w_other), BLOCK).reshape(2048, -1)
    student_other = swap(student, "core")
    t_own, t_other = token_halves(teacher_query)
    heads = jnp.stack([jnp.where(low, t_own, t_other), jnp.where(low, t_other, t_own)])
    heads = heads.reshape(2, rows // 2, 2, 2, 2, t_width).transpose(0, 4, 2, 3, 1, 5)
    teacher = exchange(heads.reshape(16, rows // 2, t_width), SPREAD).reshape(2048, t_width)
    teacher_other = swap(teacher, "core")

    kl, grad, grad_other = relation(teacher, student, teacher_other, student_other)
    hidden_other = [swap(piece, "core") for piece in hidden]
    query_grad = (grad + swap(grad_other, "core")).astype(jnp.bfloat16)
    query_grad = exchange(query_grad.reshape(4, 512, -1), BLOCK).reshape(2, 2, 512, -1)
    mine = jnp.where(low, query_grad[0], query_grad[1])
    theirs = swap(jnp.where(low, query_grad[1], query_grad[0]), "core")
    sent = exchange(weight_grad_part(hidden, hidden_other, mine, theirs), DP)
    kl_rows = owned_rows(kl)
    sent = sent.reshape(2, 2, 2, 2, 2, depth, width)
    total = None
    for xh in range(2):
        for zh in range(2):
            for yh in range(2):
                term = sent[xh, :, zh, :, yh].astype(jnp.float32)
                total = term if total is None else total + term
    return kl_rows, total.reshape(4, depth, width).transpose(1, 0, 2).reshape(depth, columns)


def solution(mesh):
    bits = Mesh(mesh.devices.reshape((2,) * 7), TP + DP)
    return jax.shard_map(
        local,
        mesh=bits,
        in_specs=(P(DP, TP), P(DP, TP), P(DP, TP)),
        out_specs=(P(TP + DP, None), P(DP, TP)),
        check_vma=False,
    )
```

```python
import functools

import jax
import jax.numpy as jnp
from jax import lax
from jax.experimental import pallas as pl
from jax.experimental.pallas import tpu as pltpu
from jax.sharding import Mesh, PartitionSpec as P

LOG2E = 1.4426950408889634
LN2 = 0.6931471805599453
LANES = 128

TP = ("yl", "core")
DP = ("xh", "xl", "zh", "zl", "yh")
BLOCK = ("zh", "yh")
SPREAD = ("zh", "yh", "xl", "zl")
SWAP = [(0, 1), (1, 0)]

CONTRACT_LAST = (((1,), (1,)), ((), ()))
CONTRACT_FIRST = (((0,), (0,)), ((), ()))
WHOLE = pl.BlockSpec(memory_space=pltpu.VMEM)


def swap(value, axis):
    return lax.ppermute(value, axis, SWAP)


def exchange(chunks, axes):
    return lax.all_to_all(chunks, axes, split_axis=0, concat_axis=0, tiled=True)


RUNS = ((0, 96, (0, 1, 2)), (96, 176, (1, 2, 0)), (176, 256, (2, 0, 1)))
CUBE = ("xl", "yl", "zl")


def hop(held, stage):
    return [swap(piece, CUBE[order[stage]]) for piece, (_, _, order) in zip(held, RUNS)]


def joined(held, far):
    return [jnp.concatenate(both) for both in zip(held, far)]


def trade(chunks):
    got = [chunks[0]]
    for r in range(1, 4):
        got.append(lax.ppermute(chunks[r], BLOCK, [(i, i ^ r) for i in range(4)]))
    return got


def after(value, *others):
    return lax.optimization_barrier((value, *others))[0]


def run_piece(refs, run, hops, first, last):
    order = RUNS[run][2]
    place = sum(hops[order[k]] << k for k in range(3))
    return refs[2 * run + place // 4][place % 4, first:last, :]


def hidden_tile(refs, dy, rel):
    rows = []
    for dx in range(2):
        for dz in range(2):
            hops = (dx, dy, dz)
            if rel == 0:
                rows += [run_piece(refs, 0, hops, 0, 96), run_piece(refs, 1, hops, 0, 32)]
            else:
                rows += [run_piece(refs, 1, hops, 32, 80), run_piece(refs, 2, hops, 0, 80)]
    return jnp.concatenate(rows, axis=0)


def token_place(dx, dz):
    return (lax.axis_index("xl") ^ dx) * 2 + (lax.axis_index("zl") ^ dz)


def project_kernel(*refs):
    hidden, (w_own, w_other, out) = refs[:6], refs[6:]
    core = lax.axis_index("core")
    features = w_own.shape[0] // 4
    parts = [None, None]
    for dy in range(2):
        for rel in range(2):
            tile = hidden_tile(hidden, dy, rel)
            block = (lax.axis_index("yl") ^ dy) * 2 + (core ^ rel)
            depth = pl.ds(pl.multiple_of(block * features, features), features)
            for i, weight in enumerate((w_own, w_other)):
                term = jnp.dot(tile, weight[depth, :], preferred_element_type=jnp.float32)
                parts[i] = term if parts[i] is None else parts[i] + term
    for i in range(2):
        value = parts[i].astype(jnp.bfloat16)
        for j in range(2):
            for dx in range(2):
                for dz in range(2):
                    at = (dx * 2 + dz) * 128
                    rows = pl.ds(pl.multiple_of(token_place(dx, dz) * 128, 128), 128)
                    slot = (core ^ i ^ lax.axis_index("zh")) * 2 + (lax.axis_index("yh") ^ j)
                    out[slot, rows, :] = value[at : at + 128, j * 128 : (j + 1) * 128]


def project(hidden, w_own, w_other):
    return pl.pallas_call(
        project_kernel,
        in_specs=[WHOLE] * 8,
        out_specs=WHOLE,
        out_shape=jax.ShapeDtypeStruct((4, 512, 128), jnp.bfloat16),
        cost_estimate=pl.CostEstimate(flops=2 * 512 * 4096 * 512, bytes_accessed=9 << 20, transcendentals=0),
        compiler_params=pltpu.CompilerParams(vmem_limit_bytes=48 << 20),
    )(*hidden, w_own, w_other)


def weight_grad_kernel(*refs):
    own, other, (q_own, q_other, out) = refs[:6], refs[6:12], refs[12:]
    core = lax.axis_index("core")

    def in_place(ref):
        rows = []
        for dx in range(2):
            for dz in range(2):
                at = pl.ds(pl.multiple_of(token_place(dx, dz) * 128, 128), 128)
                yh = lax.axis_index("yh")
                rows.append(jnp.concatenate([ref[yh, at, :], ref[1 - yh, at, :]], axis=1))
        return rows

    grad = jnp.concatenate(in_place(q_own) + in_place(q_other), axis=0)
    for dy in range(2):
        for rel in range(2):
            tile = jnp.concatenate([hidden_tile(own, dy, rel), hidden_tile(other, dy, 1 - rel)], axis=0)
            block = (lax.axis_index("yl") ^ dy) * 2 + (core ^ rel)
            value = lax.dot_general(tile, grad, CONTRACT_FIRST, preferred_element_type=jnp.float32)
            count = value.shape[0] // 128
            out[pl.ds(block * count, count)] = value.astype(jnp.bfloat16).reshape(count, 128, value.shape[1])


def weight_grad_part(own, other, q_own, q_other):
    return pl.pallas_call(
        weight_grad_kernel,
        in_specs=[WHOLE] * 14,
        out_specs=WHOLE,
        out_shape=jax.ShapeDtypeStruct((32, 128, 256), jnp.bfloat16),
        cost_estimate=pl.CostEstimate(flops=2 * 1024 * 4096 * 256, bytes_accessed=11 << 20, transcendentals=0),
        compiler_params=pltpu.CompilerParams(vmem_limit_bytes=48 << 20),
    )(*own, *other, q_own, q_other)


def lane_fold(x, op):
    acc = x[:, :LANES]
    for j in range(1, x.shape[1] // LANES):
        acc = op(acc, x[:, j * LANES : (j + 1) * LANES])
    return acc


def relation_kernel(
    block, chunk, sub, t_own, s_own, t_other, s_other, kl_ref, own_ref, other_ref, u_scr, v_scr, g_scr, kl_scr
):
    step = pl.program_id(0)
    half = t_own.shape[0]
    width = s_own.shape[1]
    student_scale = width**-0.5
    t_mul = LOG2E * t_own.shape[1] ** -0.5
    s_mul = LOG2E * student_scale

    @pl.when(step == 0)
    def _():
        own_ref[...] = jnp.zeros_like(own_ref)
        other_ref[...] = jnp.zeros_like(other_ref)

    here = lax.axis_index("zh") * 2 + lax.axis_index("yh")
    part = half // 4

    def in_order(row):
        return (row // part ^ here) * part + row % part

    mine = pl.ds(pl.multiple_of(step * block, block), block)
    first = pl.multiple_of(in_order(step * block), block)
    tr = t_own[pl.ds(first, block), :]
    sr = s_own[mine, :]
    keys = [(t, s, g, c) for t, s, g in ((t_own, s_own, own_ref), (t_other, s_other, other_ref)) for c in range(0, half, chunk)]
    mt = ms = None
    for i, (t_keys, s_keys, _, c) in enumerate(keys):
        at = slice(i * chunk, (i + 1) * chunk)
        t_at = pl.ds(pl.multiple_of(in_order(c), chunk), chunk)
        u = t_mul * lax.dot_general(tr, t_keys[t_at, :], CONTRACT_LAST, preferred_element_type=jnp.float32)
        u_scr[:, at] = u
        fold = lane_fold(u, jnp.maximum)
        mt = fold if mt is None else jnp.maximum(mt, fold)
        v = s_mul * lax.dot_general(sr, s_keys[c : c + chunk, :], CONTRACT_LAST, preferred_element_type=jnp.float32)
        v_scr[:, at] = v
        fold = lane_fold(v, jnp.maximum)
        ms = fold if ms is None else jnp.maximum(ms, fold)
    mt = jnp.max(mt, axis=1, keepdims=True)
    ms = jnp.max(ms, axis=1, keepdims=True)
    for r in range(0, block, sub):
        rows = slice(r, r + sub)
        m_t = jnp.broadcast_to(mt[rows], (sub, LANES))
        m_s = jnp.broadcast_to(ms[rows], (sub, LANES))
        zero = jnp.zeros((sub, LANES), jnp.float32)
        lt, ls, a = zero, zero, zero
        for c in range(0, 2 * half, LANES):
            x = u_scr[rows, c : c + LANES] - m_t
            y = v_scr[rows, c : c + LANES] - m_s
            et = jnp.exp2(x)
            lt = lt + et
            ls = ls + jnp.exp2(y)
            a = a + et * (x - y)
        lt = jnp.sum(lt, axis=1, keepdims=True)
        ls = jnp.sum(ls, axis=1, keepdims=True)
        a = jnp.sum(a, axis=1, keepdims=True)
        log_t = jnp.log2(lt)
        log_s = jnp.log2(ls)
        kl = (a / lt - log_t + log_s) * LN2
        kl_scr[rows, :] = jnp.broadcast_to(kl, (sub, LANES))
        z_t = jnp.broadcast_to(mt[rows] + log_t, (sub, LANES))
        z_s = jnp.broadcast_to(ms[rows] + log_s, (sub, LANES))
        for c in range(0, 2 * half, LANES):
            g = jnp.exp2(v_scr[rows, c : c + LANES] - z_s) - jnp.exp2(u_scr[rows, c : c + LANES] - z_t)
            g_scr[rows, c : c + LANES] = g.astype(jnp.bfloat16)
    kl_ref[pl.ds(first // block, 1), :] = jnp.transpose(kl_scr[...])[:1]
    acc = jnp.zeros((block, width), jnp.float32)
    for i, (_, s_keys, g_ref, c) in enumerate(keys):
        g = g_scr[:, i * chunk : (i + 1) * chunk]
        acc = acc + jnp.dot(g, s_keys[c : c + chunk, :], preferred_element_type=jnp.float32)
        g_ref[c : c + chunk, :] += lax.dot_general(g, sr, CONTRACT_FIRST, preferred_element_type=jnp.float32)
    own_ref[mine, :] += acc

    @pl.when(step == pl.num_programs(0) - 1)
    def _():
        own_ref[...] = own_ref[...] * student_scale
        other_ref[...] = other_ref[...] * student_scale


def relation(t_own, s_own, t_other, s_other, block=256, chunk=512, sub=32):
    half, t_width = t_own.shape
    s_width = s_own.shape[1]
    steps = half // block

    def whole(*shape):
        return pl.BlockSpec(shape, lambda i: (0, 0))

    return pl.pallas_call(
        functools.partial(relation_kernel, block, chunk, sub),
        grid=(steps,),
        in_specs=[whole(half, t_width), whole(half, s_width)] * 2,
        out_specs=[whole(steps, block), whole(half, s_width), whole(half, s_width)],
        out_shape=[
            jax.ShapeDtypeStruct((steps, block), jnp.float32),
            jax.ShapeDtypeStruct((half, s_width), jnp.float32),
            jax.ShapeDtypeStruct((half, s_width), jnp.float32),
        ],
        scratch_shapes=[
            pltpu.VMEM((block, 2 * half), jnp.float32),
            pltpu.VMEM((block, 2 * half), jnp.float32),
            pltpu.VMEM((block, 2 * half), jnp.bfloat16),
            pltpu.VMEM((block, LANES), jnp.float32),
        ],
        cost_estimate=pl.CostEstimate(
            flops=2 * half * 2 * half * (t_width + 3 * s_width),
            bytes_accessed=6 * half * (t_width + 3 * s_width),
            transcendentals=8 * half * half,
        ),
        compiler_params=pltpu.CompilerParams(vmem_limit_bytes=50 << 20),
    )(t_own, s_own, t_other, s_other)


def owned_rows(kl):
    kl = kl.reshape(2, 2, 2, 2, LANES).transpose(2, 0, 3, 1, 4).reshape(4, 4, LANES)
    source = lax.axis_index("xh") * 2 + lax.axis_index("core")
    got = []
    for turn in range(4):
        pairs = []
        for c in range(2):
            for dp in range(32):
                xh, xl, zh, zl, yh = ((dp >> k) & 1 for k in (4, 3, 2, 1, 0))
                quarter = turn ^ (xh * 2 + c)
                pairs.append((c * 32 + dp, zh * 32 + xl * 16 + zl * 8 + yh * 4 + quarter))
        sent = lax.dynamic_index_in_dim(kl, turn ^ source, 0, keepdims=False)
        got.append(lax.ppermute(sent, ("core",) + DP, pairs))
    got = jnp.stack(got)
    quarter = lax.axis_index(DP) % 4
    rows = [lax.dynamic_index_in_dim(got, f ^ quarter, 0, keepdims=False) for f in range(4)]
    rows = jnp.stack(rows).reshape(2, 2, 4, LANES)
    return rows.transpose(0, 2, 1, 3).reshape(1, 2 * 4 * 2 * LANES)


def local(teacher_query, student_hidden, query_weight):
    rows = teacher_query.shape[0]
    depth, columns = query_weight.shape
    t_width = teacher_query.shape[1] // 8
    width = columns // 4
    core = lax.axis_index("core")
    low = core == 0

    def token_halves(value):
        first, second = value[: rows // 2], value[rows // 2 :]
        return jnp.where(low, first, second), swap(jnp.where(low, second, first), "core")

    share = jnp.concatenate(token_halves(student_hidden))
    held = [share[None, first:last] for first, last, _ in RUNS]
    far = hop(held, 0)
    parts = jnp.moveaxis(query_weight.reshape(depth, 2, 1, 2, 1, width), 0, 4)
    parts = jnp.broadcast_to(parts, (2, 2, 2, 2, 2, depth, width)).reshape(32, depth, width)
    w_own = exchange(after(parts, *far), DP)
    held = joined(held, far)
    far = hop(held, 1)
    t_own, t_other = token_halves(teacher_query)
    heads = jnp.stack([jnp.where(low, t_own, t_other), jnp.where(low, t_other, t_own)])
    heads = heads.reshape(2, rows // 2, 2, 2, 2, t_width).transpose(0, 4, 2, 3, 1, 5)
    heads = heads.reshape(16, rows // 2, t_width)
    held = joined(held, far)
    w_own = after(w_own, *held).reshape(32 * depth, width)
    w_other = swap(w_own, "core")
    far = hop(held, 2)
    hidden = [piece for both in zip(held, far) for piece in both]
    teacher = exchange(after(heads, *far), SPREAD).reshape(2048, t_width)
    student = jnp.concatenate(trade(project(hidden, w_own, w_other)))
    teacher = after(teacher, student)
    hidden_other = [swap(piece, "core") for piece in hidden]
    teacher_other = swap(teacher, "core")
    student_other = swap(student, "core")

    kl, grad, grad_other = relation(after(teacher, *hidden_other), student, teacher_other, student_other)
    query_grad = (grad + swap(grad_other, "core")).astype(jnp.bfloat16)
    query_grad = trade(query_grad.reshape(4, 512, -1))
    near, away = jnp.stack(query_grad[:2]), jnp.stack(query_grad[2:])
    same = core == lax.axis_index("zh")
    mine = jnp.where(same, near, away)
    theirs = swap(jnp.where(same, away, near), "core")
    kl_rows = owned_rows(kl)
    sent = exchange(weight_grad_part(hidden, hidden_other, mine, after(theirs, kl_rows)), DP)
    sent = sent.reshape(2, 2, 2, 2, 2, depth, width)
    total = None
    for xh in range(2):
        for zh in range(2):
            for yh in range(2):
                term = sent[xh, :, zh, :, yh].astype(jnp.float32)
                total = term if total is None else total + term
    return kl_rows, total.reshape(4, depth, width).transpose(1, 0, 2).reshape(depth, columns)


def solution(mesh):
    bits = Mesh(mesh.devices.reshape((2,) * 7), TP + DP)
    return jax.shard_map(
        local,
        mesh=bits,
        in_specs=(P(DP, TP), P(DP, TP), P(DP, TP)),
        out_specs=(P(TP + DP, None), P(DP, TP)),
        check_vma=False,
    )
```

```python
import functools

import jax
import jax.numpy as jnp
from jax import lax
from jax.experimental import pallas as pl
from jax.experimental.pallas import tpu as pltpu
from jax.sharding import Mesh, PartitionSpec as P

LOG2E = 1.4426950408889634
LN2 = 0.6931471805599453
LANES = 128

TP = ("yl", "core")
DP = ("xh", "xl", "zh", "zl", "yh")
BLOCK = ("zh", "yh")
SPREAD = ("zh", "yh", "xl", "zl")
XZ = (("xh", "xl"), ("zh", "zl"))
SWAP = [(0, 1), (1, 0)]

CONTRACT_LAST = (((1,), (1,)), ((), ()))
CONTRACT_FIRST = (((0,), (0,)), ((), ()))
WHOLE = pl.BlockSpec(memory_space=pltpu.VMEM)


def swap(value, axis):
    return lax.ppermute(value, axis, SWAP)


def exchange(chunks, axes):
    return lax.all_to_all(chunks, axes, split_axis=0, concat_axis=0, tiled=True)


RUNS = ((0, 96, (0, 1, 2)), (96, 176, (1, 2, 0)), (176, 256, (2, 0, 1)))
CUBE = ("xl", "yl", "zl")


def hop(held, stage):
    return [swap(piece, CUBE[order[stage]]) for piece, (_, _, order) in zip(held, RUNS)]


def joined(held, far):
    return [jnp.concatenate(both) for both in zip(held, far)]


def trade(chunks):
    got = [chunks[0]]
    for r in range(1, 4):
        step = (r >> 1) * 6 + (r & 1)
        got.append(lax.ppermute(chunks[r], ("zh", "zl", "yh"), [(i, i ^ step) for i in range(8)]))
    return got


def gather_weight(weight):
    depth, columns = weight.shape
    parts = jnp.moveaxis(weight.reshape(depth, 4, columns // 4), 1, 0)
    q = (lax.axis_index("xh") ^ lax.axis_index("xl")) * 2 + (lax.axis_index("zh") ^ lax.axis_index("zl"))
    near = [lax.dynamic_index_in_dim(parts, q ^ r, 0, keepdims=False) for r in range(4)]
    got = []
    for step in range(8):
        part = near[step >> 1]
        if step:
            part = lax.ppermute(part, ("xl", "zl", "yh"), [(i, i ^ step) for i in range(8)])
        got.append(part)
    held = [jnp.stack(got[:4])[None], jnp.stack(got[4:])[None]]
    far = held
    for stage in range(2):
        if stage:
            held = joined(held, far)
        far = [
            lax.ppermute(piece, axes, [(i, i ^ 3) for i in range(4)])
            for piece, axes in zip(held, (XZ, XZ[::-1])[stage])
        ]
    return [piece for both in zip(held, far) for piece in both]


def weight_in_order(refs, out):
    depth = refs[0].shape[2]
    for a in range(2):
        for ex in range(2):
            for ez in range(2):
                first, second = (ez, ex) if a else (ex, ez)
                for b in range(2):
                    for y in range(2):
                        place = (
                            (lax.axis_index("xh") ^ ex) * 16
                            + (lax.axis_index("xl") ^ ex ^ a) * 8
                            + (lax.axis_index("zh") ^ ez) * 4
                            + (lax.axis_index("zl") ^ ez ^ b) * 2
                            + (lax.axis_index("yh") ^ y)
                        )
                        rows = pl.ds(pl.multiple_of(place * depth, depth), depth)
                        out[rows, :] = refs[2 * a + second][first, 2 * b + y]


def after(value, *others):
    return lax.optimization_barrier((value, *others))[0]


def run_piece(refs, run, hops, first, last):
    order = RUNS[run][2]
    place = sum(hops[order[k]] << k for k in range(3))
    return refs[2 * run + place // 4][place % 4, first:last, :]


def hidden_tile(refs, dy, rel):
    rows = []
    for dx in range(2):
        for dz in range(2):
            hops = (dx, dy, dz)
            if rel == 0:
                rows += [run_piece(refs, 0, hops, 0, 96), run_piece(refs, 1, hops, 0, 32)]
            else:
                rows += [run_piece(refs, 1, hops, 32, 80), run_piece(refs, 2, hops, 0, 80)]
    return jnp.concatenate(rows, axis=0)


def token_place(dx, dz):
    return (lax.axis_index("xl") ^ dx) * 2 + (lax.axis_index("zl") ^ dz)


def project_kernel(*refs):
    hidden, (out, w_own, w_other) = refs[:6], refs[14:]
    weight_in_order(refs[6:10], w_own)
    weight_in_order(refs[10:14], w_other)
    core = lax.axis_index("core")
    features = w_own.shape[0] // 4
    parts = [None, None]
    for dy in range(2):
        for rel in range(2):
            tile = hidden_tile(hidden, dy, rel)
            block = (lax.axis_index("yl") ^ dy) * 2 + (core ^ rel)
            depth = pl.ds(pl.multiple_of(block * features, features), features)
            for i, weight in enumerate((w_own, w_other)):
                term = jnp.dot(tile, weight[depth, :], preferred_element_type=jnp.float32)
                parts[i] = term if parts[i] is None else parts[i] + term
    for i in range(2):
        value = parts[i].astype(jnp.bfloat16)
        for j in range(2):
            for dx in range(2):
                for dz in range(2):
                    at = (dx * 2 + dz) * 128
                    rows = pl.ds(pl.multiple_of(token_place(dx, dz) * 128, 128), 128)
                    slot = (core ^ i ^ lax.axis_index("zh")) * 2 + (lax.axis_index("yh") ^ j)
                    out[slot, rows, :] = value[at : at + 128, j * 128 : (j + 1) * 128]


def project(hidden, w_own, w_other):
    return pl.pallas_call(
        project_kernel,
        in_specs=[WHOLE] * 14,
        out_specs=WHOLE,
        out_shape=jax.ShapeDtypeStruct((4, 512, 128), jnp.bfloat16),
        scratch_shapes=[pltpu.VMEM((4096, 256), jnp.bfloat16)] * 2,
        cost_estimate=pl.CostEstimate(flops=2 * 512 * 4096 * 512, bytes_accessed=9 << 20, transcendentals=0),
        compiler_params=pltpu.CompilerParams(vmem_limit_bytes=48 << 20),
    )(*hidden, *w_own, *w_other)


def weight_grad_kernel(*refs):
    own, other, (q_own, q_other, out) = refs[:6], refs[6:12], refs[12:]
    core = lax.axis_index("core")

    def in_place(ref):
        rows = []
        for dx in range(2):
            for dz in range(2):
                at = pl.ds(pl.multiple_of(token_place(dx, dz) * 128, 128), 128)
                yh = lax.axis_index("yh")
                rows.append(jnp.concatenate([ref[yh, at, :], ref[1 - yh, at, :]], axis=1))
        return rows

    grad = jnp.concatenate(in_place(q_own) + in_place(q_other), axis=0)
    for dy in range(2):
        for rel in range(2):
            tile = jnp.concatenate([hidden_tile(own, dy, rel), hidden_tile(other, dy, 1 - rel)], axis=0)
            block = (lax.axis_index("yl") ^ dy) * 2 + (core ^ rel)
            value = lax.dot_general(tile, grad, CONTRACT_FIRST, preferred_element_type=jnp.float32)
            count = value.shape[0] // 128
            out[pl.ds(block * count, count)] = value.astype(jnp.bfloat16).reshape(count, 128, value.shape[1])


def weight_grad_part(own, other, q_own, q_other):
    return pl.pallas_call(
        weight_grad_kernel,
        in_specs=[WHOLE] * 14,
        out_specs=WHOLE,
        out_shape=jax.ShapeDtypeStruct((32, 128, 256), jnp.bfloat16),
        cost_estimate=pl.CostEstimate(flops=2 * 1024 * 4096 * 256, bytes_accessed=11 << 20, transcendentals=0),
        compiler_params=pltpu.CompilerParams(vmem_limit_bytes=48 << 20),
    )(*own, *other, q_own, q_other)


def lane_fold(x, op):
    acc = x[:, :LANES]
    for j in range(1, x.shape[1] // LANES):
        acc = op(acc, x[:, j * LANES : (j + 1) * LANES])
    return acc


def relation_kernel(
    block, chunk, sub, t_own, s_own, t_other, s_other, kl_ref, own_ref, other_ref, u_scr, v_scr, g_scr, kl_scr
):
    step = pl.program_id(0)
    half = t_own.shape[0]
    width = s_own.shape[1]
    student_scale = width**-0.5
    t_mul = LOG2E * t_own.shape[1] ** -0.5
    s_mul = LOG2E * student_scale

    @pl.when(step == 0)
    def _():
        own_ref[...] = jnp.zeros_like(own_ref)
        other_ref[...] = jnp.zeros_like(other_ref)

    here = lax.axis_index("zh") * 2 + lax.axis_index("yh")
    part = half // 4

    def in_order(row):
        return (row // part ^ here) * part + row % part

    mine = pl.ds(pl.multiple_of(step * block, block), block)
    first = pl.multiple_of(in_order(step * block), block)
    tr = t_own[pl.ds(first, block), :]
    sr = s_own[mine, :]
    keys = [(t, s, g, c) for t, s, g in ((t_own, s_own, own_ref), (t_other, s_other, other_ref)) for c in range(0, half, chunk)]
    mt = ms = None
    for i, (t_keys, s_keys, _, c) in enumerate(keys):
        at = slice(i * chunk, (i + 1) * chunk)
        t_at = pl.ds(pl.multiple_of(in_order(c), chunk), chunk)
        u = t_mul * lax.dot_general(tr, t_keys[t_at, :], CONTRACT_LAST, preferred_element_type=jnp.float32)
        u_scr[:, at] = u
        fold = lane_fold(u, jnp.maximum)
        mt = fold if mt is None else jnp.maximum(mt, fold)
        v = s_mul * lax.dot_general(sr, s_keys[c : c + chunk, :], CONTRACT_LAST, preferred_element_type=jnp.float32)
        v_scr[:, at] = v
        fold = lane_fold(v, jnp.maximum)
        ms = fold if ms is None else jnp.maximum(ms, fold)
    mt = jnp.max(mt, axis=1, keepdims=True)
    ms = jnp.max(ms, axis=1, keepdims=True)
    for r in range(0, block, sub):
        rows = slice(r, r + sub)
        m_t = jnp.broadcast_to(mt[rows], (sub, LANES))
        m_s = jnp.broadcast_to(ms[rows], (sub, LANES))
        zero = jnp.zeros((sub, LANES), jnp.float32)
        lt, ls, a = zero, zero, zero
        for c in range(0, 2 * half, LANES):
            x = u_scr[rows, c : c + LANES] - m_t
            y = v_scr[rows, c : c + LANES] - m_s
            et = jnp.exp2(x)
            lt = lt + et
            ls = ls + jnp.exp2(y)
            a = a + et * (x - y)
        lt = jnp.sum(lt, axis=1, keepdims=True)
        ls = jnp.sum(ls, axis=1, keepdims=True)
        a = jnp.sum(a, axis=1, keepdims=True)
        log_t = jnp.log2(lt)
        log_s = jnp.log2(ls)
        kl = (a / lt - log_t + log_s) * LN2
        kl_scr[rows, :] = jnp.broadcast_to(kl, (sub, LANES))
        z_t = jnp.broadcast_to(mt[rows] + log_t, (sub, LANES))
        z_s = jnp.broadcast_to(ms[rows] + log_s, (sub, LANES))
        for c in range(0, 2 * half, LANES):
            g = jnp.exp2(v_scr[rows, c : c + LANES] - z_s) - jnp.exp2(u_scr[rows, c : c + LANES] - z_t)
            g_scr[rows, c : c + LANES] = g.astype(jnp.bfloat16)
    kl_ref[pl.ds(first // block, 1), :] = jnp.transpose(kl_scr[...])[:1]
    acc = jnp.zeros((block, width), jnp.float32)
    for i, (_, s_keys, g_ref, c) in enumerate(keys):
        g = g_scr[:, i * chunk : (i + 1) * chunk]
        acc = acc + jnp.dot(g, s_keys[c : c + chunk, :], preferred_element_type=jnp.float32)
        g_ref[c : c + chunk, :] += lax.dot_general(g, sr, CONTRACT_FIRST, preferred_element_type=jnp.float32)
    own_ref[mine, :] += acc

    @pl.when(step == pl.num_programs(0) - 1)
    def _():
        own_ref[...] = own_ref[...] * student_scale
        other_ref[...] = other_ref[...] * student_scale


def relation(t_own, s_own, t_other, s_other, block=256, chunk=512, sub=32):
    half, t_width = t_own.shape
    s_width = s_own.shape[1]
    steps = half // block

    def whole(*shape):
        return pl.BlockSpec(shape, lambda i: (0, 0))

    return pl.pallas_call(
        functools.partial(relation_kernel, block, chunk, sub),
        grid=(steps,),
        in_specs=[whole(half, t_width), whole(half, s_width)] * 2,
        out_specs=[whole(steps, block), whole(half, s_width), whole(half, s_width)],
        out_shape=[
            jax.ShapeDtypeStruct((steps, block), jnp.float32),
            jax.ShapeDtypeStruct((half, s_width), jnp.float32),
            jax.ShapeDtypeStruct((half, s_width), jnp.float32),
        ],
        scratch_shapes=[
            pltpu.VMEM((block, 2 * half), jnp.float32),
            pltpu.VMEM((block, 2 * half), jnp.float32),
            pltpu.VMEM((block, 2 * half), jnp.bfloat16),
            pltpu.VMEM((block, LANES), jnp.float32),
        ],
        cost_estimate=pl.CostEstimate(
            flops=2 * half * 2 * half * (t_width + 3 * s_width),
            bytes_accessed=6 * half * (t_width + 3 * s_width),
            transcendentals=8 * half * half,
        ),
        compiler_params=pltpu.CompilerParams(vmem_limit_bytes=50 << 20),
    )(t_own, s_own, t_other, s_other)


def owned_rows(kl):
    kl = kl.reshape(2, 2, 2, 2, LANES).transpose(2, 0, 3, 1, 4).reshape(4, 4, LANES)
    source = lax.axis_index("xh") * 2 + lax.axis_index("core")
    got = []
    for turn in range(4):
        pairs = []
        for c in range(2):
            for dp in range(32):
                xh, xl, zh, zl, yh = ((dp >> k) & 1 for k in (4, 3, 2, 1, 0))
                quarter = turn ^ (xh * 2 + c)
                pairs.append((c * 32 + dp, zh * 32 + (xh ^ xl) * 16 + (zh ^ zl) * 8 + yh * 4 + quarter))
        sent = lax.dynamic_index_in_dim(kl, turn ^ source, 0, keepdims=False)
        got.append(lax.ppermute(sent, ("core",) + DP, pairs))
    got = jnp.stack(got)
    quarter = lax.axis_index(DP) % 4
    rows = [lax.dynamic_index_in_dim(got, f ^ quarter, 0, keepdims=False) for f in range(4)]
    rows = jnp.stack(rows).reshape(2, 2, 4, LANES)
    return rows.transpose(0, 2, 1, 3).reshape(1, 2 * 4 * 2 * LANES)


def local(teacher_query, student_hidden, query_weight):
    rows = teacher_query.shape[0]
    depth, columns = query_weight.shape
    t_width = teacher_query.shape[1] // 8
    width = columns // 4
    core = lax.axis_index("core")
    low = core == 0

    def token_halves(value):
        first, second = value[: rows // 2], value[rows // 2 :]
        return jnp.where(low, first, second), swap(jnp.where(low, second, first), "core")

    share = jnp.concatenate(token_halves(student_hidden))
    held = [share[None, first:last] for first, last, _ in RUNS]
    far = hop(held, 0)
    w_own = gather_weight(query_weight)
    w_other = [swap(piece, "core") for piece in w_own]
    held = joined(held, far)
    far = hop(held, 1)
    t_own, t_other = token_halves(teacher_query)
    heads = jnp.stack([jnp.where(low, t_own, t_other), jnp.where(low, t_other, t_own)])
    heads = heads.reshape(2, rows // 2, 2, 2, 2, t_width).transpose(0, 4, 2, 3, 1, 5)
    heads = jnp.where(lax.axis_index("xh") == 0, heads, heads[:, :, ::-1])
    heads = jnp.stack([heads[0], heads[1][:, :, ::-1]])
    heads = heads.reshape(16, rows // 2, t_width)
    held = joined(held, far)
    far = hop(held, 2)
    hidden = [piece for both in zip(held, far) for piece in both]
    teacher = exchange(after(heads, *held), SPREAD).reshape(2048, t_width)
    student = jnp.concatenate(trade(project(hidden, w_own, w_other)))
    teacher = after(teacher, student)
    hidden_other = [swap(piece, "core") for piece in hidden]
    teacher_other = swap(teacher, "core")
    student_other = swap(student, "core")

    kl, grad, grad_other = relation(after(teacher, *hidden_other), student, teacher_other, student_other)
    query_grad = (grad + swap(grad_other, "core")).astype(jnp.bfloat16)
    query_grad = trade(query_grad.reshape(4, 512, -1))
    near, away = jnp.stack(query_grad[:2]), jnp.stack(query_grad[2:])
    same = core == lax.axis_index("zh")
    mine = jnp.where(same, near, away)
    theirs = swap(jnp.where(same, away, near), "core")
    sent = exchange(weight_grad_part(hidden, hidden_other, mine, theirs), DP)
    kl_rows = owned_rows(kl)
    sent = sent.reshape(2, 2, 2, 2, 2, depth, width)
    groups = []
    for q in range(4):
        total = None
        for xh in range(2):
            for zh in range(2):
                for yh in range(2):
                    term = sent[xh, xh ^ (q >> 1), zh, zh ^ (q & 1), yh].astype(jnp.float32)
                    total = term if total is None else total + term
        groups.append(total)
    return kl_rows, jnp.concatenate(groups, axis=1)


def solution(mesh):
    bits = Mesh(mesh.devices.reshape((2,) * 7), TP + DP)
    return jax.shard_map(
        local,
        mesh=bits,
        in_specs=(P(DP, TP), P(DP, TP), P(DP, TP)),
        out_specs=(P(TP + DP, None), P(DP, TP)),
        check_vma=False,
    )
```

```python
import functools

import jax
import jax.numpy as jnp
from jax import lax
from jax.experimental import pallas as pl
from jax.experimental.pallas import tpu as pltpu
from jax.sharding import Mesh, PartitionSpec as P

LOG2E = 1.4426950408889634
LN2 = 0.6931471805599453
LANES = 128

TP = ("yl", "core")
DP = ("xh", "xl", "zh", "zl", "yh")
BLOCK = ("zh", "yh")
SPREAD = ("zh", "yh", "xl", "zl")
XZ = (("xh", "xl"), ("zh", "zl"))
SWAP = [(0, 1), (1, 0)]

CONTRACT_LAST = (((1,), (1,)), ((), ()))
CONTRACT_FIRST = (((0,), (0,)), ((), ()))
WHOLE = pl.BlockSpec(memory_space=pltpu.VMEM)


def swap(value, axis):
    return lax.ppermute(value, axis, SWAP)


def exchange(chunks, axes):
    return lax.all_to_all(chunks, axes, split_axis=0, concat_axis=0, tiled=True)


RUNS = ((0, 96, (0, 1, 2)), (96, 176, (1, 2, 0)), (176, 256, (2, 0, 1)))
CUBE = ("xl", "yl", "zl")


def hop(held, stage):
    return [swap(piece, CUBE[order[stage]]) for piece, (_, _, order) in zip(held, RUNS)]


def joined(held, far):
    return [jnp.concatenate(both) for both in zip(held, far)]


def trade(chunks):
    got = [chunks[0]]
    for r in range(1, 4):
        step = (r >> 1) * 6 + (r & 1)
        got.append(lax.ppermute(chunks[r], ("zh", "zl", "yh"), [(i, i ^ step) for i in range(8)]))
    return got


def hop_weight(held, stage):
    return [
        lax.ppermute(piece, axes, [(i, i ^ 3) for i in range(4)]) for piece, axes in zip(held, (XZ, XZ[::-1])[stage])
    ]


def weight_in_order(refs, out):
    depth = refs[0].shape[2]
    for run in range(2):
        for e in range(8):
            ex, ez = (e >> 1 & 1, e >> 2) if run == 0 else (e >> 2, e >> 1 & 1)
            for b in range(2):
                place = (
                    (lax.axis_index("xh") ^ ex) * 16
                    + (lax.axis_index("xl") ^ ex ^ run) * 8
                    + (lax.axis_index("zh") ^ ez) * 4
                    + (lax.axis_index("zl") ^ ez ^ b) * 2
                    + (lax.axis_index("yh") ^ (e & 1))
                )
                rows = pl.ds(pl.multiple_of(place * depth, depth), depth)
                out[rows, :] = refs[2 * run + e // 4][e % 4, b]


def together(first, second):
    both = lax.optimization_barrier((tuple(first), tuple(second)))
    return list(both[0]), list(both[1])


def after(value, *others):
    return lax.optimization_barrier((value, *others))[0]


def run_piece(refs, run, hops, first, last):
    order = RUNS[run][2]
    place = sum(hops[order[k]] << k for k in range(3))
    return refs[2 * run + place // 4][place % 4, first:last, :]


def hidden_tile(refs, dy, rel):
    rows = []
    for dx in range(2):
        for dz in range(2):
            hops = (dx, dy, dz)
            if rel == 0:
                rows += [run_piece(refs, 0, hops, 0, 96), run_piece(refs, 1, hops, 0, 32)]
            else:
                rows += [run_piece(refs, 1, hops, 32, 80), run_piece(refs, 2, hops, 0, 80)]
    return jnp.concatenate(rows, axis=0)


def token_place(dx, dz):
    return (lax.axis_index("xl") ^ dx) * 2 + (lax.axis_index("zl") ^ dz)


def project_kernel(*refs):
    hidden, (out, w_own, w_other) = refs[:6], refs[14:]
    weight_in_order(refs[6:10], w_own)
    weight_in_order(refs[10:14], w_other)
    core = lax.axis_index("core")
    features = w_own.shape[0] // 4
    parts = [None, None]
    for dy in range(2):
        for rel in range(2):
            tile = hidden_tile(hidden, dy, rel)
            block = (lax.axis_index("yl") ^ dy) * 2 + (core ^ rel)
            depth = pl.ds(pl.multiple_of(block * features, features), features)
            for i, weight in enumerate((w_own, w_other)):
                term = jnp.dot(tile, weight[depth, :], preferred_element_type=jnp.float32)
                parts[i] = term if parts[i] is None else parts[i] + term
    for i in range(2):
        value = parts[i].astype(jnp.bfloat16)
        for j in range(2):
            for dx in range(2):
                for dz in range(2):
                    at = (dx * 2 + dz) * 128
                    rows = pl.ds(pl.multiple_of(token_place(dx, dz) * 128, 128), 128)
                    slot = (core ^ i ^ lax.axis_index("zh")) * 2 + (lax.axis_index("yh") ^ j)
                    out[slot, rows, :] = value[at : at + 128, j * 128 : (j + 1) * 128]


def project(hidden, w_own, w_other):
    return pl.pallas_call(
        project_kernel,
        in_specs=[WHOLE] * 14,
        out_specs=WHOLE,
        out_shape=jax.ShapeDtypeStruct((4, 512, 128), jnp.bfloat16),
        scratch_shapes=[pltpu.VMEM((4096, 256), jnp.bfloat16)] * 2,
        cost_estimate=pl.CostEstimate(flops=2 * 512 * 4096 * 512, bytes_accessed=9 << 20, transcendentals=0),
        compiler_params=pltpu.CompilerParams(vmem_limit_bytes=48 << 20),
    )(*hidden, *w_own, *w_other)


def weight_grad_kernel(*refs):
    own, other, (q_own, q_other, out) = refs[:6], refs[6:12], refs[12:]
    core = lax.axis_index("core")

    def in_place(ref):
        rows = []
        for dx in range(2):
            for dz in range(2):
                at = pl.ds(pl.multiple_of(token_place(dx, dz) * 128, 128), 128)
                yh = lax.axis_index("yh")
                rows.append(jnp.concatenate([ref[yh, at, :], ref[1 - yh, at, :]], axis=1))
        return rows

    grad = jnp.concatenate(in_place(q_own) + in_place(q_other), axis=0)
    for dy in range(2):
        for rel in range(2):
            tile = jnp.concatenate([hidden_tile(own, dy, rel), hidden_tile(other, dy, 1 - rel)], axis=0)
            block = (lax.axis_index("yl") ^ dy) * 2 + (core ^ rel)
            value = lax.dot_general(tile, grad, CONTRACT_FIRST, preferred_element_type=jnp.float32)
            count = value.shape[0] // 128
            out[pl.ds(block * count, count)] = value.astype(jnp.bfloat16).reshape(count, 128, value.shape[1])


def weight_grad_part(own, other, q_own, q_other):
    return pl.pallas_call(
        weight_grad_kernel,
        in_specs=[WHOLE] * 14,
        out_specs=WHOLE,
        out_shape=jax.ShapeDtypeStruct((32, 128, 256), jnp.bfloat16),
        cost_estimate=pl.CostEstimate(flops=2 * 1024 * 4096 * 256, bytes_accessed=11 << 20, transcendentals=0),
        compiler_params=pltpu.CompilerParams(vmem_limit_bytes=48 << 20),
    )(*own, *other, q_own, q_other)


def lane_fold(x, op):
    acc = x[:, :LANES]
    for j in range(1, x.shape[1] // LANES):
        acc = op(acc, x[:, j * LANES : (j + 1) * LANES])
    return acc


def relation_kernel(
    block, chunk, sub, t_own, s_own, t_other, s_other, kl_ref, own_ref, other_ref, u_scr, v_scr, g_scr, kl_scr
):
    step = pl.program_id(0)
    half = t_own.shape[0]
    width = s_own.shape[1]
    student_scale = width**-0.5
    t_mul = LOG2E * t_own.shape[1] ** -0.5
    s_mul = LOG2E * student_scale

    @pl.when(step == 0)
    def _():
        own_ref[...] = jnp.zeros_like(own_ref)
        other_ref[...] = jnp.zeros_like(other_ref)

    here = lax.axis_index("zh") * 2 + lax.axis_index("yh")
    part = half // 4

    def in_order(row):
        return (row // part ^ here) * part + row % part

    mine = pl.ds(pl.multiple_of(step * block, block), block)
    first = pl.multiple_of(in_order(step * block), block)
    tr = t_own[pl.ds(first, block), :]
    sr = s_own[mine, :]
    keys = [(t, s, g, c) for t, s, g in ((t_own, s_own, own_ref), (t_other, s_other, other_ref)) for c in range(0, half, chunk)]
    mt = ms = None
    for i, (t_keys, s_keys, _, c) in enumerate(keys):
        at = slice(i * chunk, (i + 1) * chunk)
        t_at = pl.ds(pl.multiple_of(in_order(c), chunk), chunk)
        u = t_mul * lax.dot_general(tr, t_keys[t_at, :], CONTRACT_LAST, preferred_element_type=jnp.float32)
        u_scr[:, at] = u
        fold = lane_fold(u, jnp.maximum)
        mt = fold if mt is None else jnp.maximum(mt, fold)
        v = s_mul * lax.dot_general(sr, s_keys[c : c + chunk, :], CONTRACT_LAST, preferred_element_type=jnp.float32)
        v_scr[:, at] = v
        fold = lane_fold(v, jnp.maximum)
        ms = fold if ms is None else jnp.maximum(ms, fold)
    mt = jnp.max(mt, axis=1, keepdims=True)
    ms = jnp.max(ms, axis=1, keepdims=True)
    for r in range(0, block, sub):
        rows = slice(r, r + sub)
        m_t = jnp.broadcast_to(mt[rows], (sub, LANES))
        m_s = jnp.broadcast_to(ms[rows], (sub, LANES))
        zero = jnp.zeros((sub, LANES), jnp.float32)
        lt, ls, a = zero, zero, zero
        for c in range(0, 2 * half, LANES):
            x = u_scr[rows, c : c + LANES] - m_t
            y = v_scr[rows, c : c + LANES] - m_s
            et = jnp.exp2(x)
            lt = lt + et
            ls = ls + jnp.exp2(y)
            a = a + et * (x - y)
        lt = jnp.sum(lt, axis=1, keepdims=True)
        ls = jnp.sum(ls, axis=1, keepdims=True)
        a = jnp.sum(a, axis=1, keepdims=True)
        log_t = jnp.log2(lt)
        log_s = jnp.log2(ls)
        kl = (a / lt - log_t + log_s) * LN2
        kl_scr[rows, :] = jnp.broadcast_to(kl, (sub, LANES))
        z_t = jnp.broadcast_to(mt[rows] + log_t, (sub, LANES))
        z_s = jnp.broadcast_to(ms[rows] + log_s, (sub, LANES))
        for c in range(0, 2 * half, LANES):
            g = jnp.exp2(v_scr[rows, c : c + LANES] - z_s) - jnp.exp2(u_scr[rows, c : c + LANES] - z_t)
            g_scr[rows, c : c + LANES] = g.astype(jnp.bfloat16)
    kl_ref[pl.ds(first // block, 1), :] = jnp.transpose(kl_scr[...])[:1]
    acc = jnp.zeros((block, width), jnp.float32)
    for i, (_, s_keys, g_ref, c) in enumerate(keys):
        g = g_scr[:, i * chunk : (i + 1) * chunk]
        acc = acc + jnp.dot(g, s_keys[c : c + chunk, :], preferred_element_type=jnp.float32)
        g_ref[c : c + chunk, :] += lax.dot_general(g, sr, CONTRACT_FIRST, preferred_element_type=jnp.float32)
    own_ref[mine, :] += acc

    @pl.when(step == pl.num_programs(0) - 1)
    def _():
        own_ref[...] = own_ref[...] * student_scale
        other_ref[...] = other_ref[...] * student_scale


def relation(t_own, s_own, t_other, s_other, block=256, chunk=512, sub=32):
    half, t_width = t_own.shape
    s_width = s_own.shape[1]
    steps = half // block

    def whole(*shape):
        return pl.BlockSpec(shape, lambda i: (0, 0))

    return pl.pallas_call(
        functools.partial(relation_kernel, block, chunk, sub),
        grid=(steps,),
        in_specs=[whole(half, t_width), whole(half, s_width)] * 2,
        out_specs=[whole(steps, block), whole(half, s_width), whole(half, s_width)],
        out_shape=[
            jax.ShapeDtypeStruct((steps, block), jnp.float32),
            jax.ShapeDtypeStruct((half, s_width), jnp.float32),
            jax.ShapeDtypeStruct((half, s_width), jnp.float32),
        ],
        scratch_shapes=[
            pltpu.VMEM((block, 2 * half), jnp.float32),
            pltpu.VMEM((block, 2 * half), jnp.float32),
            pltpu.VMEM((block, 2 * half), jnp.bfloat16),
            pltpu.VMEM((block, LANES), jnp.float32),
        ],
        cost_estimate=pl.CostEstimate(
            flops=2 * half * 2 * half * (t_width + 3 * s_width),
            bytes_accessed=6 * half * (t_width + 3 * s_width),
            transcendentals=8 * half * half,
        ),
        compiler_params=pltpu.CompilerParams(vmem_limit_bytes=50 << 20),
    )(t_own, s_own, t_other, s_other)


def owned_rows(kl):
    kl = kl.reshape(2, 2, 2, 2, LANES).transpose(2, 0, 3, 1, 4).reshape(4, 4, LANES)
    source = lax.axis_index("xh") * 2 + lax.axis_index("core")
    got = []
    for turn in range(4):
        pairs = []
        for c in range(2):
            for dp in range(32):
                xh, xl, zh, zl, yh = ((dp >> k) & 1 for k in (4, 3, 2, 1, 0))
                quarter = turn ^ (xh * 2 + c)
                pairs.append((c * 32 + dp, zh * 32 + (xh ^ xl) * 16 + (zh ^ zl) * 8 + yh * 4 + quarter))
        sent = lax.dynamic_index_in_dim(kl, turn ^ source, 0, keepdims=False)
        got.append(lax.ppermute(sent, ("core",) + DP, pairs))
    got = jnp.stack(got)
    quarter = lax.axis_index(DP) % 4
    rows = [lax.dynamic_index_in_dim(got, f ^ quarter, 0, keepdims=False) for f in range(4)]
    rows = jnp.stack(rows).reshape(2, 2, 4, LANES)
    return rows.transpose(0, 2, 1, 3).reshape(1, 2 * 4 * 2 * LANES)


def local(teacher_query, student_hidden, query_weight):
    rows = teacher_query.shape[0]
    depth, columns = query_weight.shape
    t_width = teacher_query.shape[1] // 8
    width = columns // 4
    core = lax.axis_index("core")
    low = core == 0

    def token_halves(value):
        first, second = value[: rows // 2], value[rows // 2 :]
        return jnp.where(low, first, second), swap(jnp.where(low, second, first), "core")

    parts = jnp.moveaxis(query_weight.reshape(depth, 4, width), 1, 0)
    q = (lax.axis_index("xh") ^ lax.axis_index("xl")) * 2 + (lax.axis_index("zh") ^ lax.axis_index("zl"))
    near = jnp.stack([lax.dynamic_index_in_dim(parts, q ^ r, 0, keepdims=False) for r in range(4)])
    share = jnp.concatenate(token_halves(student_hidden))
    held = [share[None, first:last] for first, last, _ in RUNS]
    far, blocks = together(
        hop(held, 0),
        [near[0]] + [lax.ppermute(near[r], ("xl", "zl"), [(i, i ^ r) for i in range(4)]) for r in range(1, 4)],
    )
    held = joined(held, far)
    blocks = jnp.stack(blocks)
    far, (more,) = together(hop(held, 1), [swap(blocks, "yh")])
    held = joined(held, far)
    blocks = jnp.stack([blocks, more])
    runs = [blocks[:, :2], blocks[:, 2:]]
    t_own, t_other = token_halves(teacher_query)
    heads = jnp.stack([jnp.where(low, t_own, t_other), jnp.where(low, t_other, t_own)])
    heads = heads.reshape(2, rows // 2, 2, 2, 2, t_width).transpose(0, 4, 2, 3, 1, 5)
    heads = jnp.where(lax.axis_index("xh") == 0, heads, heads[:, :, ::-1])
    heads = jnp.stack([heads[0], heads[1][:, :, ::-1]])
    heads = heads.reshape(16, rows // 2, t_width)
    far = hop(held, 2)
    hidden = [piece for both in zip(held, far) for piece in both]
    passed = hop_weight(runs, 0)
    teacher = exchange(after(heads, *passed), SPREAD).reshape(2048, t_width)
    runs = joined(runs, passed)
    w_own = [piece for both in zip(runs, hop_weight(runs, 1)) for piece in both]
    w_other = [swap(piece, "core") for piece in w_own]
    student = jnp.concatenate(trade(project(hidden, w_own, w_other)))
    teacher = after(teacher, student)
    hidden_other = [swap(piece, "core") for piece in hidden]
    teacher_other = swap(teacher, "core")
    student_other = swap(student, "core")

    kl, grad, grad_other = relation(after(teacher, *hidden_other), student, teacher_other, student_other)
    query_grad = (grad + swap(grad_other, "core")).astype(jnp.bfloat16)
    query_grad = trade(query_grad.reshape(4, 512, -1))
    near, away = jnp.stack(query_grad[:2]), jnp.stack(query_grad[2:])
    same = core == lax.axis_index("zh")
    mine = jnp.where(same, near, away)
    theirs = swap(jnp.where(same, away, near), "core")
    sent = exchange(weight_grad_part(hidden, hidden_other, mine, theirs), DP)
    kl_rows = owned_rows(kl)
    sent = sent.reshape(2, 2, 2, 2, 2, depth, width)
    groups = []
    for q in range(4):
        total = None
        for xh in range(2):
            for zh in range(2):
                for yh in range(2):
                    term = sent[xh, xh ^ (q >> 1), zh, zh ^ (q & 1), yh].astype(jnp.float32)
                    total = term if total is None else total + term
        groups.append(total)
    return kl_rows, jnp.concatenate(groups, axis=1)


def solution(mesh):
    bits = Mesh(mesh.devices.reshape((2,) * 7), TP + DP)
    return jax.shard_map(
        local,
        mesh=bits,
        in_specs=(P(DP, TP), P(DP, TP), P(DP, TP)),
        out_specs=(P(TP + DP, None), P(DP, TP)),
        check_vma=False,
    )
```

```python
import functools

import jax
import jax.numpy as jnp
from jax import lax
from jax.experimental import pallas as pl
from jax.experimental.pallas import tpu as pltpu
from jax.sharding import Mesh, PartitionSpec as P

LOG2E = 1.4426950408889634
LN2 = 0.6931471805599453
LANES = 128

TP = ("yl", "core")
DP = ("xh", "xl", "zh", "zl", "yh")
BLOCK = ("zh", "yh")
SPREAD = ("zh", "yh", "xl", "zl")
XZ = (("xh", "xl"), ("zh", "zl"))
SWAP = [(0, 1), (1, 0)]

CONTRACT_LAST = (((1,), (1,)), ((), ()))
CONTRACT_FIRST = (((0,), (0,)), ((), ()))
WHOLE = pl.BlockSpec(memory_space=pltpu.VMEM)


def swap(value, axis):
    return lax.ppermute(value, axis, SWAP)


def exchange(chunks, axes):
    return lax.all_to_all(chunks, axes, split_axis=0, concat_axis=0, tiled=True)


RUNS = ((0, 96, (0, 1, 2)), (96, 176, (1, 2, 0)), (176, 256, (2, 0, 1)))
CUBE = ("xl", "yl", "zl")


def hop(held, stage):
    return [swap(piece, CUBE[order[stage]]) for piece, (_, _, order) in zip(held, RUNS)]


def joined(held, far):
    return [jnp.concatenate(both) for both in zip(held, far)]


def trade(chunks):
    got = [chunks[0]]
    for r in range(1, 4):
        step = (r >> 1) * 6 + (r & 1)
        got.append(lax.ppermute(chunks[r], ("zh", "zl", "yh"), [(i, i ^ step) for i in range(8)]))
    return got


def hop_weight(held, stage):
    return [
        lax.ppermute(piece, axes, [(i, i ^ 3) for i in range(4)]) for piece, axes in zip(held, (XZ, XZ[::-1])[stage])
    ]


def weight_in_order(refs, out):
    depth = refs[0].shape[2]
    for run in range(2):
        for e in range(8):
            ex, ez = (e >> 1 & 1, e >> 2) if run == 0 else (e >> 2, e >> 1 & 1)
            for b in range(2):
                place = (
                    (lax.axis_index("xh") ^ ex) * 16
                    + (lax.axis_index("xl") ^ ex ^ run) * 8
                    + (lax.axis_index("zh") ^ ez) * 4
                    + (lax.axis_index("zl") ^ ez ^ b) * 2
                    + (lax.axis_index("yh") ^ (e & 1))
                )
                rows = pl.ds(pl.multiple_of(place * depth, depth), depth)
                out[rows, :] = refs[2 * run + e // 4][e % 4, b]


def together(first, second):
    both = lax.optimization_barrier((tuple(first), tuple(second)))
    return list(both[0]), list(both[1])


def after(value, *others):
    return lax.optimization_barrier((value, *others))[0]


def run_piece(refs, run, hops, first, last):
    order = RUNS[run][2]
    place = sum(hops[order[k]] << k for k in range(3))
    return refs[2 * run + place // 4][place % 4, first:last, :]


def hidden_tile(refs, dy, rel):
    rows = []
    for dx in range(2):
        for dz in range(2):
            hops = (dx, dy, dz)
            if rel == 0:
                rows += [run_piece(refs, 0, hops, 0, 96), run_piece(refs, 1, hops, 0, 32)]
            else:
                rows += [run_piece(refs, 1, hops, 32, 80), run_piece(refs, 2, hops, 0, 80)]
    return jnp.concatenate(rows, axis=0)


def token_place(dx, dz):
    return (lax.axis_index("xl") ^ dx) * 2 + (lax.axis_index("zl") ^ dz)


def project_kernel(*refs):
    hidden, (out, w_own, w_other) = refs[:6], refs[14:]
    weight_in_order(refs[6:10], w_own)
    weight_in_order(refs[10:14], w_other)
    core = lax.axis_index("core")
    features = w_own.shape[0] // 4
    parts = [None, None]
    for dy in range(2):
        for rel in range(2):
            tile = hidden_tile(hidden, dy, rel)
            block = (lax.axis_index("yl") ^ dy) * 2 + (core ^ rel)
            depth = pl.ds(pl.multiple_of(block * features, features), features)
            for i, weight in enumerate((w_own, w_other)):
                term = jnp.dot(tile, weight[depth, :], preferred_element_type=jnp.float32)
                parts[i] = term if parts[i] is None else parts[i] + term
    for i in range(2):
        value = parts[i].astype(jnp.bfloat16)
        for j in range(2):
            for dx in range(2):
                for dz in range(2):
                    at = (dx * 2 + dz) * 128
                    rows = pl.ds(pl.multiple_of(token_place(dx, dz) * 128, 128), 128)
                    slot = (core ^ i ^ lax.axis_index("zh")) * 2 + (lax.axis_index("yh") ^ j)
                    out[slot, rows, :] = value[at : at + 128, j * 128 : (j + 1) * 128]


def project(hidden, w_own, w_other):
    return pl.pallas_call(
        project_kernel,
        in_specs=[WHOLE] * 14,
        out_specs=WHOLE,
        out_shape=jax.ShapeDtypeStruct((4, 512, 128), jnp.bfloat16),
        scratch_shapes=[pltpu.VMEM((4096, 256), jnp.bfloat16)] * 2,
        cost_estimate=pl.CostEstimate(flops=2 * 512 * 4096 * 512, bytes_accessed=9 << 20, transcendentals=0),
        compiler_params=pltpu.CompilerParams(vmem_limit_bytes=48 << 20),
    )(*hidden, *w_own, *w_other)


def weight_grad_kernel(*refs):
    own, other, (q_own, q_other, out) = refs[:6], refs[6:12], refs[12:]
    core = lax.axis_index("core")

    def in_place(ref):
        rows = []
        for dx in range(2):
            for dz in range(2):
                at = pl.ds(pl.multiple_of(token_place(dx, dz) * 128, 128), 128)
                yh = lax.axis_index("yh")
                rows.append(jnp.concatenate([ref[yh, at, :], ref[1 - yh, at, :]], axis=1))
        return rows

    grad = jnp.concatenate(in_place(q_own) + in_place(q_other), axis=0)
    for dy in range(2):
        for rel in range(2):
            tile = jnp.concatenate([hidden_tile(own, dy, rel), hidden_tile(other, dy, 1 - rel)], axis=0)
            block = (lax.axis_index("yl") ^ dy) * 2 + (core ^ rel)
            value = lax.dot_general(tile, grad, CONTRACT_FIRST, preferred_element_type=jnp.float32)
            count = value.shape[0] // 128
            out[pl.ds(block * count, count)] = value.astype(jnp.bfloat16).reshape(count, 128, value.shape[1])


def weight_grad_part(own, other, q_own, q_other):
    return pl.pallas_call(
        weight_grad_kernel,
        in_specs=[WHOLE] * 14,
        out_specs=WHOLE,
        out_shape=jax.ShapeDtypeStruct((32, 128, 256), jnp.bfloat16),
        cost_estimate=pl.CostEstimate(flops=2 * 1024 * 4096 * 256, bytes_accessed=11 << 20, transcendentals=0),
        compiler_params=pltpu.CompilerParams(vmem_limit_bytes=48 << 20),
    )(*own, *other, q_own, q_other)


def lane_fold(x, op):
    acc = x[:, :LANES]
    for j in range(1, x.shape[1] // LANES):
        acc = op(acc, x[:, j * LANES : (j + 1) * LANES])
    return acc


def relation_kernel(block, pieces, t_own, s_own, t_other, s_other, kl_ref, own_ref, other_ref, *scratch):
    u_scr, v_scr, g_scr, mt_scr, ms_scr = (scratch[2 * i : 2 * i + 2] for i in range(5))
    acc_scr, kl_scr, own_t, other_t, s_own_t, s_other_t = scratch[10:]
    half, t_width = t_own.shape
    scale = s_own.shape[1] ** -0.5
    t_mul = LOG2E * t_width**-0.5
    s_mul = LOG2E * scale
    chunk = 2 * half // pieces
    sub = block // pieces
    count = half // block
    here = lax.axis_index("zh") * 2 + lax.axis_index("yh")
    part = half // 4

    def in_order(row):
        return (row // part ^ here) * part + row % part

    def keys(k):
        at = k * chunk
        if at < half:
            return t_own, s_own, s_own_t, own_t, at
        return t_other, s_other, s_other_t, other_t, at - half

    def rows_of(b):
        return pl.ds(pl.multiple_of(b * block, block), block)

    def scores(b, slot, k):
        t_keys, s_keys, _, _, at = keys(k)
        columns = slice(k * chunk, (k + 1) * chunk)
        t_rows = t_own[pl.ds(pl.multiple_of(in_order(b * block), block), block), :]
        t_at = pl.ds(pl.multiple_of(in_order(at), chunk), chunk)
        u = t_mul * lax.dot_general(t_rows, t_keys[t_at, :], CONTRACT_LAST, preferred_element_type=jnp.float32)
        u_scr[slot][:, columns] = u
        mt_scr[slot][k] = lane_fold(u, jnp.maximum)
        s_keys = s_keys[at : at + chunk, :]
        v = s_mul * lax.dot_general(s_own[rows_of(b), :], s_keys, CONTRACT_LAST, preferred_element_type=jnp.float32)
        v_scr[slot][:, columns] = v
        ms_scr[slot][k] = lane_fold(v, jnp.maximum)

    def softmax(slot, k):
        rows = slice(k * sub, (k + 1) * sub)
        u, v = u_scr[slot], v_scr[slot]
        m_t, m_s = mt_scr[slot][0, rows], ms_scr[slot][0, rows]
        for j in range(1, pieces):
            m_t = jnp.maximum(m_t, mt_scr[slot][j, rows])
            m_s = jnp.maximum(m_s, ms_scr[slot][j, rows])
        m_t = jnp.broadcast_to(jnp.max(m_t, axis=1, keepdims=True), (sub, LANES))
        m_s = jnp.broadcast_to(jnp.max(m_s, axis=1, keepdims=True), (sub, LANES))
        zero = jnp.zeros((sub, LANES), jnp.float32)
        lt, ls, a = zero, zero, zero
        for c in range(0, 2 * half, LANES):
            x = u[rows, c : c + LANES] - m_t
            y = v[rows, c : c + LANES] - m_s
            et, es = jnp.exp2(x), jnp.exp2(y)
            u[rows, c : c + LANES] = et
            v[rows, c : c + LANES] = es
            lt = lt + et
            ls = ls + es
            a = a + et * (x - y)
        lt = jnp.sum(lt, axis=1, keepdims=True)
        ls = jnp.sum(ls, axis=1, keepdims=True)
        a = jnp.sum(a, axis=1, keepdims=True)
        kl_scr[rows, :] = jnp.broadcast_to((a / lt - jnp.log2(lt) + jnp.log2(ls)) * LN2, (sub, LANES))
        z_t = jnp.broadcast_to(1.0 / lt, (sub, LANES))
        z_s = jnp.broadcast_to(1.0 / ls, (sub, LANES))
        for c in range(0, 2 * half, LANES):
            g = v[rows, c : c + LANES] * z_s - u[rows, c : c + LANES] * z_t
            g_scr[slot][rows, c : c + LANES] = g.astype(jnp.bfloat16)

    def gradients(b, slot, k):
        _, _, s_keys_t, out_t, at = keys(k)
        g = g_scr[slot][:, k * chunk : (k + 1) * chunk]
        term = lax.dot_general(s_keys_t[:, at : at + chunk], g, CONTRACT_LAST, preferred_element_type=jnp.float32)
        acc_scr[...] = term if k == 0 else acc_scr[...] + term
        out_t[:, at : at + chunk] += jnp.dot(
            jnp.transpose(s_own[rows_of(b), :]), g, preferred_element_type=jnp.float32
        )

    def close(b):
        own_ref[rows_of(b), :] += jnp.transpose(acc_scr[...])

    own_ref[...] = jnp.zeros_like(own_ref)
    own_t[...] = jnp.zeros_like(own_t)
    other_t[...] = jnp.zeros_like(other_t)
    g_scr[1][...] = jnp.zeros_like(g_scr[1])
    s_own_t[...] = jnp.transpose(s_own[...])
    s_other_t[...] = jnp.transpose(s_other[...])
    for k in range(pieces):
        scores(0, 0, k)

    def step(b, slot):
        before = jnp.maximum(b - 1, 0)
        after = jnp.minimum(b + 1, count - 1)
        for k in range(pieces):
            scores(after, 1 - slot, k)
            gradients(before, 1 - slot, k)
            softmax(slot, k)
        close(before)
        row = in_order(b * block) // block
        kl_ref[pl.ds(row, 1), :] = jnp.transpose(kl_scr[...])[:1]

    def pair(i, _):
        step(2 * i, 0)
        step(2 * i + 1, 1)
        return 0

    lax.fori_loop(0, count // 2, pair, 0)
    for k in range(pieces):
        gradients(count - 1, 1, k)
    close(count - 1)
    own_ref[...] = (own_ref[...] + jnp.transpose(own_t[...])) * scale
    other_ref[...] = jnp.transpose(other_t[...]) * scale


def relation(t_own, s_own, t_other, s_other, block=256, pieces=8):
    half, t_width = t_own.shape
    s_width = s_own.shape[1]
    return pl.pallas_call(
        functools.partial(relation_kernel, block, pieces),
        in_specs=[WHOLE] * 4,
        out_specs=[WHOLE] * 3,
        out_shape=[
            jax.ShapeDtypeStruct((half // block, block), jnp.float32),
            jax.ShapeDtypeStruct((half, s_width), jnp.float32),
            jax.ShapeDtypeStruct((half, s_width), jnp.float32),
        ],
        scratch_shapes=[pltpu.VMEM((block, 2 * half), jnp.float32)] * 4
        + [pltpu.VMEM((block, 2 * half), jnp.bfloat16)] * 2
        + [pltpu.VMEM((pieces, block, LANES), jnp.float32)] * 4
        + [pltpu.VMEM((s_width, block), jnp.float32), pltpu.VMEM((block, LANES), jnp.float32)]
        + [pltpu.VMEM((s_width, half), jnp.float32)] * 2
        + [pltpu.VMEM((s_width, half), jnp.bfloat16)] * 2,
        cost_estimate=pl.CostEstimate(
            flops=2 * half * 2 * half * (t_width + 3 * s_width),
            bytes_accessed=6 * half * (t_width + 3 * s_width),
            transcendentals=4 * half * half,
        ),
        compiler_params=pltpu.CompilerParams(vmem_limit_bytes=56 << 20),
    )(t_own, s_own, t_other, s_other)


def owned_rows(kl):
    kl = kl.reshape(2, 2, 2, 2, LANES).transpose(2, 0, 3, 1, 4).reshape(4, 4, LANES)
    source = lax.axis_index("xh") * 2 + lax.axis_index("core")
    got = []
    for turn in range(4):
        pairs = []
        for c in range(2):
            for dp in range(32):
                xh, xl, zh, zl, yh = ((dp >> k) & 1 for k in (4, 3, 2, 1, 0))
                quarter = turn ^ (xh * 2 + c)
                pairs.append((c * 32 + dp, zh * 32 + (xh ^ xl) * 16 + (zh ^ zl) * 8 + yh * 4 + quarter))
        sent = lax.dynamic_index_in_dim(kl, turn ^ source, 0, keepdims=False)
        got.append(lax.ppermute(sent, ("core",) + DP, pairs))
    got = jnp.stack(got)
    quarter = lax.axis_index(DP) % 4
    rows = [lax.dynamic_index_in_dim(got, f ^ quarter, 0, keepdims=False) for f in range(4)]
    rows = jnp.stack(rows).reshape(2, 2, 4, LANES)
    return rows.transpose(0, 2, 1, 3).reshape(1, 2 * 4 * 2 * LANES)


def local(teacher_query, student_hidden, query_weight):
    rows = teacher_query.shape[0]
    depth, columns = query_weight.shape
    t_width = teacher_query.shape[1] // 8
    width = columns // 4
    core = lax.axis_index("core")
    low = core == 0

    def token_halves(value):
        first, second = value[: rows // 2], value[rows // 2 :]
        return jnp.where(low, first, second), swap(jnp.where(low, second, first), "core")

    parts = jnp.moveaxis(query_weight.reshape(depth, 4, width), 1, 0)
    q = (lax.axis_index("xh") ^ lax.axis_index("xl")) * 2 + (lax.axis_index("zh") ^ lax.axis_index("zl"))
    near = jnp.stack([lax.dynamic_index_in_dim(parts, q ^ r, 0, keepdims=False) for r in range(4)])
    share = jnp.concatenate(token_halves(student_hidden))
    held = [share[None, first:last] for first, last, _ in RUNS]
    far, blocks = together(
        hop(held, 0),
        [near[0]] + [lax.ppermute(near[r], ("xl", "zl"), [(i, i ^ r) for i in range(4)]) for r in range(1, 4)],
    )
    held = joined(held, far)
    blocks = jnp.stack(blocks)
    t_own, t_other = token_halves(teacher_query)
    heads = jnp.stack([jnp.where(low, t_own, t_other), jnp.where(low, t_other, t_own)])
    heads = heads.reshape(2, rows // 2, 2, 2, 2, t_width).transpose(0, 4, 2, 3, 1, 5)
    heads = jnp.where(lax.axis_index("xh") == 0, heads, heads[:, :, ::-1])
    heads = jnp.stack([heads[0], heads[1][:, :, ::-1]])
    heads = heads.reshape(16, rows // 2, t_width)
    far, (more, heads) = together(hop(held, 1), [swap(blocks, "yh"), heads])
    held = joined(held, far)
    blocks = jnp.stack([blocks, more])
    runs = [blocks[:, :2], blocks[:, 2:]]
    far = hop(held, 2)
    hidden = [piece for both in zip(held, far) for piece in both]
    passed = hop_weight(runs, 0)
    teacher = exchange(heads, SPREAD).reshape(2048, t_width)
    runs = joined(runs, passed)
    w_own = [piece for both in zip(runs, hop_weight(runs, 1)) for piece in both]
    w_other = [swap(piece, "core") for piece in w_own]
    student = jnp.concatenate(trade(project(hidden, w_own, w_other)))
    hidden_other = [swap(piece, "core") for piece in hidden]
    teacher = after(teacher, student, *hidden_other)
    teacher_other = swap(teacher, "core")
    student_other = swap(student, "core")

    kl, grad, grad_other = relation(teacher, student, teacher_other, student_other)
    query_grad = (grad + swap(grad_other, "core")).astype(jnp.bfloat16)
    query_grad = trade(query_grad.reshape(4, 512, -1))
    near, away = jnp.stack(query_grad[:2]), jnp.stack(query_grad[2:])
    same = core == lax.axis_index("zh")
    mine = jnp.where(same, near, away)
    theirs = swap(jnp.where(same, away, near), "core")
    sent = exchange(weight_grad_part(hidden, hidden_other, mine, theirs), DP)
    kl_rows = owned_rows(kl)
    sent = sent.reshape(2, 2, 2, 2, 2, depth, width)
    groups = []
    for q in range(4):
        total = None
        for xh in range(2):
            for zh in range(2):
                for yh in range(2):
                    term = sent[xh, xh ^ (q >> 1), zh, zh ^ (q & 1), yh].astype(jnp.float32)
                    total = term if total is None else total + term
        groups.append(total)
    return kl_rows, jnp.concatenate(groups, axis=1)


def solution(mesh):
    bits = Mesh(mesh.devices.reshape((2,) * 7), TP + DP)
    return jax.shard_map(
        local,
        mesh=bits,
        in_specs=(P(DP, TP), P(DP, TP), P(DP, TP)),
        out_specs=(P(TP + DP, None), P(DP, TP)),
        check_vma=False,
    )
```

```python
import functools

import jax
import jax.numpy as jnp
from jax import lax
from jax.experimental import pallas as pl
from jax.experimental.pallas import tpu as pltpu
from jax.sharding import Mesh, PartitionSpec as P

LOG2E = 1.4426950408889634
LN2 = 0.6931471805599453
LANES = 128

TP = ("yl", "core")
DP = ("xh", "xl", "zh", "zl", "yh")
BLOCK = ("zh", "yh")
SPREAD = ("zh", "yh", "xl", "zl")
SWAP = [(0, 1), (1, 0)]

CONTRACT_LAST = (((1,), (1,)), ((), ()))
CONTRACT_FIRST = (((0,), (0,)), ((), ()))
WHOLE = pl.BlockSpec(memory_space=pltpu.VMEM)


def swap(value, axis):
    return lax.ppermute(value, axis, SWAP)


def exchange(chunks, axes):
    return lax.all_to_all(chunks, axes, split_axis=0, concat_axis=0, tiled=True)


RUNS = ((0, 96, (0, 1, 2)), (96, 176, (1, 2, 0)), (176, 256, (2, 0, 1)))
CUBE = ("xl", "yl", "zl")


def hop(held, stage):
    return [swap(piece, CUBE[order[stage]]) for piece, (_, _, order) in zip(held, RUNS)]


def joined(held, far):
    return [jnp.concatenate(both) for both in zip(held, far)]


def trade(chunks):
    got = [chunks[0]]
    for r in range(1, 4):
        step = (r >> 1) * 6 + (r & 1)
        got.append(lax.ppermute(chunks[r], ("zh", "zl", "yh"), [(i, i ^ step) for i in range(8)]))
    return got


def weight_in_order(refs, out):
    depth = refs[0].shape[2]
    for e, ref in enumerate(refs):
        for y in range(2):
            for r in range(4):
                place = (
                    (lax.axis_index("xh") ^ (e >> 1)) * 16
                    + (lax.axis_index("xl") ^ (e >> 1) ^ (r >> 1)) * 8
                    + (lax.axis_index("zh") ^ (e & 1)) * 4
                    + (lax.axis_index("zl") ^ (e & 1) ^ (r & 1)) * 2
                    + (lax.axis_index("yh") ^ y)
                )
                out[pl.ds(pl.multiple_of(place * depth, depth), depth), :] = ref[y, r]


def together(first, second):
    both = lax.optimization_barrier((tuple(first), tuple(second)))
    return list(both[0]), list(both[1])


def after(value, *others):
    return lax.optimization_barrier((value, *others))[0]


def run_piece(refs, run, hops, first, last):
    order = RUNS[run][2]
    near, middle, far = (hops[axis] for axis in order)
    return refs[4 * run + 2 * far + middle][near, first:last, :]


def hidden_tile(refs, dy, rel):
    rows = []
    for dx in range(2):
        for dz in range(2):
            hops = (dx, dy, dz)
            if rel == 0:
                rows += [run_piece(refs, 0, hops, 0, 96), run_piece(refs, 1, hops, 0, 32)]
            else:
                rows += [run_piece(refs, 1, hops, 32, 80), run_piece(refs, 2, hops, 0, 80)]
    return jnp.concatenate(rows, axis=0)


def token_place(dx, dz):
    return (lax.axis_index("xl") ^ dx) * 2 + (lax.axis_index("zl") ^ dz)


def project_kernel(*refs):
    hidden, (out, w_own, w_other) = refs[:12], refs[20:]
    weight_in_order(refs[12:16], w_own)
    weight_in_order(refs[16:20], w_other)
    core = lax.axis_index("core")
    features = w_own.shape[0] // 4
    parts = [None, None]
    for dy in range(2):
        for rel in range(2):
            tile = hidden_tile(hidden, dy, rel)
            block = (lax.axis_index("yl") ^ dy) * 2 + (core ^ rel)
            depth = pl.ds(pl.multiple_of(block * features, features), features)
            for i, weight in enumerate((w_own, w_other)):
                term = jnp.dot(tile, weight[depth, :], preferred_element_type=jnp.float32)
                parts[i] = term if parts[i] is None else parts[i] + term
    for i in range(2):
        value = parts[i].astype(jnp.bfloat16)
        for j in range(2):
            for dx in range(2):
                for dz in range(2):
                    at = (dx * 2 + dz) * 128
                    rows = pl.ds(pl.multiple_of(token_place(dx, dz) * 128, 128), 128)
                    slot = (core ^ i ^ lax.axis_index("zh")) * 2 + (lax.axis_index("yh") ^ j)
                    out[slot, rows, :] = value[at : at + 128, j * 128 : (j + 1) * 128]


def project(hidden, w_own, w_other):
    return pl.pallas_call(
        project_kernel,
        in_specs=[WHOLE] * 20,
        out_specs=WHOLE,
        out_shape=jax.ShapeDtypeStruct((4, 512, 128), jnp.bfloat16),
        scratch_shapes=[pltpu.VMEM((4096, 256), jnp.bfloat16)] * 2,
        cost_estimate=pl.CostEstimate(flops=2 * 512 * 4096 * 512, bytes_accessed=9 << 20, transcendentals=0),
        compiler_params=pltpu.CompilerParams(vmem_limit_bytes=48 << 20),
    )(*hidden, *w_own, *w_other)


def weight_grad_kernel(*refs):
    own, other, (q_own, q_other, out) = refs[:12], refs[12:24], refs[24:]
    core = lax.axis_index("core")

    def in_place(ref):
        rows = []
        for dx in range(2):
            for dz in range(2):
                at = pl.ds(pl.multiple_of(token_place(dx, dz) * 128, 128), 128)
                yh = lax.axis_index("yh")
                rows.append(jnp.concatenate([ref[yh, at, :], ref[1 - yh, at, :]], axis=1))
        return rows

    grad = jnp.concatenate(in_place(q_own) + in_place(q_other), axis=0)
    for dy in range(2):
        for rel in range(2):
            tile = jnp.concatenate([hidden_tile(own, dy, rel), hidden_tile(other, dy, 1 - rel)], axis=0)
            block = (lax.axis_index("yl") ^ dy) * 2 + (core ^ rel)
            value = lax.dot_general(tile, grad, CONTRACT_FIRST, preferred_element_type=jnp.float32)
            count = value.shape[0] // 128
            out[pl.ds(block * count, count)] = value.astype(jnp.bfloat16).reshape(count, 128, value.shape[1])


def weight_grad_part(own, other, q_own, q_other):
    return pl.pallas_call(
        weight_grad_kernel,
        in_specs=[WHOLE] * 26,
        out_specs=WHOLE,
        out_shape=jax.ShapeDtypeStruct((32, 128, 256), jnp.bfloat16),
        cost_estimate=pl.CostEstimate(flops=2 * 1024 * 4096 * 256, bytes_accessed=11 << 20, transcendentals=0),
        compiler_params=pltpu.CompilerParams(vmem_limit_bytes=48 << 20),
    )(*own, *other, q_own, q_other)


def lane_fold(x, op):
    acc = x[:, :LANES]
    for j in range(1, x.shape[1] // LANES):
        acc = op(acc, x[:, j * LANES : (j + 1) * LANES])
    return acc


def relation_kernel(block, pieces, t_own, s_own, t_other, s_other, kl_ref, own_ref, other_ref, *scratch):
    u_scr, v_scr, g_scr, mt_scr, ms_scr = (scratch[2 * i : 2 * i + 2] for i in range(5))
    acc_scr, kl_scr, own_t, other_t, s_own_t, s_other_t = scratch[10:]
    half, t_width = t_own.shape
    scale = s_own.shape[1] ** -0.5
    t_mul = LOG2E * t_width**-0.5
    s_mul = LOG2E * scale
    chunk = 2 * half // pieces
    sub = block // pieces
    count = half // block
    here = lax.axis_index("zh") * 2 + lax.axis_index("yh")
    part = half // 4

    def in_order(row):
        return (row // part ^ here) * part + row % part

    def keys(k):
        at = k * chunk
        if at < half:
            return t_own, s_own, s_own_t, own_t, at
        return t_other, s_other, s_other_t, other_t, at - half

    def rows_of(b):
        return pl.ds(pl.multiple_of(b * block, block), block)

    def scores(b, slot, k):
        t_keys, s_keys, _, _, at = keys(k)
        columns = slice(k * chunk, (k + 1) * chunk)
        t_rows = t_own[pl.ds(pl.multiple_of(in_order(b * block), block), block), :]
        t_at = pl.ds(pl.multiple_of(in_order(at), chunk), chunk)
        u = t_mul * lax.dot_general(t_rows, t_keys[t_at, :], CONTRACT_LAST, preferred_element_type=jnp.float32)
        u_scr[slot][:, columns] = u
        mt_scr[slot][k] = lane_fold(u, jnp.maximum)
        s_keys = s_keys[at : at + chunk, :]
        v = s_mul * lax.dot_general(s_own[rows_of(b), :], s_keys, CONTRACT_LAST, preferred_element_type=jnp.float32)
        v_scr[slot][:, columns] = v
        ms_scr[slot][k] = lane_fold(v, jnp.maximum)

    def softmax(slot, k):
        rows = slice(k * sub, (k + 1) * sub)
        u, v = u_scr[slot], v_scr[slot]
        m_t, m_s = mt_scr[slot][0, rows], ms_scr[slot][0, rows]
        for j in range(1, pieces):
            m_t = jnp.maximum(m_t, mt_scr[slot][j, rows])
            m_s = jnp.maximum(m_s, ms_scr[slot][j, rows])
        m_t = jnp.broadcast_to(jnp.max(m_t, axis=1, keepdims=True), (sub, LANES))
        m_s = jnp.broadcast_to(jnp.max(m_s, axis=1, keepdims=True), (sub, LANES))
        zero = jnp.zeros((sub, LANES), jnp.float32)
        lt, ls, a = zero, zero, zero
        for c in range(0, 2 * half, LANES):
            x = u[rows, c : c + LANES] - m_t
            y = v[rows, c : c + LANES] - m_s
            et, es = jnp.exp2(x), jnp.exp2(y)
            u[rows, c : c + LANES] = et
            v[rows, c : c + LANES] = es
            lt = lt + et
            ls = ls + es
            a = a + et * (x - y)
        lt = jnp.sum(lt, axis=1, keepdims=True)
        ls = jnp.sum(ls, axis=1, keepdims=True)
        a = jnp.sum(a, axis=1, keepdims=True)
        kl_scr[rows, :] = jnp.broadcast_to((a / lt - jnp.log2(lt) + jnp.log2(ls)) * LN2, (sub, LANES))
        z_t = jnp.broadcast_to(1.0 / lt, (sub, LANES))
        z_s = jnp.broadcast_to(1.0 / ls, (sub, LANES))
        for c in range(0, 2 * half, LANES):
            g = v[rows, c : c + LANES] * z_s - u[rows, c : c + LANES] * z_t
            g_scr[slot][rows, c : c + LANES] = g.astype(jnp.bfloat16)

    def gradients(b, slot, k):
        _, _, s_keys_t, out_t, at = keys(k)
        g = g_scr[slot][:, k * chunk : (k + 1) * chunk]
        term = lax.dot_general(s_keys_t[:, at : at + chunk], g, CONTRACT_LAST, preferred_element_type=jnp.float32)
        acc_scr[...] = term if k == 0 else acc_scr[...] + term
        out_t[:, at : at + chunk] += jnp.dot(
            jnp.transpose(s_own[rows_of(b), :]), g, preferred_element_type=jnp.float32
        )

    def close(b):
        own_ref[rows_of(b), :] += jnp.transpose(acc_scr[...])

    own_ref[...] = jnp.zeros_like(own_ref)
    own_t[...] = jnp.zeros_like(own_t)
    other_t[...] = jnp.zeros_like(other_t)
    g_scr[1][...] = jnp.zeros_like(g_scr[1])
    s_own_t[...] = jnp.transpose(s_own[...])
    s_other_t[...] = jnp.transpose(s_other[...])
    for k in range(pieces):
        scores(0, 0, k)

    def step(b, slot):
        before = jnp.maximum(b - 1, 0)
        after = jnp.minimum(b + 1, count - 1)
        for k in range(pieces):
            scores(after, 1 - slot, k)
            gradients(before, 1 - slot, k)
            softmax(slot, k)
        close(before)
        row = in_order(b * block) // block
        kl_ref[pl.ds(row, 1), :] = jnp.transpose(kl_scr[...])[:1]

    def pair(i, _):
        step(2 * i, 0)
        step(2 * i + 1, 1)
        return 0

    lax.fori_loop(0, count // 2, pair, 0)
    for k in range(pieces):
        gradients(count - 1, 1, k)
    close(count - 1)
    own_ref[...] = (own_ref[...] + jnp.transpose(own_t[...])) * scale
    other_ref[...] = jnp.transpose(other_t[...]) * scale


def relation(t_own, s_own, t_other, s_other, block=256, pieces=8):
    half, t_width = t_own.shape
    s_width = s_own.shape[1]
    return pl.pallas_call(
        functools.partial(relation_kernel, block, pieces),
        in_specs=[WHOLE] * 4,
        out_specs=[WHOLE] * 3,
        out_shape=[
            jax.ShapeDtypeStruct((half // block, block), jnp.float32),
            jax.ShapeDtypeStruct((half, s_width), jnp.float32),
            jax.ShapeDtypeStruct((half, s_width), jnp.float32),
        ],
        scratch_shapes=[pltpu.VMEM((block, 2 * half), jnp.float32)] * 4
        + [pltpu.VMEM((block, 2 * half), jnp.bfloat16)] * 2
        + [pltpu.VMEM((pieces, block, LANES), jnp.float32)] * 4
        + [pltpu.VMEM((s_width, block), jnp.float32), pltpu.VMEM((block, LANES), jnp.float32)]
        + [pltpu.VMEM((s_width, half), jnp.float32)] * 2
        + [pltpu.VMEM((s_width, half), jnp.bfloat16)] * 2,
        cost_estimate=pl.CostEstimate(
            flops=2 * half * 2 * half * (t_width + 3 * s_width),
            bytes_accessed=6 * half * (t_width + 3 * s_width),
            transcendentals=4 * half * half,
        ),
        compiler_params=pltpu.CompilerParams(vmem_limit_bytes=56 << 20),
    )(t_own, s_own, t_other, s_other)


def owned_rows(kl):
    kl = kl.reshape(2, 2, 2, 2, LANES).transpose(2, 0, 3, 1, 4).reshape(4, 4, LANES)
    source = lax.axis_index("xh") * 2 + lax.axis_index("core")
    got = []
    for turn in range(4):
        pairs = []
        for c in range(2):
            for dp in range(32):
                xh, xl, zh, zl, yh = ((dp >> k) & 1 for k in (4, 3, 2, 1, 0))
                quarter = turn ^ (xh * 2 + c)
                pairs.append((c * 32 + dp, zh * 32 + (xh ^ xl) * 16 + (zh ^ zl) * 8 + yh * 4 + quarter))
        sent = lax.dynamic_index_in_dim(kl, turn ^ source, 0, keepdims=False)
        got.append(lax.ppermute(sent, ("core",) + DP, pairs))
    got = jnp.stack(got)
    quarter = lax.axis_index(DP) % 4
    rows = [lax.dynamic_index_in_dim(got, f ^ quarter, 0, keepdims=False) for f in range(4)]
    rows = jnp.stack(rows).reshape(2, 2, 4, LANES)
    return rows.transpose(0, 2, 1, 3).reshape(1, 2 * 4 * 2 * LANES)


def local(teacher_query, student_hidden, query_weight):
    rows = teacher_query.shape[0]
    depth, columns = query_weight.shape
    t_width = teacher_query.shape[1] // 8
    width = columns // 4
    core = lax.axis_index("core")
    low = core == 0

    def token_halves(value):
        first, second = value[: rows // 2], value[rows // 2 :]
        return jnp.where(low, first, second), swap(jnp.where(low, second, first), "core")

    parts = jnp.moveaxis(query_weight.reshape(depth, 4, width), 1, 0)
    q = (lax.axis_index("xh") ^ lax.axis_index("xl")) * 2 + (lax.axis_index("zh") ^ lax.axis_index("zl"))
    near = jnp.stack([lax.dynamic_index_in_dim(parts, q ^ r, 0, keepdims=False) for r in range(4)])
    share = jnp.concatenate(token_halves(student_hidden))
    held = [share[None, first:last] for first, last, _ in RUNS]
    far, blocks = together(
        hop(held, 0),
        [near[0]] + [lax.ppermute(near[r], ("xl", "zl"), [(i, i ^ r) for i in range(4)]) for r in range(1, 4)],
    )
    blocks = jnp.stack(blocks)
    t_own, t_other = token_halves(teacher_query)
    heads = jnp.stack([jnp.where(low, t_own, t_other), jnp.where(low, t_other, t_own)])
    heads = heads.reshape(2, rows // 2, 2, 2, 2, t_width).transpose(0, 4, 2, 3, 1, 5)
    heads = jnp.where(lax.axis_index("xh") == 0, heads, heads[:, :, ::-1])
    heads = jnp.stack([heads[0], heads[1][:, :, ::-1]])
    heads = heads.reshape(16, rows // 2, t_width)
    held = joined(held, far)
    across = hop(held, 2)
    far, (more, heads) = together(hop(held, 1), [swap(blocks, "yh"), heads])
    hidden = [piece for run in zip(held, far, across, hop(far, 2)) for piece in run]
    blocks = jnp.stack([blocks, more])
    w_own = [blocks]
    for e in range(1, 4):
        step = (e >> 1) * 12 + (e & 1) * 3
        w_own.append(lax.ppermute(blocks, ("xh", "xl", "zh", "zl"), [(i, i ^ step) for i in range(16)]))
    teacher = exchange(heads, SPREAD).reshape(2048, t_width)
    w_other = [swap(piece, "core") for piece in w_own]
    student = jnp.concatenate(trade(project(hidden, w_own, w_other)))
    hidden_other = [swap(piece, "core") for piece in hidden]
    teacher = after(teacher, student, *hidden_other)
    teacher_other = swap(teacher, "core")
    student_other = swap(student, "core")

    kl, grad, grad_other = relation(teacher, student, teacher_other, student_other)
    grad_other = swap(grad_other, "core").reshape(4, 512, -1)
    query_grad = [(mine + theirs).astype(jnp.bfloat16) for mine, theirs in zip(grad.reshape(4, 512, -1), grad_other)]
    query_grad = trade(query_grad)
    near, away = jnp.stack(query_grad[:2]), jnp.stack(query_grad[2:])
    same = core == lax.axis_index("zh")
    mine = jnp.where(same, near, away)
    theirs = swap(jnp.where(same, away, near), "core")
    sent = exchange(weight_grad_part(hidden, hidden_other, mine, theirs), DP)
    kl_rows = owned_rows(kl)
    sent = sent.reshape(2, 2, 2, 2, 2, depth, width)
    groups = []
    for q in range(4):
        total = None
        for xh in range(2):
            for zh in range(2):
                for yh in range(2):
                    term = sent[xh, xh ^ (q >> 1), zh, zh ^ (q & 1), yh].astype(jnp.float32)
                    total = term if total is None else total + term
        groups.append(total)
    return kl_rows, jnp.concatenate(groups, axis=1)


def solution(mesh):
    bits = Mesh(mesh.devices.reshape((2,) * 7), TP + DP)
    return jax.shard_map(
        local,
        mesh=bits,
        in_specs=(P(DP, TP), P(DP, TP), P(DP, TP)),
        out_specs=(P(TP + DP, None), P(DP, TP)),
        check_vma=False,
    )
```

```python
import functools

import jax
import jax.numpy as jnp
from jax import lax
from jax.experimental import pallas as pl
from jax.experimental.pallas import tpu as pltpu
from jax.sharding import Mesh, PartitionSpec as P

LOG2E = 1.4426950408889634
LN2 = 0.6931471805599453
LANES = 128

TP = ("yl", "core")
DP = ("xh", "xl", "zh", "zl", "yh")
BLOCK = ("zh", "yh")
SPREAD = ("zh", "yh", "xl", "zl")
XZ = (("xh", "xl"), ("zh", "zl"))
SWAP = [(0, 1), (1, 0)]

CONTRACT_LAST = (((1,), (1,)), ((), ()))
CONTRACT_FIRST = (((0,), (0,)), ((), ()))
WHOLE = pl.BlockSpec(memory_space=pltpu.VMEM)


def swap(value, axis):
    return lax.ppermute(value, axis, SWAP)


def exchange(chunks, axes):
    return lax.all_to_all(chunks, axes, split_axis=0, concat_axis=0, tiled=True)


def trade(chunks):
    got = [chunks[0]]
    for r in range(1, 4):
        step = (r >> 1) * 6 + (r & 1)
        got.append(lax.ppermute(chunks[r], ("zh", "zl", "yh"), [(i, i ^ step) for i in range(8)]))
    return got


def hop_weight(held, stage):
    return [
        lax.ppermute(piece, axes, [(i, i ^ 3) for i in range(4)]) for piece, axes in zip(held, (XZ, XZ[::-1])[stage])
    ]


def weight_in_order(refs, out):
    depth = refs[0].shape[2]
    for run in range(2):
        for e in range(8):
            ex, ez = (e >> 1 & 1, e >> 2) if run == 0 else (e >> 2, e >> 1 & 1)
            for b in range(2):
                place = (
                    (lax.axis_index("xh") ^ ex) * 16
                    + (lax.axis_index("xl") ^ ex ^ run) * 8
                    + (lax.axis_index("zh") ^ ez) * 4
                    + (lax.axis_index("zl") ^ ez ^ b) * 2
                    + (lax.axis_index("yh") ^ (e & 1))
                )
                rows = pl.ds(pl.multiple_of(place * depth, depth), depth)
                out[rows, :] = refs[2 * run + e // 4][e % 4, b]


def project_kernel(*refs):
    hidden, (out, w_own, w_other) = refs[0], refs[9:]
    weight_in_order(refs[1:5], w_own)
    weight_in_order(refs[5:9], w_other)
    core = lax.axis_index("core")
    features = w_own.shape[0] // 4
    parts = [None, None]
    mine = pl.ds(pl.multiple_of(core * 128, 128), 128)
    for block in range(4):
        tile = hidden[block, :, mine, :].reshape(512, features)
        for i, weight in enumerate((w_own, w_other)):
            rows = slice(block * features, (block + 1) * features)
            term = jnp.dot(tile, weight[rows, :], preferred_element_type=jnp.float32)
            parts[i] = term if parts[i] is None else parts[i] + term
    for i in range(2):
        value = parts[i].astype(jnp.bfloat16)
        for j in range(2):
            slot = (core ^ i ^ lax.axis_index("zh")) * 2 + (lax.axis_index("yh") ^ j)
            out[slot] = value[:, j * 128 : (j + 1) * 128]


def project(hidden, w_own, w_other):
    return pl.pallas_call(
        project_kernel,
        in_specs=[WHOLE] * 9,
        out_specs=WHOLE,
        out_shape=jax.ShapeDtypeStruct((4, 512, 128), jnp.bfloat16),
        scratch_shapes=[pltpu.VMEM((4096, 256), jnp.bfloat16)] * 2,
        cost_estimate=pl.CostEstimate(flops=2 * 512 * 4096 * 512, bytes_accessed=9 << 20, transcendentals=0),
        compiler_params=pltpu.CompilerParams(vmem_limit_bytes=48 << 20),
    )(hidden, *w_own, *w_other)


def weight_grad_kernel(hidden, q_own, q_other, out, grad):
    core, yh = lax.axis_index("core"), lax.axis_index("yh")
    for ref, half in ((q_own, core), (q_other, 1 - core)):
        for chip in range(4):
            rows = pl.ds(pl.multiple_of(chip * 256 + half * 128, 128), 128)
            at = slice(chip * 128, (chip + 1) * 128)
            grad[rows, :] = jnp.concatenate([ref[yh, at, :], ref[1 - yh, at, :]], axis=1)
    features = hidden.shape[-1]
    count = features // 128
    for block in range(4):
        tile = hidden[block].reshape(1024, features)
        value = lax.dot_general(tile, grad[...], CONTRACT_FIRST, preferred_element_type=jnp.float32)
        out[block * count : (block + 1) * count] = value.astype(jnp.bfloat16).reshape(count, 128, value.shape[1])


def weight_grad_part(hidden, q_own, q_other):
    return pl.pallas_call(
        weight_grad_kernel,
        in_specs=[WHOLE] * 3,
        out_specs=WHOLE,
        out_shape=jax.ShapeDtypeStruct((32, 128, 256), jnp.bfloat16),
        scratch_shapes=[pltpu.VMEM((1024, 256), jnp.bfloat16)],
        cost_estimate=pl.CostEstimate(flops=2 * 1024 * 4096 * 256, bytes_accessed=11 << 20, transcendentals=0),
        compiler_params=pltpu.CompilerParams(vmem_limit_bytes=48 << 20),
    )(hidden, q_own, q_other)


def lane_fold(x, op):
    acc = x[:, :LANES]
    for j in range(1, x.shape[1] // LANES):
        acc = op(acc, x[:, j * LANES : (j + 1) * LANES])
    return acc


def relation_kernel(block, pieces, t_own, s_own, t_other, s_other, kl_ref, own_ref, other_ref, *scratch):
    u_scr, v_scr, g_scr, mt_scr, ms_scr = (scratch[2 * i : 2 * i + 2] for i in range(5))
    acc_scr, kl_scr, own_t, other_t, s_own_t, s_other_t = scratch[10:]
    half, t_width = t_own.shape
    scale = s_own.shape[1] ** -0.5
    t_mul = LOG2E * t_width**-0.5
    s_mul = LOG2E * scale
    chunk = 2 * half // pieces
    sub = block // pieces
    count = half // block
    here = lax.axis_index("zh") * 2 + lax.axis_index("yh")
    part = half // 4

    def in_order(row):
        return (row // part ^ here) * part + row % part

    def keys(k):
        at = k * chunk
        if at < half:
            return t_own, s_own, s_own_t, own_t, at
        return t_other, s_other, s_other_t, other_t, at - half

    def rows_of(b):
        return pl.ds(pl.multiple_of(b * block, block), block)

    def scores(b, slot, k):
        t_keys, s_keys, _, _, at = keys(k)
        columns = slice(k * chunk, (k + 1) * chunk)
        t_rows = t_own[pl.ds(pl.multiple_of(in_order(b * block), block), block), :]
        t_at = pl.ds(pl.multiple_of(in_order(at), chunk), chunk)
        u = t_mul * lax.dot_general(t_rows, t_keys[t_at, :], CONTRACT_LAST, preferred_element_type=jnp.float32)
        u_scr[slot][:, columns] = u
        mt_scr[slot][k] = lane_fold(u, jnp.maximum)
        s_keys = s_keys[at : at + chunk, :]
        v = s_mul * lax.dot_general(s_own[rows_of(b), :], s_keys, CONTRACT_LAST, preferred_element_type=jnp.float32)
        v_scr[slot][:, columns] = v
        ms_scr[slot][k] = lane_fold(v, jnp.maximum)

    def softmax(slot, k):
        rows = slice(k * sub, (k + 1) * sub)
        u, v = u_scr[slot], v_scr[slot]
        m_t, m_s = mt_scr[slot][0, rows], ms_scr[slot][0, rows]
        for j in range(1, pieces):
            m_t = jnp.maximum(m_t, mt_scr[slot][j, rows])
            m_s = jnp.maximum(m_s, ms_scr[slot][j, rows])
        m_t = jnp.broadcast_to(jnp.max(m_t, axis=1, keepdims=True), (sub, LANES))
        m_s = jnp.broadcast_to(jnp.max(m_s, axis=1, keepdims=True), (sub, LANES))
        zero = jnp.zeros((sub, LANES), jnp.float32)
        lt, ls, a = zero, zero, zero
        for c in range(0, 2 * half, LANES):
            x = u[rows, c : c + LANES] - m_t
            y = v[rows, c : c + LANES] - m_s
            et, es = jnp.exp2(x), jnp.exp2(y)
            u[rows, c : c + LANES] = et
            v[rows, c : c + LANES] = es
            lt = lt + et
            ls = ls + es
            a = a + et * (x - y)
        lt = jnp.sum(lt, axis=1, keepdims=True)
        ls = jnp.sum(ls, axis=1, keepdims=True)
        a = jnp.sum(a, axis=1, keepdims=True)
        kl_scr[rows, :] = jnp.broadcast_to((a / lt - jnp.log2(lt) + jnp.log2(ls)) * LN2, (sub, LANES))
        z_t = jnp.broadcast_to(1.0 / lt, (sub, LANES))
        z_s = jnp.broadcast_to(1.0 / ls, (sub, LANES))
        for c in range(0, 2 * half, LANES):
            g = v[rows, c : c + LANES] * z_s - u[rows, c : c + LANES] * z_t
            g_scr[slot][rows, c : c + LANES] = g.astype(jnp.bfloat16)

    def gradients(b, slot, k):
        _, _, s_keys_t, out_t, at = keys(k)
        g = g_scr[slot][:, k * chunk : (k + 1) * chunk]
        term = lax.dot_general(s_keys_t[:, at : at + chunk], g, CONTRACT_LAST, preferred_element_type=jnp.float32)
        acc_scr[...] = term if k == 0 else acc_scr[...] + term
        out_t[:, at : at + chunk] += jnp.dot(
            jnp.transpose(s_own[rows_of(b), :]), g, preferred_element_type=jnp.float32
        )

    def close(b):
        own_ref[rows_of(b), :] += jnp.transpose(acc_scr[...])

    own_ref[...] = jnp.zeros_like(own_ref)
    own_t[...] = jnp.zeros_like(own_t)
    other_t[...] = jnp.zeros_like(other_t)
    g_scr[1][...] = jnp.zeros_like(g_scr[1])
    s_own_t[...] = jnp.transpose(s_own[...])
    s_other_t[...] = jnp.transpose(s_other[...])
    for k in range(pieces):
        scores(0, 0, k)

    def step(b, slot):
        before = jnp.maximum(b - 1, 0)
        after = jnp.minimum(b + 1, count - 1)
        for k in range(pieces):
            scores(after, 1 - slot, k)
            gradients(before, 1 - slot, k)
            softmax(slot, k)
        close(before)
        row = in_order(b * block) // block
        kl_ref[pl.ds(row, 1), :] = jnp.transpose(kl_scr[...])[:1]

    def pair(i, _):
        step(2 * i, 0)
        step(2 * i + 1, 1)
        return 0

    lax.fori_loop(0, count // 2, pair, 0)
    for k in range(pieces):
        gradients(count - 1, 1, k)
    close(count - 1)
    own_ref[...] = (own_ref[...] + jnp.transpose(own_t[...])) * scale
    other_ref[...] = jnp.transpose(other_t[...]) * scale


def relation(t_own, s_own, t_other, s_other, block=256, pieces=8):
    half, t_width = t_own.shape
    s_width = s_own.shape[1]
    return pl.pallas_call(
        functools.partial(relation_kernel, block, pieces),
        in_specs=[WHOLE] * 4,
        out_specs=[WHOLE] * 3,
        out_shape=[
            jax.ShapeDtypeStruct((half // block, block), jnp.float32),
            jax.ShapeDtypeStruct((half, s_width), jnp.float32),
            jax.ShapeDtypeStruct((half, s_width), jnp.float32),
        ],
        scratch_shapes=[pltpu.VMEM((block, 2 * half), jnp.float32)] * 4
        + [pltpu.VMEM((block, 2 * half), jnp.bfloat16)] * 2
        + [pltpu.VMEM((pieces, block, LANES), jnp.float32)] * 4
        + [pltpu.VMEM((s_width, block), jnp.float32), pltpu.VMEM((block, LANES), jnp.float32)]
        + [pltpu.VMEM((s_width, half), jnp.float32)] * 2
        + [pltpu.VMEM((s_width, half), jnp.bfloat16)] * 2,
        cost_estimate=pl.CostEstimate(
            flops=2 * half * 2 * half * (t_width + 3 * s_width),
            bytes_accessed=6 * half * (t_width + 3 * s_width),
            transcendentals=4 * half * half,
        ),
        compiler_params=pltpu.CompilerParams(vmem_limit_bytes=56 << 20),
    )(t_own, s_own, t_other, s_other)


def owned_rows(kl):
    kl = kl.reshape(2, 2, 2, 2, LANES).transpose(2, 0, 3, 1, 4).reshape(4, 4, LANES)
    source = lax.axis_index("xh") * 2 + lax.axis_index("core")
    got = []
    for turn in range(4):
        pairs = []
        for c in range(2):
            for dp in range(32):
                xh, xl, zh, zl, yh = ((dp >> k) & 1 for k in (4, 3, 2, 1, 0))
                quarter = turn ^ (xh * 2 + c)
                pairs.append((c * 32 + dp, zh * 32 + (xh ^ xl) * 16 + (zh ^ zl) * 8 + yh * 4 + quarter))
        sent = lax.dynamic_index_in_dim(kl, turn ^ source, 0, keepdims=False)
        got.append(lax.ppermute(sent, ("core",) + DP, pairs))
    got = jnp.stack(got)
    quarter = lax.axis_index(DP) % 4
    rows = [lax.dynamic_index_in_dim(got, f ^ quarter, 0, keepdims=False) for f in range(4)]
    rows = jnp.stack(rows).reshape(2, 2, 4, LANES)
    return rows.transpose(0, 2, 1, 3).reshape(1, 2 * 4 * 2 * LANES)


def local(teacher_query, student_hidden, query_weight):
    rows = teacher_query.shape[0]
    depth, columns = query_weight.shape
    t_width = teacher_query.shape[1] // 8
    width = columns // 4
    core = lax.axis_index("core")
    low = core == 0
    hidden = lax.all_gather(student_hidden, TP + ("xl", "zl"), axis=0).reshape(4, 4, rows, columns)
    parts = jnp.moveaxis(query_weight.reshape(depth, 4, width), 1, 0)
    q = (lax.axis_index("xh") ^ lax.axis_index("xl")) * 2 + (lax.axis_index("zh") ^ lax.axis_index("zl"))
    near = jnp.stack([lax.dynamic_index_in_dim(parts, q ^ r, 0, keepdims=False) for r in range(4)])
    blocks = jnp.stack(
        [near[0]] + [lax.ppermute(near[r], ("xl", "zl"), [(i, i ^ r) for i in range(4)]) for r in range(1, 4)]
    )
    blocks = jnp.stack([blocks, swap(blocks, "yh")])
    runs = [blocks[:, :2], blocks[:, 2:]]
    runs = [jnp.concatenate(both) for both in zip(runs, hop_weight(runs, 0))]
    w_own = [piece for both in zip(runs, hop_weight(runs, 1)) for piece in both]
    w_other = [swap(piece, "core") for piece in w_own]
    first, second = teacher_query[: rows // 2], teacher_query[rows // 2 :]
    t_own, t_other = jnp.where(low, first, second), swap(jnp.where(low, second, first), "core")
    heads = jnp.stack([jnp.where(low, t_own, t_other), jnp.where(low, t_other, t_own)])
    heads = heads.reshape(2, rows // 2, 2, 2, 2, t_width).transpose(0, 4, 2, 3, 1, 5)
    heads = jnp.where(lax.axis_index("xh") == 0, heads, heads[:, :, ::-1])
    heads = jnp.stack([heads[0], heads[1][:, :, ::-1]])
    heads = heads.reshape(16, rows // 2, t_width)
    teacher = exchange(heads, SPREAD).reshape(2048, t_width)
    teacher_other = swap(teacher, "core")
    student = jnp.concatenate(trade(project(hidden, w_own, w_other)))
    student_other = swap(student, "core")

    kl, grad, grad_other = relation(teacher, student, teacher_other, student_other)
    query_grad = (grad + swap(grad_other, "core")).astype(jnp.bfloat16)
    query_grad = trade(query_grad.reshape(4, 512, -1))
    near, away = jnp.stack(query_grad[:2]), jnp.stack(query_grad[2:])
    same = core == lax.axis_index("zh")
    mine = jnp.where(same, near, away)
    theirs = swap(jnp.where(same, away, near), "core")
    sent = exchange(weight_grad_part(hidden, mine, theirs), DP)
    kl_rows = owned_rows(kl)
    sent = sent.reshape(2, 2, 2, 2, 2, depth, width)
    groups = []
    for q in range(4):
        total = None
        for xh in range(2):
            for zh in range(2):
                for yh in range(2):
                    term = sent[xh, xh ^ (q >> 1), zh, zh ^ (q & 1), yh].astype(jnp.float32)
                    total = term if total is None else total + term
        groups.append(total)
    return kl_rows, jnp.concatenate(groups, axis=1)


def solution(mesh):
    bits = Mesh(mesh.devices.reshape((2,) * 7), TP + DP)
    return jax.shard_map(
        local,
        mesh=bits,
        in_specs=(P(DP, TP), P(DP, TP), P(DP, TP)),
        out_specs=(P(TP + DP, None), P(DP, TP)),
        check_vma=False,
    )
```

```python
import functools

import jax
import jax.numpy as jnp
from jax import lax
from jax.experimental import pallas as pl
from jax.experimental.pallas import tpu as pltpu
from jax.sharding import Mesh, PartitionSpec as P

LOG2E = 1.4426950408889634
LN2 = 0.6931471805599453
LANES = 128

TP = ("yl", "core")
DP = ("xh", "xl", "zh", "zl", "yh")
BLOCK = ("zh", "yh")
SPREAD = ("zh", "yh", "xl", "zl")
XZ = (("xh", "xl"), ("zh", "zl"))
SWAP = [(0, 1), (1, 0)]

CONTRACT_LAST = (((1,), (1,)), ((), ()))
CONTRACT_FIRST = (((0,), (0,)), ((), ()))
WHOLE = pl.BlockSpec(memory_space=pltpu.VMEM)


def swap(value, axis):
    return lax.ppermute(value, axis, SWAP)


def exchange(chunks, axes):
    return lax.all_to_all(chunks, axes, split_axis=0, concat_axis=0, tiled=True)


RUNS = ((0, 80, (0, 1, 2)), (80, 160, (1, 2, 0)), (160, 256, (2, 0, 1)))
CUBE = ("xl", "yl", "zl")


def hop(held, stage):
    return [swap(piece, CUBE[order[stage]]) for piece, (_, _, order) in zip(held, RUNS)]


def joined(held, far):
    return [jnp.concatenate(both) for both in zip(held, far)]


def trade(chunks):
    got = [chunks[0]]
    for r in range(1, 4):
        step = (r >> 1) * 6 + (r & 1)
        got.append(lax.ppermute(chunks[r], ("zh", "zl", "yh"), [(i, i ^ step) for i in range(8)]))
    return got


def hop_weight(held, stage):
    return [
        lax.ppermute(piece, axes, [(i, i ^ 3) for i in range(4)]) for piece, axes in zip(held, (XZ, XZ[::-1])[stage])
    ]


def weight_in_order(refs, out):
    depth = refs[0].shape[2]
    for run in range(2):
        for e in range(8):
            ex, ez = (e >> 1 & 1, e >> 2) if run == 0 else (e >> 2, e >> 1 & 1)
            for b in range(2):
                place = (
                    (lax.axis_index("xh") ^ ex) * 16
                    + (lax.axis_index("xl") ^ ex ^ run) * 8
                    + (lax.axis_index("zh") ^ ez) * 4
                    + (lax.axis_index("zl") ^ ez ^ b) * 2
                    + (lax.axis_index("yh") ^ (e & 1))
                )
                rows = pl.ds(pl.multiple_of(place * depth, depth), depth)
                out[rows, :] = refs[2 * run + e // 4][e % 4, b]


def together(first, second):
    both = lax.optimization_barrier((tuple(first), tuple(second)))
    return list(both[0]), list(both[1])


def after(value, *others):
    return lax.optimization_barrier((value, *others))[0]


def run_piece(refs, run, hops, first, last):
    order = RUNS[run][2]
    place = sum(hops[order[k]] << k for k in range(3))
    return refs[2 * run + place // 4][place % 4, first:last, :]


def hidden_tile(refs, dy, rel):
    rows = []
    for dx in range(2):
        for dz in range(2):
            hops = (dx, dy, dz)
            if rel == 0:
                rows += [run_piece(refs, 0, hops, 0, 80), run_piece(refs, 1, hops, 0, 48)]
            else:
                rows += [run_piece(refs, 1, hops, 48, 80), run_piece(refs, 2, hops, 0, 96)]
    return jnp.concatenate(rows, axis=0)


def token_place(dx, dz):
    return (lax.axis_index("xl") ^ dx) * 2 + (lax.axis_index("zl") ^ dz)


def project_kernel(*refs):
    hidden, (out, w_own, w_other) = refs[:6], refs[14:]
    weight_in_order(refs[6:10], w_own)
    weight_in_order(refs[10:14], w_other)
    core = lax.axis_index("core")
    features = w_own.shape[0] // 4
    parts = [None, None]
    for dy in range(2):
        for rel in range(2):
            tile = hidden_tile(hidden, dy, rel)
            block = (lax.axis_index("yl") ^ dy) * 2 + (core ^ rel)
            depth = pl.ds(pl.multiple_of(block * features, features), features)
            for i, weight in enumerate((w_own, w_other)):
                term = jnp.dot(tile, weight[depth, :], preferred_element_type=jnp.float32)
                parts[i] = term if parts[i] is None else parts[i] + term
    for i in range(2):
        value = parts[i].astype(jnp.bfloat16)
        for j in range(2):
            for dx in range(2):
                for dz in range(2):
                    at = (dx * 2 + dz) * 128
                    rows = pl.ds(pl.multiple_of(token_place(dx, dz) * 128, 128), 128)
                    slot = (core ^ i ^ lax.axis_index("zh")) * 2 + (lax.axis_index("yh") ^ j)
                    out[slot, rows, :] = value[at : at + 128, j * 128 : (j + 1) * 128]


def project(hidden, w_own, w_other):
    return pl.pallas_call(
        project_kernel,
        in_specs=[WHOLE] * 14,
        out_specs=WHOLE,
        out_shape=jax.ShapeDtypeStruct((4, 512, 128), jnp.bfloat16),
        scratch_shapes=[pltpu.VMEM((4096, 256), jnp.bfloat16)] * 2,
        cost_estimate=pl.CostEstimate(flops=2 * 512 * 4096 * 512, bytes_accessed=9 << 20, transcendentals=0),
        compiler_params=pltpu.CompilerParams(vmem_limit_bytes=48 << 20),
    )(*hidden, *w_own, *w_other)


def weight_grad_kernel(*refs):
    own, other, (q_own, q_other, out) = refs[:6], refs[6:12], refs[12:]
    core = lax.axis_index("core")

    def in_place(ref):
        rows = []
        for dx in range(2):
            for dz in range(2):
                at = pl.ds(pl.multiple_of(token_place(dx, dz) * 128, 128), 128)
                yh = lax.axis_index("yh")
                rows.append(jnp.concatenate([ref[yh, at, :], ref[1 - yh, at, :]], axis=1))
        return rows

    grad = jnp.concatenate(in_place(q_own) + in_place(q_other), axis=0)
    for dy in range(2):
        for rel in range(2):
            tile = jnp.concatenate([hidden_tile(own, dy, rel), hidden_tile(other, dy, 1 - rel)], axis=0)
            block = (lax.axis_index("yl") ^ dy) * 2 + (core ^ rel)
            value = lax.dot_general(tile, grad, CONTRACT_FIRST, preferred_element_type=jnp.float32)
            count = value.shape[0] // 128
            out[pl.ds(block * count, count)] = value.astype(jnp.bfloat16).reshape(count, 128, value.shape[1])


def weight_grad_part(own, other, q_own, q_other):
    return pl.pallas_call(
        weight_grad_kernel,
        in_specs=[WHOLE] * 14,
        out_specs=WHOLE,
        out_shape=jax.ShapeDtypeStruct((32, 128, 256), jnp.bfloat16),
        cost_estimate=pl.CostEstimate(flops=2 * 1024 * 4096 * 256, bytes_accessed=11 << 20, transcendentals=0),
        compiler_params=pltpu.CompilerParams(vmem_limit_bytes=48 << 20),
    )(*own, *other, q_own, q_other)


def lane_fold(x, op):
    acc = x[:, :LANES]
    for j in range(1, x.shape[1] // LANES):
        acc = op(acc, x[:, j * LANES : (j + 1) * LANES])
    return acc


def relation_kernel(block, pieces, t_own, s_own, t_other, s_other, kl_ref, own_ref, other_ref, *scratch):
    u_scr, v_scr, g_scr, mt_scr, ms_scr = (scratch[2 * i : 2 * i + 2] for i in range(5))
    acc_scr, kl_scr, own_t, other_t, s_own_t, s_other_t = scratch[10:]
    half, t_width = t_own.shape
    scale = s_own.shape[1] ** -0.5
    t_mul = LOG2E * t_width**-0.5
    s_mul = LOG2E * scale
    chunk = 2 * half // pieces
    sub = block // pieces
    count = half // block
    here = lax.axis_index("zh") * 2 + lax.axis_index("yh")
    part = half // 4

    def in_order(row):
        return (row // part ^ here) * part + row % part

    def keys(k):
        at = k * chunk
        if at < half:
            return t_own, s_own, s_own_t, own_t, at
        return t_other, s_other, s_other_t, other_t, at - half

    def rows_of(b):
        return pl.ds(pl.multiple_of(b * block, block), block)

    def scores(b, slot, k):
        t_keys, s_keys, _, _, at = keys(k)
        columns = slice(k * chunk, (k + 1) * chunk)
        t_rows = t_own[pl.ds(pl.multiple_of(in_order(b * block), block), block), :]
        t_at = pl.ds(pl.multiple_of(in_order(at), chunk), chunk)
        u = t_mul * lax.dot_general(t_rows, t_keys[t_at, :], CONTRACT_LAST, preferred_element_type=jnp.float32)
        u_scr[slot][:, columns] = u
        mt_scr[slot][k] = lane_fold(u, jnp.maximum)
        s_keys = s_keys[at : at + chunk, :]
        v = s_mul * lax.dot_general(s_own[rows_of(b), :], s_keys, CONTRACT_LAST, preferred_element_type=jnp.float32)
        v_scr[slot][:, columns] = v
        ms_scr[slot][k] = lane_fold(v, jnp.maximum)

    def softmax(slot, k):
        rows = slice(k * sub, (k + 1) * sub)
        u, v = u_scr[slot], v_scr[slot]
        m_t, m_s = mt_scr[slot][0, rows], ms_scr[slot][0, rows]
        for j in range(1, pieces):
            m_t = jnp.maximum(m_t, mt_scr[slot][j, rows])
            m_s = jnp.maximum(m_s, ms_scr[slot][j, rows])
        m_t = jnp.broadcast_to(jnp.max(m_t, axis=1, keepdims=True), (sub, LANES))
        m_s = jnp.broadcast_to(jnp.max(m_s, axis=1, keepdims=True), (sub, LANES))
        zero = jnp.zeros((sub, LANES), jnp.float32)
        lt, ls, a = zero, zero, zero
        for c in range(0, 2 * half, LANES):
            x = u[rows, c : c + LANES] - m_t
            y = v[rows, c : c + LANES] - m_s
            et, es = jnp.exp2(x), jnp.exp2(y)
            u[rows, c : c + LANES] = et
            v[rows, c : c + LANES] = es
            lt = lt + et
            ls = ls + es
            a = a + et * (x - y)
        lt = jnp.sum(lt, axis=1, keepdims=True)
        ls = jnp.sum(ls, axis=1, keepdims=True)
        a = jnp.sum(a, axis=1, keepdims=True)
        kl_scr[rows, :] = jnp.broadcast_to((a / lt - jnp.log2(lt) + jnp.log2(ls)) * LN2, (sub, LANES))
        z_t = jnp.broadcast_to(1.0 / lt, (sub, LANES))
        z_s = jnp.broadcast_to(1.0 / ls, (sub, LANES))
        for c in range(0, 2 * half, LANES):
            g = v[rows, c : c + LANES] * z_s - u[rows, c : c + LANES] * z_t
            g_scr[slot][rows, c : c + LANES] = g.astype(jnp.bfloat16)

    def gradients(b, slot, k):
        _, _, s_keys_t, out_t, at = keys(k)
        g = g_scr[slot][:, k * chunk : (k + 1) * chunk]
        term = lax.dot_general(s_keys_t[:, at : at + chunk], g, CONTRACT_LAST, preferred_element_type=jnp.float32)
        acc_scr[...] = term if k == 0 else acc_scr[...] + term
        out_t[:, at : at + chunk] += jnp.dot(
            jnp.transpose(s_own[rows_of(b), :]), g, preferred_element_type=jnp.float32
        )

    def close(b):
        own_ref[rows_of(b), :] += jnp.transpose(acc_scr[...])

    own_ref[...] = jnp.zeros_like(own_ref)
    own_t[...] = jnp.zeros_like(own_t)
    other_t[...] = jnp.zeros_like(other_t)
    g_scr[1][...] = jnp.zeros_like(g_scr[1])
    s_own_t[...] = jnp.transpose(s_own[...])
    s_other_t[...] = jnp.transpose(s_other[...])
    for k in range(pieces):
        scores(0, 0, k)

    def step(b, slot):
        before = jnp.maximum(b - 1, 0)
        after = jnp.minimum(b + 1, count - 1)
        for k in range(pieces):
            scores(after, 1 - slot, k)
            gradients(before, 1 - slot, k)
            softmax(slot, k)
        close(before)
        row = in_order(b * block) // block
        kl_ref[pl.ds(row, 1), :] = jnp.transpose(kl_scr[...])[:1]

    def pair(i, _):
        step(2 * i, 0)
        step(2 * i + 1, 1)
        return 0

    lax.fori_loop(0, count // 2, pair, 0)
    for k in range(pieces):
        gradients(count - 1, 1, k)
    close(count - 1)
    own_ref[...] = (own_ref[...] + jnp.transpose(own_t[...])) * scale
    other_ref[...] = jnp.transpose(other_t[...]) * scale


def relation(t_own, s_own, t_other, s_other, block=256, pieces=8):
    half, t_width = t_own.shape
    s_width = s_own.shape[1]
    return pl.pallas_call(
        functools.partial(relation_kernel, block, pieces),
        in_specs=[WHOLE] * 4,
        out_specs=[WHOLE] * 3,
        out_shape=[
            jax.ShapeDtypeStruct((half // block, block), jnp.float32),
            jax.ShapeDtypeStruct((half, s_width), jnp.float32),
            jax.ShapeDtypeStruct((half, s_width), jnp.float32),
        ],
        scratch_shapes=[pltpu.VMEM((block, 2 * half), jnp.float32)] * 4
        + [pltpu.VMEM((block, 2 * half), jnp.bfloat16)] * 2
        + [pltpu.VMEM((pieces, block, LANES), jnp.float32)] * 4
        + [pltpu.VMEM((s_width, block), jnp.float32), pltpu.VMEM((block, LANES), jnp.float32)]
        + [pltpu.VMEM((s_width, half), jnp.float32)] * 2
        + [pltpu.VMEM((s_width, half), jnp.bfloat16)] * 2,
        cost_estimate=pl.CostEstimate(
            flops=2 * half * 2 * half * (t_width + 3 * s_width),
            bytes_accessed=6 * half * (t_width + 3 * s_width),
            transcendentals=4 * half * half,
        ),
        compiler_params=pltpu.CompilerParams(vmem_limit_bytes=56 << 20),
    )(t_own, s_own, t_other, s_other)


def owned_rows(kl):
    kl = kl.reshape(2, 2, 2, 2, LANES).transpose(2, 0, 3, 1, 4).reshape(4, 4, LANES)
    source = lax.axis_index("xh") * 2 + lax.axis_index("core")
    got = []
    for turn in range(4):
        pairs = []
        for c in range(2):
            for dp in range(32):
                xh, xl, zh, zl, yh = ((dp >> k) & 1 for k in (4, 3, 2, 1, 0))
                quarter = turn ^ (xh * 2 + c)
                pairs.append((c * 32 + dp, zh * 32 + (xh ^ xl) * 16 + (zh ^ zl) * 8 + yh * 4 + quarter))
        sent = lax.dynamic_index_in_dim(kl, turn ^ source, 0, keepdims=False)
        got.append(lax.ppermute(sent, ("core",) + DP, pairs))
    got = jnp.stack(got)
    quarter = lax.axis_index(DP) % 4
    rows = [lax.dynamic_index_in_dim(got, f ^ quarter, 0, keepdims=False) for f in range(4)]
    rows = jnp.stack(rows).reshape(2, 2, 4, LANES)
    return rows.transpose(0, 2, 1, 3).reshape(1, 2 * 4 * 2 * LANES)


def local(teacher_query, student_hidden, query_weight):
    rows = teacher_query.shape[0]
    depth, columns = query_weight.shape
    t_width = teacher_query.shape[1] // 8
    width = columns // 4
    core = lax.axis_index("core")
    low = core == 0

    def token_halves(value):
        first, second = value[: rows // 2], value[rows // 2 :]
        return jnp.where(low, first, second), swap(jnp.where(low, second, first), "core")

    parts = jnp.moveaxis(query_weight.reshape(depth, 4, width), 1, 0)
    q = (lax.axis_index("xh") ^ lax.axis_index("xl")) * 2 + (lax.axis_index("zh") ^ lax.axis_index("zl"))
    near = jnp.stack([lax.dynamic_index_in_dim(parts, q ^ r, 0, keepdims=False) for r in range(4)])
    share = jnp.concatenate(token_halves(student_hidden))
    held = [share[None, first:last] for first, last, _ in RUNS]
    far, blocks = together(
        hop(held, 0),
        [near[0]] + [lax.ppermute(near[r], ("xl", "zl"), [(i, i ^ r) for i in range(4)]) for r in range(1, 4)],
    )
    held = joined(held, far)
    blocks = jnp.stack(blocks)
    t_own, t_other = token_halves(teacher_query)
    heads = jnp.stack([jnp.where(low, t_own, t_other), jnp.where(low, t_other, t_own)])
    heads = heads.reshape(2, rows // 2, 2, 2, 2, t_width).transpose(0, 4, 2, 3, 1, 5)
    heads = jnp.where(lax.axis_index("xh") == 0, heads, heads[:, :, ::-1])
    heads = jnp.stack([heads[0], heads[1][:, :, ::-1]])
    heads = heads.reshape(16, rows // 2, t_width)
    far, (more, heads) = together(hop(held, 1), [swap(blocks, "yh"), heads])
    held = joined(held, far)
    blocks = jnp.stack([blocks, more])
    runs = [blocks[:, :2], blocks[:, 2:]]
    far = hop(held, 2)
    hidden = [piece for both in zip(held, far) for piece in both]
    passed = hop_weight(runs, 0)
    teacher = exchange(heads, SPREAD).reshape(2048, t_width)
    runs = joined(runs, passed)
    w_own = [piece for both in zip(runs, hop_weight(runs, 1)) for piece in both]
    w_other = [swap(piece, "core") for piece in w_own]
    student = jnp.concatenate(trade(project(hidden, w_own, w_other)))
    teacher_other = swap(teacher, "core")
    behind, _ = together(hidden, [teacher])
    hidden_other = [swap(piece, "core") for piece in behind]
    student_other = swap(student, "core")

    kl, grad, grad_other = relation(after(teacher, *hidden_other), student, teacher_other, student_other)
    query_grad = (grad + swap(grad_other, "core")).astype(jnp.bfloat16)
    query_grad = trade(query_grad.reshape(4, 512, -1))
    near, away = jnp.stack(query_grad[:2]), jnp.stack(query_grad[2:])
    same = core == lax.axis_index("zh")
    mine = jnp.where(same, near, away)
    theirs = swap(jnp.where(same, away, near), "core")
    sent = exchange(weight_grad_part(hidden, hidden_other, mine, theirs), DP)
    kl_rows = owned_rows(kl)
    sent = sent.reshape(2, 2, 2, 2, 2, depth, width)
    groups = []
    for q in range(4):
        total = None
        for xh in range(2):
            for zh in range(2):
                for yh in range(2):
                    term = sent[xh, xh ^ (q >> 1), zh, zh ^ (q & 1), yh].astype(jnp.float32)
                    total = term if total is None else total + term
        groups.append(total)
    return kl_rows, jnp.concatenate(groups, axis=1)


def solution(mesh):
    bits = Mesh(mesh.devices.reshape((2,) * 7), TP + DP)
    return jax.shard_map(
        local,
        mesh=bits,
        in_specs=(P(DP, TP), P(DP, TP), P(DP, TP)),
        out_specs=(P(TP + DP, None), P(DP, TP)),
        check_vma=False,
    )
```

```python
import functools

import jax
import jax.numpy as jnp
from jax import lax
from jax.experimental import pallas as pl
from jax.experimental.pallas import tpu as pltpu
from jax.sharding import Mesh, PartitionSpec as P

LOG2E = 1.4426950408889634
LN2 = 0.6931471805599453
LANES = 128

TP = ("yl", "core")
DP = ("xh", "xl", "zh", "zl", "yh")
BLOCK = ("zh", "yh")
SPREAD = ("zh", "yh", "xl", "zl")
XZ = (("xh", "xl"), ("zh", "zl"))
SWAP = [(0, 1), (1, 0)]

CONTRACT_LAST = (((1,), (1,)), ((), ()))
CONTRACT_FIRST = (((0,), (0,)), ((), ()))
WHOLE = pl.BlockSpec(memory_space=pltpu.VMEM)


def swap(value, axis):
    return lax.ppermute(value, axis, SWAP)


def exchange(chunks, axes):
    return lax.all_to_all(chunks, axes, split_axis=0, concat_axis=0, tiled=True)


RUNS = ((0, 80, (0, 1, 2)), (80, 160, (1, 2, 0)), (160, 256, (2, 0, 1)))
CUBE = ("xl", "yl", "zl")


def hop(held, stage):
    return [swap(piece, CUBE[order[stage]]) for piece, (_, _, order) in zip(held, RUNS)]


def joined(held, far):
    return [jnp.concatenate(both) for both in zip(held, far)]


def trade(chunks):
    got = [chunks[0]]
    for r in range(1, 4):
        step = (r >> 1) * 6 + (r & 1)
        got.append(lax.ppermute(chunks[r], ("zh", "zl", "yh"), [(i, i ^ step) for i in range(8)]))
    return got


def hop_weight(held, stage):
    return [
        lax.ppermute(piece, axes, [(i, i ^ 3) for i in range(4)]) for piece, axes in zip(held, (XZ, XZ[::-1])[stage])
    ]


def weight_in_order(refs, out):
    depth = refs[0].shape[2]
    for run in range(2):
        for e in range(8):
            ex, ez = (e >> 1 & 1, e >> 2) if run == 0 else (e >> 2, e >> 1 & 1)
            for b in range(2):
                place = (
                    (lax.axis_index("xh") ^ ex) * 16
                    + (lax.axis_index("xl") ^ ex ^ run) * 8
                    + (lax.axis_index("zh") ^ ez) * 4
                    + (lax.axis_index("zl") ^ ez ^ b) * 2
                    + (lax.axis_index("yh") ^ (e & 1))
                )
                rows = pl.ds(pl.multiple_of(place * depth, depth), depth)
                out[rows, :] = refs[2 * run + e // 4][e % 4, b]


def together(first, second):
    both = lax.optimization_barrier((tuple(first), tuple(second)))
    return list(both[0]), list(both[1])


def after(value, *others):
    return lax.optimization_barrier((value, *others))[0]


def run_piece(refs, run, hops, first, last):
    order = RUNS[run][2]
    place = sum(hops[order[k]] << k for k in range(3))
    return refs[2 * run + place // 4][place % 4, first:last, :]


def hidden_tile(refs, dy, rel):
    rows = []
    for dx in range(2):
        for dz in range(2):
            hops = (dx, dy, dz)
            if rel == 0:
                rows += [run_piece(refs, 0, hops, 0, 80), run_piece(refs, 1, hops, 0, 48)]
            else:
                rows += [run_piece(refs, 1, hops, 48, 80), run_piece(refs, 2, hops, 0, 96)]
    return jnp.concatenate(rows, axis=0)


def token_place(dx, dz):
    return (lax.axis_index("xl") ^ dx) * 2 + (lax.axis_index("zl") ^ dz)


def project_kernel(*refs):
    hidden, (out, w_own, w_other) = refs[:6], refs[14:]
    weight_in_order(refs[6:10], w_own)
    weight_in_order(refs[10:14], w_other)
    core = lax.axis_index("core")
    features = w_own.shape[0] // 4
    parts = [None, None]
    for dy in range(2):
        for rel in range(2):
            tile = hidden_tile(hidden, dy, rel)
            block = (lax.axis_index("yl") ^ dy) * 2 + (core ^ rel)
            depth = pl.ds(pl.multiple_of(block * features, features), features)
            for i, weight in enumerate((w_own, w_other)):
                term = jnp.dot(tile, weight[depth, :], preferred_element_type=jnp.float32)
                parts[i] = term if parts[i] is None else parts[i] + term
    for i in range(2):
        value = parts[i].astype(jnp.bfloat16)
        for j in range(2):
            for dx in range(2):
                for dz in range(2):
                    at = (dx * 2 + dz) * 128
                    rows = pl.ds(pl.multiple_of(token_place(dx, dz) * 128, 128), 128)
                    slot = (core ^ i ^ lax.axis_index("zh")) * 2 + (lax.axis_index("yh") ^ j)
                    out[slot, rows, :] = value[at : at + 128, j * 128 : (j + 1) * 128]


def project(hidden, w_own, w_other):
    return pl.pallas_call(
        project_kernel,
        in_specs=[WHOLE] * 14,
        out_specs=WHOLE,
        out_shape=jax.ShapeDtypeStruct((4, 512, 128), jnp.bfloat16),
        scratch_shapes=[pltpu.VMEM((4096, 256), jnp.bfloat16)] * 2,
        cost_estimate=pl.CostEstimate(flops=2 * 512 * 4096 * 512, bytes_accessed=9 << 20, transcendentals=0),
        compiler_params=pltpu.CompilerParams(vmem_limit_bytes=48 << 20),
    )(*hidden, *w_own, *w_other)


def weight_grad_kernel(*refs):
    own, other, (q_own, q_other, out) = refs[:6], refs[6:12], refs[12:]
    core = lax.axis_index("core")

    def in_place(ref):
        rows = []
        for dx in range(2):
            for dz in range(2):
                at = pl.ds(pl.multiple_of(token_place(dx, dz) * 128, 128), 128)
                yh = lax.axis_index("yh")
                rows.append(jnp.concatenate([ref[yh, at, :], ref[1 - yh, at, :]], axis=1))
        return rows

    grad = jnp.concatenate(in_place(q_own) + in_place(q_other), axis=0)
    for dy in range(2):
        for rel in range(2):
            tile = jnp.concatenate([hidden_tile(own, dy, rel), hidden_tile(other, dy, 1 - rel)], axis=0)
            block = (lax.axis_index("yl") ^ dy) * 2 + (core ^ rel)
            value = lax.dot_general(tile, grad, CONTRACT_FIRST, preferred_element_type=jnp.float32)
            count = value.shape[0] // 128
            out[pl.ds(block * count, count)] = value.astype(jnp.bfloat16).reshape(count, 128, value.shape[1])


def weight_grad_part(own, other, q_own, q_other):
    return pl.pallas_call(
        weight_grad_kernel,
        in_specs=[WHOLE] * 14,
        out_specs=WHOLE,
        out_shape=jax.ShapeDtypeStruct((32, 128, 256), jnp.bfloat16),
        cost_estimate=pl.CostEstimate(flops=2 * 1024 * 4096 * 256, bytes_accessed=11 << 20, transcendentals=0),
        compiler_params=pltpu.CompilerParams(vmem_limit_bytes=48 << 20),
    )(*own, *other, q_own, q_other)


def lane_fold(x, op):
    acc = x[:, :LANES]
    for j in range(1, x.shape[1] // LANES):
        acc = op(acc, x[:, j * LANES : (j + 1) * LANES])
    return acc


def relation_kernel(block, pieces, t_own, s_own, t_other, s_other, kl_ref, own_ref, other_ref, *scratch):
    u_scr, v_scr, g_scr, mt_scr, ms_scr = (scratch[2 * i : 2 * i + 2] for i in range(5))
    acc_scr, kl_scr, own_t, other_t, s_own_t, s_other_t = scratch[10:]
    half, t_width = t_own.shape
    scale = s_own.shape[1] ** -0.5
    t_mul = LOG2E * t_width**-0.5
    s_mul = LOG2E * scale
    chunk = 2 * half // pieces
    sub = block // pieces
    count = half // block
    here = lax.axis_index("zh") * 2 + lax.axis_index("yh")
    part = half // 4

    def in_order(row):
        return (row // part ^ here) * part + row % part

    def keys(k):
        at = k * chunk
        if at < half:
            return t_own, s_own, s_own_t, own_t, at
        return t_other, s_other, s_other_t, other_t, at - half

    def rows_of(b):
        return pl.ds(pl.multiple_of(b * block, block), block)

    def scores(b, slot, k):
        t_keys, s_keys, _, _, at = keys(k)
        columns = slice(k * chunk, (k + 1) * chunk)
        t_rows = t_own[pl.ds(pl.multiple_of(in_order(b * block), block), block), :]
        t_at = pl.ds(pl.multiple_of(in_order(at), chunk), chunk)
        u = t_mul * lax.dot_general(t_rows, t_keys[t_at, :], CONTRACT_LAST, preferred_element_type=jnp.float32)
        u_scr[slot][:, columns] = u
        mt_scr[slot][k] = lane_fold(u, jnp.maximum)
        s_keys = s_keys[at : at + chunk, :]
        v = s_mul * lax.dot_general(s_own[rows_of(b), :], s_keys, CONTRACT_LAST, preferred_element_type=jnp.float32)
        v_scr[slot][:, columns] = v
        ms_scr[slot][k] = lane_fold(v, jnp.maximum)

    def softmax(slot, k):
        rows = slice(k * sub, (k + 1) * sub)
        u, v = u_scr[slot], v_scr[slot]
        m_t, m_s = mt_scr[slot][0, rows], ms_scr[slot][0, rows]
        for j in range(1, pieces):
            m_t = jnp.maximum(m_t, mt_scr[slot][j, rows])
            m_s = jnp.maximum(m_s, ms_scr[slot][j, rows])
        m_t = jnp.broadcast_to(jnp.max(m_t, axis=1, keepdims=True), (sub, LANES))
        m_s = jnp.broadcast_to(jnp.max(m_s, axis=1, keepdims=True), (sub, LANES))
        zero = jnp.zeros((sub, LANES), jnp.float32)
        lt, ls, a = zero, zero, zero
        for c in range(0, 2 * half, LANES):
            x = u[rows, c : c + LANES] - m_t
            y = v[rows, c : c + LANES] - m_s
            et, es = jnp.exp2(x), jnp.exp2(y)
            u[rows, c : c + LANES] = et
            v[rows, c : c + LANES] = es
            lt = lt + et
            ls = ls + es
            a = a + et * (x - y)
        lt = jnp.sum(lt, axis=1, keepdims=True)
        ls = jnp.sum(ls, axis=1, keepdims=True)
        a = jnp.sum(a, axis=1, keepdims=True)
        kl_scr[rows, :] = jnp.broadcast_to((a / lt - jnp.log2(lt) + jnp.log2(ls)) * LN2, (sub, LANES))
        z_t = jnp.broadcast_to(1.0 / lt, (sub, LANES))
        z_s = jnp.broadcast_to(1.0 / ls, (sub, LANES))
        for c in range(0, 2 * half, LANES):
            g = v[rows, c : c + LANES] * z_s - u[rows, c : c + LANES] * z_t
            g_scr[slot][rows, c : c + LANES] = g.astype(jnp.bfloat16)

    def gradients(b, slot, k):
        _, _, s_keys_t, out_t, at = keys(k)
        g = g_scr[slot][:, k * chunk : (k + 1) * chunk]
        term = lax.dot_general(s_keys_t[:, at : at + chunk], g, CONTRACT_LAST, preferred_element_type=jnp.float32)
        acc_scr[...] = term if k == 0 else acc_scr[...] + term
        out_t[:, at : at + chunk] += jnp.dot(
            jnp.transpose(s_own[rows_of(b), :]), g, preferred_element_type=jnp.float32
        )

    def close(b):
        own_ref[rows_of(b), :] += jnp.transpose(acc_scr[...])

    own_ref[...] = jnp.zeros_like(own_ref)
    own_t[...] = jnp.zeros_like(own_t)
    other_t[...] = jnp.zeros_like(other_t)
    g_scr[1][...] = jnp.zeros_like(g_scr[1])
    s_own_t[...] = jnp.transpose(s_own[...])
    s_other_t[...] = jnp.transpose(s_other[...])
    for k in range(pieces):
        scores(0, 0, k)

    def step(b, slot):
        before = jnp.maximum(b - 1, 0)
        after = jnp.minimum(b + 1, count - 1)
        for k in range(pieces):
            scores(after, 1 - slot, k)
            gradients(before, 1 - slot, k)
            softmax(slot, k)
        close(before)
        row = in_order(b * block) // block
        kl_ref[pl.ds(row, 1), :] = jnp.transpose(kl_scr[...])[:1]

    def pair(i, _):
        step(2 * i, 0)
        step(2 * i + 1, 1)
        return 0

    lax.fori_loop(0, count // 2, pair, 0)
    for k in range(pieces):
        gradients(count - 1, 1, k)
    close(count - 1)
    own_ref[...] = (own_ref[...] + jnp.transpose(own_t[...])) * scale
    other_ref[...] = jnp.transpose(other_t[...]) * scale


def relation(t_own, s_own, t_other, s_other, block=256, pieces=8):
    half, t_width = t_own.shape
    s_width = s_own.shape[1]
    return pl.pallas_call(
        functools.partial(relation_kernel, block, pieces),
        in_specs=[WHOLE] * 4,
        out_specs=[WHOLE] * 3,
        out_shape=[
            jax.ShapeDtypeStruct((half // block, block), jnp.float32),
            jax.ShapeDtypeStruct((half, s_width), jnp.float32),
            jax.ShapeDtypeStruct((half, s_width), jnp.float32),
        ],
        scratch_shapes=[pltpu.VMEM((block, 2 * half), jnp.float32)] * 4
        + [pltpu.VMEM((block, 2 * half), jnp.bfloat16)] * 2
        + [pltpu.VMEM((pieces, block, LANES), jnp.float32)] * 4
        + [pltpu.VMEM((s_width, block), jnp.float32), pltpu.VMEM((block, LANES), jnp.float32)]
        + [pltpu.VMEM((s_width, half), jnp.float32)] * 2
        + [pltpu.VMEM((s_width, half), jnp.bfloat16)] * 2,
        cost_estimate=pl.CostEstimate(
            flops=2 * half * 2 * half * (t_width + 3 * s_width),
            bytes_accessed=6 * half * (t_width + 3 * s_width),
            transcendentals=4 * half * half,
        ),
        compiler_params=pltpu.CompilerParams(vmem_limit_bytes=56 << 20),
    )(t_own, s_own, t_other, s_other)


def owned_rows(kl):
    kl = kl.reshape(2, 2, 2, 2, LANES).transpose(2, 0, 3, 1, 4).reshape(4, 4, LANES)
    source = lax.axis_index("xh") * 2 + lax.axis_index("core")
    got = []
    for turn in range(4):
        pairs = []
        for c in range(2):
            for dp in range(32):
                xh, xl, zh, zl, yh = ((dp >> k) & 1 for k in (4, 3, 2, 1, 0))
                quarter = turn ^ (xh * 2 + c)
                pairs.append((c * 32 + dp, zh * 32 + (xh ^ xl) * 16 + (zh ^ zl) * 8 + yh * 4 + quarter))
        sent = lax.dynamic_index_in_dim(kl, turn ^ source, 0, keepdims=False)
        got.append(lax.ppermute(sent, ("core",) + DP, pairs))
    got = jnp.stack(got)
    quarter = lax.axis_index(DP) % 4
    rows = [lax.dynamic_index_in_dim(got, f ^ quarter, 0, keepdims=False) for f in range(4)]
    rows = jnp.stack(rows).reshape(2, 2, 4, LANES)
    return rows.transpose(0, 2, 1, 3).reshape(1, 2 * 4 * 2 * LANES)


def local(teacher_query, student_hidden, query_weight):
    rows = teacher_query.shape[0]
    depth, columns = query_weight.shape
    t_width = teacher_query.shape[1] // 8
    width = columns // 4
    core = lax.axis_index("core")
    low = core == 0

    def token_halves(value):
        first, second = value[: rows // 2], value[rows // 2 :]
        return jnp.where(low, first, second), swap(jnp.where(low, second, first), "core")

    parts = jnp.moveaxis(query_weight.reshape(depth, 4, width), 1, 0)
    q = (lax.axis_index("xh") ^ lax.axis_index("xl")) * 2 + (lax.axis_index("zh") ^ lax.axis_index("zl"))
    near = jnp.stack([lax.dynamic_index_in_dim(parts, q ^ r, 0, keepdims=False) for r in range(4)])
    share = jnp.concatenate(token_halves(student_hidden))
    held = [share[None, first:last] for first, last, _ in RUNS]
    far, blocks = together(
        hop(held, 0),
        [near[0]] + [lax.ppermute(near[r], ("xl", "zl"), [(i, i ^ r) for i in range(4)]) for r in range(1, 4)],
    )
    held = joined(held, far)
    blocks = jnp.stack(blocks)
    t_own, t_other = token_halves(teacher_query)
    heads = jnp.stack([jnp.where(low, t_own, t_other), jnp.where(low, t_other, t_own)])
    heads = heads.reshape(2, rows // 2, 2, 2, 2, t_width).transpose(0, 4, 2, 3, 1, 5)
    heads = jnp.where(lax.axis_index("xh") == 0, heads, heads[:, :, ::-1])
    heads = jnp.stack([heads[0], heads[1][:, :, ::-1]])
    heads = heads.reshape(16, rows // 2, t_width)
    far, (more, heads) = together(hop(held, 1), [swap(blocks, "yh"), heads])
    held = joined(held, far)
    blocks = jnp.stack([blocks, more])
    runs = [blocks[:, :2], blocks[:, 2:]]
    far = hop(held, 2)
    hidden = [piece for both in zip(held, far) for piece in both]
    passed = hop_weight(runs, 0)
    teacher = exchange(heads, SPREAD).reshape(2048, t_width)
    runs = joined(runs, passed)
    w_own = [piece for both in zip(runs, hop_weight(runs, 1)) for piece in both]
    w_other = [swap(piece, "core") for piece in w_own]
    student = jnp.concatenate(trade(project(hidden, w_own, w_other)))
    hidden_other = [swap(piece, "core") for piece in hidden]
    teacher = after(teacher, student, *hidden_other)
    teacher_other = swap(teacher, "core")
    student_other = swap(student, "core")

    kl, grad, grad_other = relation(teacher, student, teacher_other, student_other)
    grad_other = swap(grad_other, "core").reshape(4, 512, -1)
    query_grad = [(mine + theirs).astype(jnp.bfloat16) for mine, theirs in zip(grad.reshape(4, 512, -1), grad_other)]
    query_grad = trade(query_grad)
    near, away = jnp.stack(query_grad[:2]), jnp.stack(query_grad[2:])
    same = core == lax.axis_index("zh")
    mine = jnp.where(same, near, away)
    theirs = swap(jnp.where(same, away, near), "core")
    sent = exchange(weight_grad_part(hidden, hidden_other, mine, theirs), DP)
    kl_rows = owned_rows(kl)
    sent = sent.reshape(2, 2, 2, 2, 2, depth, width)
    groups = []
    for q in range(4):
        total = None
        for xh in range(2):
            for zh in range(2):
                for yh in range(2):
                    term = sent[xh, xh ^ (q >> 1), zh, zh ^ (q & 1), yh].astype(jnp.float32)
                    total = term if total is None else total + term
        groups.append(total)
    return kl_rows, jnp.concatenate(groups, axis=1)


def solution(mesh):
    bits = Mesh(mesh.devices.reshape((2,) * 7), TP + DP)
    return jax.shard_map(
        local,
        mesh=bits,
        in_specs=(P(DP, TP), P(DP, TP), P(DP, TP)),
        out_specs=(P(TP + DP, None), P(DP, TP)),
        check_vma=False,
    )
```

```python
import functools

import jax
import jax.numpy as jnp
from jax import lax
from jax.experimental import pallas as pl
from jax.experimental.pallas import tpu as pltpu
from jax.sharding import Mesh, PartitionSpec as P

LOG2E = 1.4426950408889634
LN2 = 0.6931471805599453
LANES = 128

TP = ("yl", "core")
DP = ("xh", "xl", "zh", "zl", "yh")
BLOCK = ("zh", "yh")
SPREAD = ("zh", "yh", "xl", "zl")
XZ = (("xh", "xl"), ("zh", "zl"))
SWAP = [(0, 1), (1, 0)]

CONTRACT_LAST = (((1,), (1,)), ((), ()))
CONTRACT_FIRST = (((0,), (0,)), ((), ()))
WHOLE = pl.BlockSpec(memory_space=pltpu.VMEM)


def swap(value, axis):
    return lax.ppermute(value, axis, SWAP)


def exchange(chunks, axes):
    return lax.all_to_all(chunks, axes, split_axis=0, concat_axis=0, tiled=True)


RUNS = ((0, 80, (0, 1, 2)), (80, 160, (1, 2, 0)), (160, 256, (2, 0, 1)))
CUBE = ("xl", "yl", "zl")


def hop(held, stage):
    return [swap(piece, CUBE[order[stage]]) for piece, (_, _, order) in zip(held, RUNS)]


def joined(held, far):
    return [jnp.concatenate(both) for both in zip(held, far)]


def trade(chunks):
    got = [chunks[0]]
    for r in range(1, 4):
        step = (r >> 1) * 6 + (r & 1)
        got.append(lax.ppermute(chunks[r], ("zh", "zl", "yh"), [(i, i ^ step) for i in range(8)]))
    return got


def hop_weight(held, stage):
    return [
        lax.ppermute(piece, axes, [(i, i ^ 3) for i in range(4)]) for piece, axes in zip(held, (XZ, XZ[::-1])[stage])
    ]


def weight_in_order(refs, out):
    depth = refs[0].shape[2]
    for run in range(2):
        for e in range(8):
            ex, ez = (e >> 1 & 1, e >> 2) if run == 0 else (e >> 2, e >> 1 & 1)
            for b in range(2):
                place = (
                    (lax.axis_index("xh") ^ ex) * 16
                    + (lax.axis_index("xl") ^ ex ^ run) * 8
                    + (lax.axis_index("zh") ^ ez) * 4
                    + (lax.axis_index("zl") ^ ez ^ b) * 2
                    + (lax.axis_index("yh") ^ (e & 1))
                )
                rows = pl.ds(pl.multiple_of(place * depth, depth), depth)
                out[rows, :] = refs[2 * run + e // 4][e % 4, b]


def together(first, second):
    both = lax.optimization_barrier((tuple(first), tuple(second)))
    return list(both[0]), list(both[1])


def after(value, *others):
    return lax.optimization_barrier((value, *others))[0]


def run_piece(refs, run, hops, first, last):
    order = RUNS[run][2]
    place = sum(hops[order[k]] << k for k in range(3))
    return refs[2 * run + place // 4][place % 4, first:last, :]


def hidden_tile(refs, dy, rel):
    rows = []
    for dx in range(2):
        for dz in range(2):
            hops = (dx, dy, dz)
            if rel == 0:
                rows += [run_piece(refs, 0, hops, 0, 80), run_piece(refs, 1, hops, 0, 48)]
            else:
                rows += [run_piece(refs, 1, hops, 48, 80), run_piece(refs, 2, hops, 0, 96)]
    return jnp.concatenate(rows, axis=0)


def token_place(dx, dz):
    return (lax.axis_index("xl") ^ dx) * 2 + (lax.axis_index("zl") ^ dz)


def project_kernel(*refs):
    hidden, (out, w_own, w_other) = refs[:6], refs[14:]
    weight_in_order(refs[6:10], w_own)
    weight_in_order(refs[10:14], w_other)
    core = lax.axis_index("core")
    features = w_own.shape[0] // 4
    parts = [None, None]
    for dy in range(2):
        for rel in range(2):
            tile = hidden_tile(hidden, dy, rel)
            block = (lax.axis_index("yl") ^ dy) * 2 + (core ^ rel)
            depth = pl.ds(pl.multiple_of(block * features, features), features)
            for i, weight in enumerate((w_own, w_other)):
                term = jnp.dot(tile, weight[depth, :], preferred_element_type=jnp.float32)
                parts[i] = term if parts[i] is None else parts[i] + term
    for i in range(2):
        value = parts[i].astype(jnp.bfloat16)
        for j in range(2):
            for dx in range(2):
                for dz in range(2):
                    at = (dx * 2 + dz) * 128
                    rows = pl.ds(pl.multiple_of(token_place(dx, dz) * 128, 128), 128)
                    slot = (core ^ i ^ lax.axis_index("zh")) * 2 + (lax.axis_index("yh") ^ j)
                    out[slot, rows, :] = value[at : at + 128, j * 128 : (j + 1) * 128]


def project(hidden, w_own, w_other):
    return pl.pallas_call(
        project_kernel,
        in_specs=[WHOLE] * 14,
        out_specs=WHOLE,
        out_shape=jax.ShapeDtypeStruct((4, 512, 128), jnp.bfloat16),
        scratch_shapes=[pltpu.VMEM((4096, 256), jnp.bfloat16)] * 2,
        cost_estimate=pl.CostEstimate(flops=2 * 512 * 4096 * 512, bytes_accessed=9 << 20, transcendentals=0),
        compiler_params=pltpu.CompilerParams(vmem_limit_bytes=48 << 20),
    )(*hidden, *w_own, *w_other)


def weight_grad_kernel(*refs):
    own, other, (q_own, q_other, out) = refs[:6], refs[6:12], refs[12:]
    core = lax.axis_index("core")

    def in_place(ref):
        rows = []
        for dx in range(2):
            for dz in range(2):
                at = pl.ds(pl.multiple_of(token_place(dx, dz) * 128, 128), 128)
                yh = lax.axis_index("yh")
                rows.append(jnp.concatenate([ref[yh, at, :], ref[1 - yh, at, :]], axis=1))
        return rows

    grad_t = jnp.transpose(jnp.concatenate(in_place(q_own) + in_place(q_other), axis=0))
    for dy in range(2):
        for rel in range(2):
            tile = jnp.concatenate([hidden_tile(own, dy, rel), hidden_tile(other, dy, 1 - rel)], axis=0)
            block = (lax.axis_index("yl") ^ dy) * 2 + (core ^ rel)
            value = jnp.dot(grad_t, tile, preferred_element_type=jnp.float32).astype(jnp.bfloat16)
            value = jnp.transpose(value)
            count = value.shape[0] // 128
            out[pl.ds(block * count, count)] = value.reshape(count, 128, value.shape[1])


def weight_grad_part(own, other, q_own, q_other):
    return pl.pallas_call(
        weight_grad_kernel,
        in_specs=[WHOLE] * 14,
        out_specs=WHOLE,
        out_shape=jax.ShapeDtypeStruct((32, 128, 256), jnp.bfloat16),
        cost_estimate=pl.CostEstimate(flops=2 * 1024 * 4096 * 256, bytes_accessed=11 << 20, transcendentals=0),
        compiler_params=pltpu.CompilerParams(vmem_limit_bytes=48 << 20),
    )(*own, *other, q_own, q_other)


def lane_fold(x, op):
    acc = x[:, :LANES]
    for j in range(1, x.shape[1] // LANES):
        acc = op(acc, x[:, j * LANES : (j + 1) * LANES])
    return acc


def relation_kernel(block, pieces, t_own, s_own, t_other, s_other, kl_ref, own_ref, other_ref, *scratch):
    u_scr, v_scr, g_scr, mt_scr, ms_scr = (scratch[2 * i : 2 * i + 2] for i in range(5))
    acc_scr, kl_scr, own_t, other_t, s_own_t, s_other_t = scratch[10:]
    half, t_width = t_own.shape
    scale = s_own.shape[1] ** -0.5
    t_mul = LOG2E * t_width**-0.5
    s_mul = LOG2E * scale
    chunk = 2 * half // pieces
    sub = block // pieces
    count = half // block
    here = lax.axis_index("zh") * 2 + lax.axis_index("yh")
    part = half // 4

    def in_order(row):
        return (row // part ^ here) * part + row % part

    def keys(k):
        at = k * chunk
        if at < half:
            return t_own, s_own, s_own_t, own_t, at
        return t_other, s_other, s_other_t, other_t, at - half

    def rows_of(b):
        return pl.ds(pl.multiple_of(b * block, block), block)

    def scores(b, slot, k):
        t_keys, s_keys, _, _, at = keys(k)
        columns = slice(k * chunk, (k + 1) * chunk)
        t_rows = t_own[pl.ds(pl.multiple_of(in_order(b * block), block), block), :]
        t_at = pl.ds(pl.multiple_of(in_order(at), chunk), chunk)
        u = t_mul * lax.dot_general(t_rows, t_keys[t_at, :], CONTRACT_LAST, preferred_element_type=jnp.float32)
        u_scr[slot][:, columns] = u
        mt_scr[slot][k] = lane_fold(u, jnp.maximum)
        s_keys = s_keys[at : at + chunk, :]
        v = s_mul * lax.dot_general(s_own[rows_of(b), :], s_keys, CONTRACT_LAST, preferred_element_type=jnp.float32)
        v_scr[slot][:, columns] = v
        ms_scr[slot][k] = lane_fold(v, jnp.maximum)

    def softmax(slot, k):
        rows = slice(k * sub, (k + 1) * sub)
        u, v = u_scr[slot], v_scr[slot]
        m_t, m_s = mt_scr[slot][0, rows], ms_scr[slot][0, rows]
        for j in range(1, pieces):
            m_t = jnp.maximum(m_t, mt_scr[slot][j, rows])
            m_s = jnp.maximum(m_s, ms_scr[slot][j, rows])
        m_t = jnp.broadcast_to(jnp.max(m_t, axis=1, keepdims=True), (sub, LANES))
        m_s = jnp.broadcast_to(jnp.max(m_s, axis=1, keepdims=True), (sub, LANES))
        zero = jnp.zeros((sub, LANES), jnp.float32)
        lt, ls, a = zero, zero, zero
        for c in range(0, 2 * half, LANES):
            x = u[rows, c : c + LANES] - m_t
            y = v[rows, c : c + LANES] - m_s
            et, es = jnp.exp2(x), jnp.exp2(y)
            u[rows, c : c + LANES] = et
            v[rows, c : c + LANES] = es
            lt = lt + et
            ls = ls + es
            a = a + et * (x - y)
        lt = jnp.sum(lt, axis=1, keepdims=True)
        ls = jnp.sum(ls, axis=1, keepdims=True)
        a = jnp.sum(a, axis=1, keepdims=True)
        kl_scr[rows, :] = jnp.broadcast_to((a / lt - jnp.log2(lt) + jnp.log2(ls)) * LN2, (sub, LANES))
        z_t = jnp.broadcast_to(1.0 / lt, (sub, LANES))
        z_s = jnp.broadcast_to(1.0 / ls, (sub, LANES))
        for c in range(0, 2 * half, LANES):
            g = v[rows, c : c + LANES] * z_s - u[rows, c : c + LANES] * z_t
            g_scr[slot][rows, c : c + LANES] = g.astype(jnp.bfloat16)

    def gradients(b, slot, k):
        _, _, s_keys_t, out_t, at = keys(k)
        g = g_scr[slot][:, k * chunk : (k + 1) * chunk]
        term = lax.dot_general(s_keys_t[:, at : at + chunk], g, CONTRACT_LAST, preferred_element_type=jnp.float32)
        acc_scr[...] = term if k == 0 else acc_scr[...] + term
        out_t[:, at : at + chunk] += jnp.dot(
            jnp.transpose(s_own[rows_of(b), :]), g, preferred_element_type=jnp.float32
        )

    def close(b):
        own_ref[rows_of(b), :] += jnp.transpose(acc_scr[...])

    own_ref[...] = jnp.zeros_like(own_ref)
    own_t[...] = jnp.zeros_like(own_t)
    other_t[...] = jnp.zeros_like(other_t)
    g_scr[1][...] = jnp.zeros_like(g_scr[1])
    s_own_t[...] = jnp.transpose(s_own[...])
    s_other_t[...] = jnp.transpose(s_other[...])
    for k in range(pieces):
        scores(0, 0, k)

    def step(b, slot):
        before = jnp.maximum(b - 1, 0)
        after = jnp.minimum(b + 1, count - 1)
        for k in range(pieces):
            scores(after, 1 - slot, k)
            gradients(before, 1 - slot, k)
            softmax(slot, k)
        close(before)
        row = in_order(b * block) // block
        kl_ref[pl.ds(row, 1), :] = jnp.transpose(kl_scr[...])[:1]

    def pair(i, _):
        step(2 * i, 0)
        step(2 * i + 1, 1)
        return 0

    lax.fori_loop(0, count // 2, pair, 0)
    for k in range(pieces):
        gradients(count - 1, 1, k)
    close(count - 1)
    own_ref[...] = (own_ref[...] + jnp.transpose(own_t[...])) * scale
    other_ref[...] = jnp.transpose(other_t[...]) * scale


def relation(t_own, s_own, t_other, s_other, block=256, pieces=8):
    half, t_width = t_own.shape
    s_width = s_own.shape[1]
    return pl.pallas_call(
        functools.partial(relation_kernel, block, pieces),
        in_specs=[WHOLE] * 4,
        out_specs=[WHOLE] * 3,
        out_shape=[
            jax.ShapeDtypeStruct((half // block, block), jnp.float32),
            jax.ShapeDtypeStruct((half, s_width), jnp.float32),
            jax.ShapeDtypeStruct((half, s_width), jnp.float32),
        ],
        scratch_shapes=[pltpu.VMEM((block, 2 * half), jnp.float32)] * 4
        + [pltpu.VMEM((block, 2 * half), jnp.bfloat16)] * 2
        + [pltpu.VMEM((pieces, block, LANES), jnp.float32)] * 4
        + [pltpu.VMEM((s_width, block), jnp.float32), pltpu.VMEM((block, LANES), jnp.float32)]
        + [pltpu.VMEM((s_width, half), jnp.float32)] * 2
        + [pltpu.VMEM((s_width, half), jnp.bfloat16)] * 2,
        cost_estimate=pl.CostEstimate(
            flops=2 * half * 2 * half * (t_width + 3 * s_width),
            bytes_accessed=6 * half * (t_width + 3 * s_width),
            transcendentals=4 * half * half,
        ),
        compiler_params=pltpu.CompilerParams(vmem_limit_bytes=56 << 20),
    )(t_own, s_own, t_other, s_other)


def owned_rows(kl):
    kl = kl.reshape(2, 2, 2, 2, LANES).transpose(2, 0, 3, 1, 4).reshape(4, 4, LANES)
    source = lax.axis_index("xh") * 2 + lax.axis_index("core")
    got = []
    for turn in range(4):
        pairs = []
        for c in range(2):
            for dp in range(32):
                xh, xl, zh, zl, yh = ((dp >> k) & 1 for k in (4, 3, 2, 1, 0))
                quarter = turn ^ (xh * 2 + c)
                pairs.append((c * 32 + dp, zh * 32 + (xh ^ xl) * 16 + (zh ^ zl) * 8 + yh * 4 + quarter))
        sent = lax.dynamic_index_in_dim(kl, turn ^ source, 0, keepdims=False)
        got.append(lax.ppermute(sent, ("core",) + DP, pairs))
    got = jnp.stack(got)
    quarter = lax.axis_index(DP) % 4
    rows = [lax.dynamic_index_in_dim(got, f ^ quarter, 0, keepdims=False) for f in range(4)]
    rows = jnp.stack(rows).reshape(2, 2, 4, LANES)
    return rows.transpose(0, 2, 1, 3).reshape(1, 2 * 4 * 2 * LANES)


def local(teacher_query, student_hidden, query_weight):
    rows = teacher_query.shape[0]
    depth, columns = query_weight.shape
    t_width = teacher_query.shape[1] // 8
    width = columns // 4
    core = lax.axis_index("core")
    low = core == 0

    def token_halves(value):
        first, second = value[: rows // 2], value[rows // 2 :]
        return jnp.where(low, first, second), swap(jnp.where(low, second, first), "core")

    parts = jnp.moveaxis(query_weight.reshape(depth, 4, width), 1, 0)
    q = (lax.axis_index("xh") ^ lax.axis_index("xl")) * 2 + (lax.axis_index("zh") ^ lax.axis_index("zl"))
    near = jnp.stack([lax.dynamic_index_in_dim(parts, q ^ r, 0, keepdims=False) for r in range(4)])
    share = jnp.concatenate(token_halves(student_hidden))
    held = [share[None, first:last] for first, last, _ in RUNS]
    far, blocks = together(
        hop(held, 0),
        [near[0]] + [lax.ppermute(near[r], ("xl", "zl"), [(i, i ^ r) for i in range(4)]) for r in range(1, 4)],
    )
    held = joined(held, far)
    blocks = jnp.stack(blocks)
    t_own, t_other = token_halves(teacher_query)
    heads = jnp.stack([jnp.where(low, t_own, t_other), jnp.where(low, t_other, t_own)])
    heads = heads.reshape(2, rows // 2, 2, 2, 2, t_width).transpose(0, 4, 2, 3, 1, 5)
    heads = jnp.where(lax.axis_index("xh") == 0, heads, heads[:, :, ::-1])
    heads = jnp.stack([heads[0], heads[1][:, :, ::-1]])
    heads = heads.reshape(16, rows // 2, t_width)
    far, (more, heads) = together(hop(held, 1), [swap(blocks, "yh"), heads])
    held = joined(held, far)
    blocks = jnp.stack([blocks, more])
    runs = [blocks[:, :2], blocks[:, 2:]]
    far = hop(held, 2)
    hidden = [piece for both in zip(held, far) for piece in both]
    passed = hop_weight(runs, 0)
    teacher = exchange(heads, SPREAD).reshape(2048, t_width)
    runs = joined(runs, passed)
    w_own = [piece for both in zip(runs, hop_weight(runs, 1)) for piece in both]
    w_other = [swap(piece, "core") for piece in w_own]
    student = jnp.concatenate(trade(project(hidden, w_own, w_other)))
    hidden_other = [swap(piece, "core") for piece in hidden]
    teacher = after(teacher, student, *hidden_other)
    teacher_other = swap(teacher, "core")
    student_other = swap(student, "core")

    kl, grad, grad_other = relation(teacher, student, teacher_other, student_other)
    grad_other = swap(grad_other, "core").reshape(4, 512, -1)
    query_grad = [(mine + theirs).astype(jnp.bfloat16) for mine, theirs in zip(grad.reshape(4, 512, -1), grad_other)]
    query_grad = trade(query_grad)
    near, away = jnp.stack(query_grad[:2]), jnp.stack(query_grad[2:])
    same = core == lax.axis_index("zh")
    mine = jnp.where(same, near, away)
    theirs = swap(jnp.where(same, away, near), "core")
    sent = exchange(weight_grad_part(hidden, hidden_other, mine, theirs), DP)
    kl_rows = owned_rows(kl)
    sent = sent.reshape(2, 2, 2, 2, 2, depth, width)
    groups = []
    for q in range(4):
        total = None
        for xh in range(2):
            for zh in range(2):
                for yh in range(2):
                    term = sent[xh, xh ^ (q >> 1), zh, zh ^ (q & 1), yh].astype(jnp.float32)
                    total = term if total is None else total + term
        groups.append(total)
    return kl_rows, jnp.concatenate(groups, axis=1)


def solution(mesh):
    bits = Mesh(mesh.devices.reshape((2,) * 7), TP + DP)
    return jax.shard_map(
        local,
        mesh=bits,
        in_specs=(P(DP, TP), P(DP, TP), P(DP, TP)),
        out_specs=(P(TP + DP, None), P(DP, TP)),
        check_vma=False,
    )
```
